32 devices in a mesh: seq: 16 (over z, y, x), tp: 2 (over core).
Axes of the slice: x: 2, y: 2, z: 4, core: 2. Of those that a mesh axis runs over, the one named last changes fastest.
Arguments:
- inputs: bfloat16 [16384, 768], P('seq'), may hold values from -6 to 6
- cotangent: bfloat16 [16384, 768], P('seq'), may hold values from -6 to 6
- query_weight: bfloat16 [768, 768], P(None, 'tp'), may hold values from -0.21875 to 0.21875
- key_weight: bfloat16 [768, 768], P(None, 'tp'), may hold values from -0.21875 to 0.21875
- value_weight: bfloat16 [768, 768], P(None, 'tp'), may hold values from -0.21875 to 0.21875
- out_weight: bfloat16 [768, 768], P('tp'), may hold values from -0.21875 to 0.21875
- up_weight: bfloat16 [768, 3072], P(None, 'tp'), may hold values from -0.21875 to 0.21875
- down_weight: bfloat16 [3072, 768], P('tp'), may hold values from -0.21875 to 0.21875
- conv_taps: float32 [12, 33], P('tp'), may hold values from -1 to 1
- attn_gain: float32 [768], replicated, may hold values from 0.5 to 1.5
- attn_shift: float32 [768], replicated, may hold values from -1 to 1
- ffn_gain: float32 [768], replicated, may hold values from 0.5 to 1.5
- ffn_shift: float32 [768], replicated, may hold values from -1 to 1
- hyperplanes: bfloat16 [32, 8, 64], replicated, may hold values from -6 to 6
- lengths: int32 [32], replicated, may hold values from 1 to 4096, 16384 in all
Outputs:
- output: bfloat16 [16384, 768], P('seq')
- grad_inputs: float32 [16384, 768], P('seq')
- grad_query: float32 [768, 768], P(None, 'tp')
- grad_key: float32 [768, 768], P(None, 'tp')
- grad_value: float32 [768, 768], P(None, 'tp')
- grad_out: float32 [768, 768], P('tp')
- grad_up: float32 [768, 3072], P(None, 'tp')
- grad_down: float32 [3072, 768], P('tp')
- grad_taps: float32 [12, 33], P('tp')
- grad_attn_gain: float32 [768], replicated
- grad_attn_shift: float32 [768], replicated
- grad_ffn_gain: float32 [768], replicated
- grad_ffn_shift: float32 [768], replicated
- occupancy: float32 [12, 32, 256], P('tp')
The draws below stay inside these ranges and needn't reach their ends.
Inputs may be any that keep to these rules, and one draw needn't show every extreme that they name: The 32 lengths sum to 16384, and the longest is exactly 4096; sequences lie one after another along the tokens.
All inputs are finite; a program needn't handle non-finite values.
Results may differ from the reference program's by a relative error of at most 0.018.
Values may be sent and summed in bfloat16 or wider, within the bound.
A program may use at most 256 MiB of HBM per device.

```python
import math
import jax
import jax.numpy as jnp
import numpy as np
from jax import lax

D = 768
HEADS = 12
HEAD_DIM = 64
FF = 3072
TAU = 8
BITS = 8
HASHES = 32
CONV = 33
MOST = 4096
TOK_DEV = 1024
TOKENS = 16384
NDOCS = 32
REACH = 4
HALF = 16


def steps_of(key, shape, shards, smallest, largest):
    def one(position, blocks):
        steps = jax.random.uniform(jax.random.fold_in(jax.random.fold_in(key, 6), position), (blocks,), jnp.float32, smallest / len(shards), largest / len(shards))
        return jnp.repeat(jnp.exp(steps), shape[position] // blocks).reshape((-1,) + (1,) * (len(shape) - position - 1))

    level = one(*shards[0])
    for cut in shards[1:]:
        level = level * one(*cut)
    return level


def profile(number_of, total, bound, slope):
    loads = [(1 << 20) // math.isqrt(rank ** slope) + 1 for rank in range(2, number_of + 1)]
    rest, given = total - bound - (number_of - 1), [1] * (number_of - 1)
    while rest > 0:
        free = [i for i in range(number_of - 1) if given[i] < bound]
        pool, remaining = sum([loads[i] for i in free]), rest
        for i in free:
            more = min(bound - given[i], max(1, remaining * loads[i] // pool), rest)
            given[i] = given[i] + more
            rest = rest - more
    return np.array([bound] + given)


def uneven(own_key, count, total, limit, lean):
    if count == 2:
        one = jax.random.randint(own_key, (), max(1, total - limit), min(limit, total - 1) + 1)
        return jnp.stack([one, total - one])
    sizes = jnp.asarray(profile(count, total, limit, lean), jnp.int32)
    couples = (count - 1) // 2
    donor, receiver = sizes[1:1 + 2 * couples:2], sizes[2:2 + 2 * couples:2]
    room = jnp.minimum(donor - 1, limit - receiver)
    passed = jax.random.randint(jax.random.fold_in(own_key, 1), (couples,), 0, 1 << 20) % (room + 1)
    sizes = sizes.at[1:1 + 2 * couples:2].set(donor - passed).at[2:2 + 2 * couples:2].set(receiver + passed)
    return sizes[jax.random.permutation(jax.random.fold_in(own_key, 2), count)]


def bell_draw(stream_key, shape, scale, reach, cuts=(), held_as=jnp.bfloat16):
    values = jax.random.normal(stream_key, shape, jnp.float32) * scale
    if len(cuts) > 0:
        values = steps_of(stream_key, shape, cuts, -0.22, 0.18) * values
    return jnp.clip(values, min=-reach, max=reach).astype(held_as)


def setup_inputs(seed: int = 0) -> dict:
    keys = jax.random.split(jax.random.key(seed), 16)
    return {
        "inputs": bell_draw(keys[0], (TOKENS, D), 1.0, 6.0, ((0, 16),)),
        "cotangent": bell_draw(keys[1], (TOKENS, D), 1.0, 6.0, ((0, 16),)),
        "query_weight": bell_draw(keys[2], (D, D), D ** -0.5, 0.21875, ((1, 2),)),
        "key_weight": bell_draw(keys[3], (D, D), D ** -0.5, 0.21875, ((1, 2),)),
        "value_weight": bell_draw(keys[4], (D, D), D ** -0.5, 0.21875, ((1, 2),)),
        "out_weight": bell_draw(keys[5], (D, D), D ** -0.5, 0.21875, ((0, 2),)),
        "up_weight": bell_draw(keys[6], (D, FF), D ** -0.5, 0.21875, ((1, 2),)),
        "down_weight": bell_draw(keys[7], (FF, D), (FF // 4) ** -0.5, 0.21875, ((0, 2),)),
        "conv_taps": bell_draw(keys[8], (HEADS, CONV), CONV ** -0.5, 1.0, ((0, 2),), jnp.float32),
        "attn_gain": jnp.clip(1.0 + 0.1 * jax.random.normal(keys[9], (D,), jnp.float32), 0.5, 1.5),
        "attn_shift": bell_draw(keys[10], (D,), 0.2, 1.0, (), jnp.float32),
        "ffn_gain": jnp.clip(1.0 + 0.1 * jax.random.normal(keys[11], (D,), jnp.float32), 0.5, 1.5),
        "ffn_shift": bell_draw(keys[12], (D,), 0.2, 1.0, (), jnp.float32),
        "hyperplanes": bell_draw(keys[13], (HASHES, BITS, HEAD_DIM), 1.0, 6.0),
        "lengths": uneven(keys[14], NDOCS, TOKENS, MOST, 2).astype(jnp.int32),
    }


EPS_UNIT = 1e-06
EPS_LAYER = 1e-05
SHARP = 4.0
CLIP_EDGE = 0.999
PRECISE = lax.Precision.HIGHEST

@jax.custom_vjp
def low(v):
    return lax.optimization_barrier(v.astype(jnp.bfloat16)).astype(jnp.float32)

@jax.custom_vjp
def low_back(v):
    return v

def low_keep(v):
    return (low(v), None)

def low_pass(kept, grad):
    return (grad,)

def back_keep(v):
    return (v, None)

def back_low(kept, grad):
    return (low(grad),)
low.defvjp(low_keep, low_pass)
low_back.defvjp(back_keep, back_low)

def doc_ids(lengths, positions, all_tokens):
    doc_ends = jnp.cumsum(lengths).astype(jnp.int32)
    doc_index = lax.optimization_barrier(jnp.sum((doc_ends[None, :] <= positions[:, None]).astype(jnp.int32), axis=1)).astype(jnp.int32)
    inside = (positions >= 0) & (positions < all_tokens)
    return jnp.where(inside, doc_index, -1).astype(jnp.int32)

def unit_rows(vectors):
    return vectors * lax.rsqrt(lax.optimization_barrier(jnp.mean(vectors * vectors, axis=-1, keepdims=True)) + EPS_UNIT) * (1.0 / math.sqrt(vectors.shape[-1]))

def layer_norm(vectors, gain_row, shift_row):
    center = vectors - lax.optimization_barrier(jnp.mean(vectors, axis=-1, keepdims=True))
    spread = lax.optimization_barrier(jnp.mean(center * center, axis=-1, keepdims=True))
    return center * lax.rsqrt(spread + EPS_LAYER) * gain_row + shift_row

def collide_of(scores):
    clipped = jnp.clip(scores, -CLIP_EDGE, CLIP_EDGE)
    return 1.0 - jnp.arccos(clipped) * (1.0 / math.pi)

def attend(query_unit, key_unit, values, doc):
    margin = REACH * TOK_DEV
    window = (2 * REACH + 1) * TOK_DEV
    key_pad = jnp.pad(key_unit, ((margin, margin), (0, 0), (0, 0)))
    value_pad = jnp.pad(values, ((margin, margin), (0, 0), (0, 0)))
    doc_pad = jnp.pad(doc, (margin, margin), constant_values=-1)

    def one_block(block_index):
        row_start = (block_index * TOK_DEV).astype(jnp.int32)
        query_block = lax.dynamic_slice_in_dim(query_unit, row_start, TOK_DEV, 0)
        query_docs = lax.dynamic_slice_in_dim(doc, row_start, TOK_DEV, 0)
        key_block = lax.dynamic_slice_in_dim(key_pad, row_start, window, 0)
        value_block = lax.dynamic_slice_in_dim(value_pad, row_start, window, 0)
        key_docs = lax.dynamic_slice_in_dim(doc_pad, row_start, window, 0)
        same_doc = query_docs[:, None] == key_docs[None, :]
        scores = low_back(jnp.einsum('qhd,khd->hqk', query_block, key_block, precision=PRECISE))
        weights = low(jnp.where(same_doc[None], collide_of(scores) ** TAU, 0.0))
        return jnp.einsum('hqk,khd->qhd', weights, value_block, precision=PRECISE)
    blocks = lax.map(jax.checkpoint(one_block), jnp.arange(TOKENS // TOK_DEV, dtype=jnp.int32))
    return blocks.reshape(TOKENS, HEADS, HEAD_DIM)

def convolve(values, doc, conv_taps):
    value_pad = jnp.pad(values, ((HALF, HALF), (0, 0), (0, 0)))
    doc_pad = jnp.pad(doc, (HALF, HALF), constant_values=-1)
    running = jnp.zeros(values.shape, jnp.float32)
    for offset in range(CONV):
        same_doc = (doc_pad[offset:offset + TOKENS] == doc)[:, None, None]
        running = running + jnp.where(same_doc, conv_taps[None, :, offset, None] * value_pad[offset:offset + TOKENS], 0.0)
    return running

def forward(inputs, query_weight, key_weight, value_weight, out_weight, up_weight, down_weight, conv_taps, attn_gain, attn_shift, ffn_gain, ffn_shift, doc):
    head_shape = (TOKENS, HEADS, HEAD_DIM)
    queries = low_back(jnp.dot(inputs, query_weight, precision=PRECISE))
    keys_raw = low_back(jnp.dot(inputs, key_weight, precision=PRECISE))
    values = low(low_back(jnp.dot(inputs, value_weight, precision=PRECISE))).reshape(head_shape)
    query_unit = low(unit_rows(queries.reshape(head_shape)))
    key_unit = low(unit_rows(keys_raw.reshape(head_shape)))
    gathered = low_back(attend(query_unit, key_unit, values, doc))
    normed = gathered * lax.rsqrt(lax.optimization_barrier(jnp.mean(gathered * gathered, axis=-1, keepdims=True)) + EPS_UNIT)
    mixed = low(low_back((normed + convolve(values, doc, conv_taps)).reshape(TOKENS, D)))
    attn_out = low_back(jnp.dot(mixed, out_weight, precision=PRECISE))
    first_norm = layer_norm(inputs + attn_out, attn_gain, attn_shift)
    hidden = low_back(jnp.dot(low(first_norm), up_weight, precision=PRECISE))
    active = low(jax.nn.gelu(hidden, approximate=False))
    ffn_out = low_back(jnp.dot(active, down_weight, precision=PRECISE))
    return layer_norm(first_norm + ffn_out, ffn_gain, ffn_shift)

def bucket_probs(bit_prob, bit_table):
    running = jnp.ones(bit_prob.shape[:-1] + (bit_table.shape[0],), jnp.float32)
    for bit_index in range(bit_table.shape[1]):
        chosen = bit_table[:, bit_index] == 1
        running = running * jnp.where(chosen, bit_prob[..., bit_index:bit_index + 1], 1.0 - bit_prob[..., bit_index:bit_index + 1])
    return running

def occupancy_of(inputs, key_weight, hyperplanes):
    half_bits = BITS // 2
    bit_table = jnp.arange(2 ** half_bits)[:, None] // (2 ** jnp.arange(half_bits))[None, :] % 2

    def one_block(block_index):
        row_start = (block_index * TOK_DEV).astype(jnp.int32)
        rows_in = lax.dynamic_slice_in_dim(inputs, row_start, TOK_DEV, 0)
        projected_keys = jnp.dot(rows_in, key_weight, precision=PRECISE).reshape(TOK_DEV, HEADS, HEAD_DIM)
        key_unit = low(unit_rows(projected_keys))
        projected = jnp.einsum('thd,mbd->thmb', key_unit, hyperplanes, precision=PRECISE)
        bit_prob = jax.nn.sigmoid(SHARP * projected)
        low_half = bucket_probs(bit_prob[..., :half_bits], bit_table)
        high_half = bucket_probs(bit_prob[..., half_bits:], bit_table)
        return jnp.einsum('thmc,thme->hmec', low_half, high_half, precision=PRECISE)
    summed = lax.optimization_barrier(jnp.sum(lax.map(one_block, jnp.arange(TOKENS // TOK_DEV, dtype=jnp.int32)), axis=0))
    return summed.reshape(HEADS, HASHES, 2 ** BITS) * (2.0 ** BITS / TOKENS)

def reference(inputs, cotangent, query_weight, key_weight, value_weight, out_weight, up_weight, down_weight, conv_taps, attn_gain, attn_shift, ffn_gain, ffn_shift, hyperplanes, lengths):
    doc = doc_ids(lengths, jnp.arange(TOKENS, dtype=jnp.int32), TOKENS)
    floats = [array.astype(jnp.float32) for array in (inputs, query_weight, key_weight, value_weight, out_weight, up_weight, down_weight, conv_taps, attn_gain, attn_shift, ffn_gain, ffn_shift)]

    def run_layer(*params):
        return forward(*params, doc)
    result, pullback = jax.vjp(run_layer, *floats)
    gradients = pullback(cotangent.astype(jnp.float32))
    occupancy = occupancy_of(floats[0], floats[2], hyperplanes.astype(jnp.float32))
    return (result.astype(jnp.bfloat16), gradients[0], gradients[1], gradients[2], gradients[3], gradients[4], gradients[5], gradients[6], gradients[7], gradients[8], gradients[9], gradients[10], gradients[11], occupancy)
```

```python
from functools import partial
import math

import jax
import jax.numpy as jnp
from jax import lax
from jax.experimental import pallas as pl
from jax.experimental.pallas import tpu as pltpu
from jax.sharding import PartitionSpec as P

TAU = 8
BITS = 8
CONV = 33
MOST = 4096
RIM = (CONV - 1) // 2

EPS_UNIT = 1e-06
EPS_LAYER = 1e-05
SHARP = 4.0
CLIP_EDGE = 0.999

TILE = 256
CHUNK = 512
PAIR = 128
STRIP = 128
FAR_ID = 1 << 20

F32 = jnp.float32
BF16 = jnp.bfloat16

ARC = (
    0.49999961256980896,
    -0.06828052550554276,
    0.027964841574430466,
    -0.014291195198893547,
    0.006136968266218901,
    -0.001371906721033156,
)


def params(**kwargs):
    return pltpu.CompilerParams(vmem_limit_bytes=56 << 20, **kwargs)


def nn(left, right):
    return lax.dot_general(left, right, (((1,), (0,)), ((), ())), preferred_element_type=F32)


def nt(left, right):
    return lax.dot_general(left, right, (((1,), (1,)), ((), ())), preferred_element_type=F32)


def tn(left, right):
    return lax.dot_general(left, right, (((0,), (0,)), ((), ())), preferred_element_type=F32)


def head_masks(head_dim):
    lanes = lax.broadcasted_iota(jnp.int32, (1, PAIR), 1)
    first = (lanes < head_dim).astype(F32)
    return first.astype(BF16), (1.0 - first).astype(BF16)


def head_sum(rows, head_dim):
    here = lax.broadcasted_iota(jnp.int32, (PAIR, PAIR), 0) // head_dim
    there = lax.broadcasted_iota(jnp.int32, (PAIR, PAIR), 1) // head_dim
    ones = (here == there).astype(F32).astype(BF16)
    sums = []
    for start in range(0, rows.shape[1], PAIR):
        part = rows[:, start : start + PAIR]
        high = part.astype(BF16)
        low = (part - high.astype(F32)).astype(BF16)
        sums.append(nn(high, ones) + nn(low, ones))
    return jnp.concatenate(sums, axis=1)


def project_kernel(units, head_dim, x_ref, w_ref, *out_refs):
    width = out_refs[-1].shape[1]
    whole = nn(x_ref[...], w_ref[...])
    for index in range(units):
        part = whole[:, index * width : (index + 1) * width]
        scale = lax.rsqrt(head_sum(part * part, head_dim) * (1.0 / head_dim) + EPS_UNIT)
        scale = scale * (1.0 / math.sqrt(head_dim))
        out_refs[2 * index][...] = (part * scale).astype(BF16)
        out_refs[2 * index + 1][...] = scale
    out_refs[-1][...] = whole[:, units * width :].astype(BF16)


def project(x, weight, units, head_dim):
    rows, depth = x.shape
    width = weight.shape[1] // (units + 1)
    row_spec = pl.BlockSpec((CHUNK, width), lambda i: (i, 0))
    unit_shapes = [
        jax.ShapeDtypeStruct((rows, width), BF16),
        jax.ShapeDtypeStruct((rows, width), F32),
    ]
    return pl.pallas_call(
        partial(project_kernel, units, head_dim),
        grid=(rows // CHUNK,),
        in_specs=[
            pl.BlockSpec((CHUNK, depth), lambda i: (i, 0)),
            pl.BlockSpec(weight.shape, lambda i: (0, 0)),
        ],
        out_specs=[row_spec] * (2 * units + 1),
        out_shape=unit_shapes * units + [jax.ShapeDtypeStruct((rows, width), BF16)],
        compiler_params=params(),
        cost_estimate=pl.CostEstimate(
            flops=2 * rows * depth * weight.shape[1],
            bytes_accessed=rows * (depth * 2 + width * (6 * units + 2)),
            transcendentals=0,
        ),
        name="project",
    )(x, weight)


def collide_parts(scores):
    size = jnp.minimum(jnp.abs(scores), CLIP_EDGE)
    rest = 1.0 - size
    root = lax.rsqrt(rest)
    poly = ARC[5]
    for factor in ARC[4::-1]:
        poly = poly * size + factor
    angle = (rest * root) * poly
    return size, root, jnp.where(scores < 0.0, angle, 1.0 - angle)


def tile_facts(table, tiles_q, tiles_k, qi, kt):
    q_low, q_high = table[qi], table[tiles_q + qi]
    k_low, k_high = table[2 * tiles_q + kt], table[2 * tiles_q + tiles_k + kt]
    needed = (k_high >= q_low) & (k_low <= q_high)
    whole = (q_low == q_high) & (k_low == k_high)
    return needed, whole


def attend_kernel(head_dim, seeded, table, q_ref, k_ref, v_ref, qcol_ref, krow_ref, *rest):
    out_ref = rest[-1]
    tiles_q, tiles_k = q_ref.shape[0] // TILE, k_ref.shape[0] // TILE
    masks = head_masks(head_dim)
    if seeded:
        out_ref[...] = rest[0][...]
    else:
        out_ref[...] = jnp.zeros_like(out_ref)

    def q_loop(qi, carry):
        rows = pl.ds(pl.multiple_of(qi * TILE, TILE), TILE)

        def k_loop(kt, inner):
            needed, whole = tile_facts(table, tiles_q, tiles_k, qi, kt)

            def part(same):
                cols = pl.ds(pl.multiple_of(kt * TILE, TILE), TILE)
                q, k, v = q_ref[rows, :], k_ref[cols, :], v_ref[cols, :]
                total = None
                for mask in masks:
                    chance = collide_parts(nt(q * mask, k))[2]
                    chance = chance * chance
                    chance = chance * chance
                    chance = chance * chance
                    if same is not None:
                        chance = jnp.where(same, chance, 0.0)
                    term = nn(chance.astype(BF16), v * mask)
                    total = term if total is None else total + term
                out_ref[rows, :] += total

            @pl.when(needed & whole)
            def _():
                part(None)

            @pl.when(needed & jnp.logical_not(whole))
            def _():
                ids = qcol_ref[rows, :]
                part(jnp.concatenate([ids, ids], axis=1) == krow_ref[pl.ds(kt, 1), :])

            return inner

        return lax.fori_loop(0, tiles_k, k_loop, carry)

    lax.fori_loop(0, tiles_q, q_loop, 0)


def attend(q, k, v, own_ids, key_ids, head_dim, seed=None):
    tokens, width = q.shape
    far = k.shape[0]
    table, qcol, krow = mask_tables(own_ids, key_ids)
    operands = [q, k, v, qcol, krow]
    q_spec = pl.BlockSpec((tokens, PAIR), lambda p, t: (0, p))
    k_spec = pl.BlockSpec((far, PAIR), lambda p, t: (0, p))
    specs = [
        q_spec,
        k_spec,
        k_spec,
        pl.BlockSpec(qcol.shape, lambda p, t: (0, 0)),
        pl.BlockSpec(krow.shape, lambda p, t: (0, 0)),
    ]
    if seed is not None:
        operands.append(seed)
        specs.append(q_spec)
    return pl.pallas_call(
        partial(attend_kernel, head_dim, seed is not None),
        grid_spec=pltpu.PrefetchScalarGridSpec(
            num_scalar_prefetch=1, grid=(width // PAIR,), in_specs=specs, out_specs=q_spec
        ),
        out_shape=jax.ShapeDtypeStruct((tokens, width), F32),
        compiler_params=params(),
        cost_estimate=pl.CostEstimate(
            flops=8 * tokens * far * width, bytes_accessed=far * width * 4, transcendentals=0
        ),
        name="attend",
    )(table, *operands)


def mask_tables(own_ids, key_ids):
    table = jnp.concatenate(
        [
            own_ids[::TILE],
            own_ids[TILE - 1 :: TILE],
            key_ids[::TILE],
            key_ids[TILE - 1 :: TILE],
        ]
    )
    qcol = jnp.broadcast_to(own_ids[:, None], (own_ids.shape[0], PAIR))
    return table, qcol, key_ids.reshape(-1, TILE)


def back_attend_kernel(
    head_dim,
    seeded,
    table,
    q_ref,
    g_ref,
    k_ref,
    v_ref,
    kcol_ref,
    qrow_ref,
    *rest,
):
    dk_ref, dv_ref, dq_ref, acc_k, acc_v = rest[-5:]
    tiles_q, tiles_k = q_ref.shape[0] // TILE, k_ref.shape[0] // TILE
    masks = head_masks(head_dim)
    if seeded:
        dq_ref[...] = rest[0][...]
    else:
        dq_ref[...] = jnp.zeros_like(dq_ref)

    def k_loop(kt, carry):
        cols = pl.ds(pl.multiple_of(kt * TILE, TILE), TILE)
        acc_k[...] = jnp.zeros_like(acc_k)
        acc_v[...] = jnp.zeros_like(acc_v)

        def q_loop(qi, inner):
            needed, whole = tile_facts(table, tiles_q, tiles_k, qi, kt)

            def part(same):
                rows = pl.ds(pl.multiple_of(qi * TILE, TILE), TILE)
                q, g, k, v = q_ref[rows, :], g_ref[rows, :], k_ref[cols, :], v_ref[cols, :]
                k_turned = k.T
                sum_k, sum_v = None, None
                for index, mask in enumerate(masks):
                    q_half, g_half = q * mask, g * mask
                    scores = nt(k, q_half)
                    size, root, chance = collide_parts(scores)
                    second = chance * chance
                    fourth = second * second
                    weights = fourth * fourth
                    slope = (fourth * second) * (chance * (root * lax.rsqrt(1.0 + size)))
                    inside = jnp.abs(scores) <= CLIP_EDGE
                    if same is not None:
                        inside = inside & same
                        weights = jnp.where(same, weights, 0.0)
                    slope = jnp.where(inside, nt(v, g_half) * slope, 0.0).astype(BF16)
                    term_v = nn(weights.astype(BF16), g_half)
                    term_k = nn(slope, q_half)
                    sum_v = term_v if sum_v is None else sum_v + term_v
                    sum_k = term_k if sum_k is None else sum_k + term_k
                    half = slice(index * head_dim, (index + 1) * head_dim)
                    dq_ref[half, rows] += nn(k_turned[half, :], slope)
                acc_v[...] += sum_v
                acc_k[...] += sum_k

            @pl.when(needed & whole)
            def _():
                part(None)

            @pl.when(needed & jnp.logical_not(whole))
            def _():
                ids = kcol_ref[cols, :]
                part(jnp.concatenate([ids, ids], axis=1) == qrow_ref[pl.ds(qi, 1), :])

            return inner

        lax.fori_loop(0, tiles_q, q_loop, 0)
        dk_ref[cols, :] = acc_k[...].astype(BF16)
        dv_ref[cols, :] = acc_v[...].astype(BF16)
        return carry

    lax.fori_loop(0, tiles_k, k_loop, 0)


def back_attend(q, g, k, v, own_ids, key_ids, head_dim, seed=None):
    tokens, width = q.shape
    far = k.shape[0]
    table, _, _ = mask_tables(own_ids, key_ids)
    kcol = jnp.broadcast_to(key_ids[:, None], (far, PAIR))
    qrow = own_ids.reshape(-1, TILE)
    q_spec = pl.BlockSpec((tokens, PAIR), lambda p, t: (0, p))
    k_spec = pl.BlockSpec((far, PAIR), lambda p, t: (0, p))
    dq_spec = pl.BlockSpec((PAIR, tokens), lambda p, t: (p, 0))
    specs = [
        q_spec,
        q_spec,
        k_spec,
        k_spec,
        pl.BlockSpec(kcol.shape, lambda p, t: (0, 0)),
        pl.BlockSpec(qrow.shape, lambda p, t: (0, 0)),
    ]
    operands = [q, g, k, v, kcol, qrow]
    if seed is not None:
        operands.append(seed)
        specs.append(dq_spec)
    return pl.pallas_call(
        partial(back_attend_kernel, head_dim, seed is not None),
        grid_spec=pltpu.PrefetchScalarGridSpec(
            num_scalar_prefetch=1,
            grid=(width // PAIR,),
            in_specs=specs,
            out_specs=[k_spec, k_spec, dq_spec],
            scratch_shapes=[pltpu.VMEM((TILE, PAIR), F32), pltpu.VMEM((TILE, PAIR), F32)],
        ),
        out_shape=[
            jax.ShapeDtypeStruct((far, width), BF16),
            jax.ShapeDtypeStruct((far, width), BF16),
            jax.ShapeDtypeStruct((width, tokens), F32),
        ],
        compiler_params=params(),
        cost_estimate=pl.CostEstimate(
            flops=16 * tokens * far * width, bytes_accessed=far * width * 8, transcendentals=0
        ),
        name="back_attend",
    )(table, *operands)


def back_project_kernel(units, turned, head_dim, need, x_ref, w_ref, *refs):
    dx_ref, dw_ref = refs[-2:]
    step = pl.program_id(0)

    @pl.when(step == 0)
    def _():
        dw_ref[...] = jnp.zeros_like(dw_ref)

    @pl.when(need[step] > 0)
    def _():
        grads = []
        for index in range(units):
            unit_ref, scale_ref, grad_ref = refs[3 * index : 3 * index + 3]
            grad = grad_ref[...].astype(F32)
            if index < turned:
                grad = grad.T
            unit = unit_ref[...].astype(F32)
            inner = head_sum(grad * unit, head_dim)
            grads.append(
                ((TAU / math.pi) * scale_ref[...] * (grad - unit * inner)).astype(BF16)
            )
        value_refs = refs[3 * units : -2]
        value = value_refs[0][...].astype(F32)
        for extra in value_refs[1:]:
            value = value + extra[...].astype(F32)
        grads.append(value.astype(BF16))
        joined = jnp.concatenate(grads, axis=1)
        dx_ref[...] = nt(joined, w_ref[...]).astype(BF16)
        dw_ref[...] += tn(x_ref[...], joined)

    @pl.when(need[step] == 0)
    def _():
        dx_ref[...] = jnp.zeros_like(dx_ref)


def back_project(x, weight, parts, turned, values, need, head_dim):
    rows, depth = x.shape
    width = values[0].shape[1]
    row_spec = pl.BlockSpec((CHUNK, width), lambda i, n: (i, 0))
    wide_spec = pl.BlockSpec((CHUNK, depth), lambda i, n: (i, 0))
    weight_spec = pl.BlockSpec(weight.shape, lambda i, n: (0, 0))
    specs, operands = [wide_spec, weight_spec], [x, weight]
    for index, (unit, scale, grad) in enumerate(parts):
        operands += [unit, scale, grad]
        specs += [row_spec, row_spec]
        specs.append(
            pl.BlockSpec((width, CHUNK), lambda i, n: (0, i)) if index < turned else row_spec
        )
    operands += values
    specs += [row_spec] * len(values)
    return pl.pallas_call(
        partial(back_project_kernel, len(parts), turned, head_dim),
        grid_spec=pltpu.PrefetchScalarGridSpec(
            num_scalar_prefetch=1,
            grid=(rows // CHUNK,),
            in_specs=specs,
            out_specs=[wide_spec, weight_spec],
        ),
        out_shape=[
            jax.ShapeDtypeStruct((rows, depth), BF16),
            jax.ShapeDtypeStruct(weight.shape, F32),
        ],
        compiler_params=params(),
        cost_estimate=pl.CostEstimate(
            flops=4 * rows * depth * weight.shape[1],
            bytes_accessed=rows * 12 * depth,
            transcendentals=0,
        ),
        name="back_project",
    )(need, *operands)


def band_windows(ids_ext, tokens):
    start = STRIP // 2
    return jnp.stack(
        [ids_ext[start + row : start + row + 2 * STRIP] for row in range(0, tokens, STRIP)]
    )


def lane_taps(conv_taps, mirrored):
    front = STRIP // 2 - RIM
    heads = conv_taps.shape[0]
    taps = conv_taps[:, ::-1] if mirrored else conv_taps
    return jnp.pad(taps, ((0, -heads % 8), (front, 2 * STRIP - front - CONV)))


def fill_bands(taps_ref, bands, heads):
    for head in range(heads):
        row = jnp.broadcast_to(taps_ref[head : head + 1, :], (STRIP, 2 * STRIP))
        bands[head] = pltpu.roll(row, 0, 1, stride=1, stride_axis=0)


def band_product(band, same, window):
    band = jnp.where(same, band, 0.0)
    high = band.astype(BF16)
    low = (band - high.astype(F32)).astype(BF16)
    return nn(high, window) + nn(low, window)


def mix_kernel(head_dim, g_ref, v_ref, qcol_ref, krow_ref, taps_ref, out_ref, bands):
    heads = g_ref.shape[1] // head_dim
    step = pl.program_id(0)

    @pl.when(step == 0)
    def _():
        fill_bands(taps_ref, bands, heads)

    masks = head_masks(head_dim)
    window = v_ref[pl.ds(pl.multiple_of(step * STRIP + STRIP // 2, STRIP // 2), 2 * STRIP), :]
    ids = qcol_ref[...]
    same = jnp.concatenate([ids, ids], axis=1) == krow_ref[pl.ds(step, 1), :]
    pieces = []
    for pair in range(heads // 2):
        values = window[:, pair * PAIR : (pair + 1) * PAIR]
        total = None
        for index, mask in enumerate(masks):
            term = band_product(bands[2 * pair + index], same, values * mask)
            total = term if total is None else total + term
        pieces.append(total)
    gathered = g_ref[...]
    scale = lax.rsqrt(head_sum(gathered * gathered, head_dim) * (1.0 / head_dim) + EPS_UNIT)
    out_ref[...] = (gathered * scale + jnp.concatenate(pieces, axis=1)).astype(BF16)


def mix(gathered, values_ext, own_ids, ids_ext, conv_taps, head_dim):
    tokens, width = gathered.shape
    heads = width // head_dim
    qcol = jnp.broadcast_to(own_ids[:, None], (tokens, PAIR))
    krow = band_windows(ids_ext, tokens)
    taps = lane_taps(conv_taps, False)
    row_spec = pl.BlockSpec((STRIP, width), lambda i: (i, 0))
    return pl.pallas_call(
        partial(mix_kernel, head_dim),
        grid=(tokens // STRIP,),
        in_specs=[
            row_spec,
            pl.BlockSpec(values_ext.shape, lambda i: (0, 0)),
            pl.BlockSpec((STRIP, PAIR), lambda i: (i, 0)),
            pl.BlockSpec(krow.shape, lambda i: (0, 0)),
            pl.BlockSpec(taps.shape, lambda i: (0, 0)),
        ],
        out_specs=row_spec,
        out_shape=jax.ShapeDtypeStruct((tokens, width), BF16),
        scratch_shapes=[pltpu.VMEM((heads, STRIP, 2 * STRIP), F32)],
        compiler_params=params(),
        cost_estimate=pl.CostEstimate(
            flops=4 * tokens * 2 * STRIP * width, bytes_accessed=tokens * width * 8, transcendentals=0
        ),
        name="mix",
    )(gathered, values_ext, qcol, krow, taps)


def back_norm_kernel(head_dim, g_ref, m_ref, out_ref):
    gathered, grad = g_ref[...], m_ref[...].astype(F32)
    scale = lax.rsqrt(head_sum(gathered * gathered, head_dim) * (1.0 / head_dim) + EPS_UNIT)
    mean = head_sum(grad * gathered, head_dim) * (1.0 / head_dim)
    out_ref[...] = (scale * (grad - (scale * scale) * gathered * mean)).astype(BF16)


def back_norm(gathered, grad_mixed, head_dim):
    tokens, width = gathered.shape
    row_spec = pl.BlockSpec((TILE, width), lambda i: (i, 0))
    return pl.pallas_call(
        partial(back_norm_kernel, head_dim),
        grid=(tokens // TILE,),
        in_specs=[row_spec, row_spec],
        out_specs=row_spec,
        out_shape=jax.ShapeDtypeStruct((tokens, width), BF16),
        compiler_params=params(),
        cost_estimate=pl.CostEstimate(
            flops=tokens * width * 512, bytes_accessed=tokens * width * 8, transcendentals=0
        ),
        name="back_norm",
    )(gathered, grad_mixed)


def back_conv_kernel(
    head_dim, v_ref, m_ref, col_ref, row_ref, taps_ref, dv_ref, tap_ref, bands, sums
):
    heads = dv_ref.shape[1] // head_dim
    step = pl.program_id(0)

    @pl.when(step == 0)
    def _():
        fill_bands(taps_ref, bands, heads)
        sums[...] = jnp.zeros_like(sums)

    masks = head_masks(head_dim)
    around = pl.ds(pl.multiple_of(step * STRIP + STRIP // 2, STRIP // 2), 2 * STRIP)
    centre = pl.ds(pl.multiple_of(step * STRIP + STRIP, STRIP), STRIP)
    ids = col_ref[...]
    same = jnp.concatenate([ids, ids], axis=1) == row_ref[pl.ds(step, 1), :]
    pieces = []
    for pair in range(heads // 2):
        cols = slice(pair * PAIR, (pair + 1) * PAIR)
        grads = m_ref[around, cols]
        values = v_ref[around, cols]
        here = m_ref[centre, cols]
        total = None
        for index, mask in enumerate(masks):
            head = 2 * pair + index
            term = band_product(bands[head], same, grads * mask)
            total = term if total is None else total + term
            sums[head] += jnp.where(same, nt(here * mask, values), 0.0)
        pieces.append(total)
    dv_ref[...] = jnp.concatenate(pieces, axis=1)

    @pl.when(step == pl.num_programs(0) - 1)
    def _():
        tap_ref[...] = jnp.zeros_like(tap_ref)
        places = [lax.broadcasted_iota(jnp.int32, (STRIP, STRIP), d) for d in (0, 1)]
        flip = (places[0] + places[1] == STRIP - 1).astype(F32).astype(BF16)
        for head in range(heads):
            whole = sums[head]
            high = whole.astype(BF16)
            low = (whole - high.astype(F32)).astype(BF16)
            turned = pltpu.roll(
                nn(flip, high) + nn(flip, low), STRIP + 1, 1, stride=1, stride_axis=0
            )
            tap_ref[head : head + 1, :] = jnp.sum(turned, axis=0, keepdims=True)


def back_conv(values_ext, grad_ext, own_ids, ids_ext, conv_taps, head_dim):
    tokens, width = own_ids.shape[0], values_ext.shape[1]
    heads = width // head_dim
    col = jnp.broadcast_to(own_ids[:, None], (tokens, PAIR))
    row = band_windows(ids_ext, tokens)
    taps = lane_taps(conv_taps, True)
    front = STRIP // 2 - RIM
    grad_values, tap_sums = pl.pallas_call(
        partial(back_conv_kernel, head_dim),
        grid=(tokens // STRIP,),
        in_specs=[
            pl.BlockSpec(values_ext.shape, lambda i: (0, 0)),
            pl.BlockSpec(grad_ext.shape, lambda i: (0, 0)),
            pl.BlockSpec((STRIP, PAIR), lambda i: (i, 0)),
            pl.BlockSpec(row.shape, lambda i: (0, 0)),
            pl.BlockSpec(taps.shape, lambda i: (0, 0)),
        ],
        out_specs=[
            pl.BlockSpec((STRIP, width), lambda i: (i, 0)),
            pl.BlockSpec(taps.shape, lambda i: (0, 0)),
        ],
        out_shape=[
            jax.ShapeDtypeStruct((tokens, width), F32),
            jax.ShapeDtypeStruct(taps.shape, F32),
        ],
        scratch_shapes=[
            pltpu.VMEM((heads, STRIP, 2 * STRIP), F32),
            pltpu.VMEM((heads, STRIP, 2 * STRIP), F32),
        ],
        compiler_params=params(),
        cost_estimate=pl.CostEstimate(
            flops=6 * tokens * 2 * STRIP * width, bytes_accessed=tokens * width * 8, transcendentals=0
        ),
        name="back_conv",
    )(values_ext, grad_ext, col, row, taps)
    return grad_values, tap_sums[:heads, front : front + CONV]


def occupancy_kernel(head_dim, hashes, k_ref, w_ref, out_ref):
    combos = 4
    lanes = hashes * combos
    wide = hashes * combos * combos

    @pl.when(pl.program_id(1) == 0)
    def _():
        out_ref[...] = jnp.zeros_like(out_ref)

    source = lax.broadcasted_iota(jnp.int32, (lanes, wide), 0)
    target = lax.broadcasted_iota(jnp.int32, (lanes, wide), 1)
    same_hash = (source // combos) == (target // (combos * combos))
    picks = []
    for divisor in (1, combos):
        chosen = same_hash & ((source % combos) == ((target // divisor) % combos))
        picks.append(chosen.astype(F32).astype(BF16))
    keys = k_ref[...]
    for index in range(2):
        signed = nn(keys, w_ref[index])
        halves = []
        for half in range(2):
            product = None
            for pick in range(2):
                start = (half * 2 + pick) * 2 * lanes
                one = 1.0 + jnp.exp(-signed[:, start : start + lanes])
                two = 1.0 + jnp.exp(-signed[:, start + lanes : start + 2 * lanes])
                spread = nn((1.0 / (one * two)).astype(BF16), picks[pick])
                product = spread if product is None else product * spread
            halves.append(product.astype(BF16))
        low, high = halves
        for start in range(0, wide, PAIR):
            block = slice(start, start + PAIR)
            out_ref[index, block, :] += tn(high[:, block], low[:, block])


def occupancy(key_unit, hyperplanes, scale):
    tokens, width = key_unit.shape
    hashes, bits, head_dim = hyperplanes.shape
    pairs = width // PAIR
    wide = hashes * 16
    planes = SHARP * hyperplanes.astype(F32)
    columns = []
    for group in range(bits // 2):
        for bit in range(2):
            signs = 2.0 * ((jnp.arange(4) // (2**bit)) % 2).astype(F32) - 1.0
            plane = planes[:, 2 * group + bit, :]
            columns.append((plane.T[:, :, None] * signs).reshape(head_dim, hashes * 4))
    weight = jnp.concatenate(columns, axis=1).astype(BF16)
    blank = jnp.zeros_like(weight)
    weights = jnp.stack(
        [jnp.concatenate([weight, blank], axis=0), jnp.concatenate([blank, weight], axis=0)]
    )
    counts = pl.pallas_call(
        partial(occupancy_kernel, head_dim, hashes),
        grid=(pairs, tokens // TILE),
        in_specs=[
            pl.BlockSpec((TILE, PAIR), lambda p, t: (t, p)),
            pl.BlockSpec(weights.shape, lambda p, t: (0, 0, 0)),
        ],
        out_specs=pl.BlockSpec((2, wide, PAIR), lambda p, t: (p, 0, 0)),
        out_shape=jax.ShapeDtypeStruct((2 * pairs, wide, PAIR), F32),
        compiler_params=params(),
        cost_estimate=pl.CostEstimate(
            flops=tokens * width * 16000, bytes_accessed=tokens * width * 4, transcendentals=0
        ),
        name="occupancy",
    )(key_unit, weights)
    blocks = counts.reshape(2 * pairs, wide // PAIR, PAIR // 16, 16, PAIR // 16, 16)
    picked = jnp.stack([blocks[:, :, i, :, i, :] for i in range(PAIR // 16)], axis=2)
    return picked.reshape(2 * pairs, hashes, 256) * scale


def doc_ids(lengths, positions, all_tokens):
    doc_ends = jnp.cumsum(lengths)
    doc_index = jnp.sum((doc_ends[None, :] <= positions[:, None]).astype(jnp.int32), axis=1)
    doc_index = jnp.where(positions < 0, -1, doc_index)
    return jnp.where(positions >= all_tokens, FAR_ID, doc_index)


def shifted(block, axis, distance):
    count = lax.axis_size(axis)
    route = [(i, i + distance) for i in range(count) if 0 <= i + distance < count]
    return lax.ppermute(block, axis, route)


def swapped(block, axis):
    return lax.ppermute(block, axis, [(0, 1), (1, 0)])


def tp_sum(partial_low):
    return partial_low.astype(F32) + swapped(partial_low, "tp").astype(F32)


def with_rims(block):
    rows, width = block.shape
    below = shifted(block[rows - RIM :], "seq", 1)
    above = shifted(block[:RIM], "seq", -1)
    blank = jnp.zeros((STRIP - RIM, width), block.dtype)
    return jnp.concatenate([blank, below, block, above, blank], axis=0)


def layer_norm(vectors, gain_row, shift_row):
    center = vectors - jnp.mean(vectors, axis=-1, keepdims=True)
    spread = jnp.mean(center * center, axis=-1, keepdims=True)
    return center * lax.rsqrt(spread + EPS_LAYER) * gain_row + shift_row


def body(
    inputs,
    cotangent,
    query_weight,
    key_weight,
    value_weight,
    out_weight,
    up_weight,
    down_weight,
    conv_taps,
    attn_gain,
    attn_shift,
    ffn_gain,
    ffn_shift,
    hyperplanes,
    lengths,
):
    tokens, depth = inputs.shape
    head_dim = hyperplanes.shape[2]
    width = query_weight.shape[1]
    half = tokens // 2
    my_index = lax.axis_index("seq")
    my_side = lax.axis_index("tp")
    all_tokens = tokens * lax.axis_size("seq")
    far_reach = (MOST + tokens - 2) // tokens
    near = [d for d in range(1, far_reach + 1) if d <= far_reach // 2]
    far = [d for d in range(1, far_reach + 1) if d > far_reach // 2]
    groups = [[s * d for d in part for s in (1, -1)] for part in (near, far)]

    own_ids = doc_ids(lengths, my_index * tokens + jnp.arange(tokens, dtype=jnp.int32), all_tokens)
    ids_ext = doc_ids(
        lengths,
        my_index * tokens - STRIP + jnp.arange(tokens + 2 * STRIP, dtype=jnp.int32),
        all_tokens,
    )

    mine_rows = lax.dynamic_slice_in_dim(inputs, my_side * half, half, 0)
    group_x, group_ids = [], []
    for distances in groups:
        mine = jnp.concatenate([shifted(mine_rows, "seq", d) for d in distances], axis=0)
        group_x.append(jnp.concatenate([mine, swapped(mine, "tp")], axis=0))
        spots = [
            (my_index - d) * tokens + side * half + jnp.arange(half, dtype=jnp.int32)
            for side in (my_side, 1 - my_side)
            for d in distances
        ]
        group_ids.append(doc_ids(lengths, jnp.concatenate(spots), all_tokens))

    weight_qkv = jnp.concatenate([query_weight, key_weight, value_weight], axis=1)
    weight_kv = weight_qkv[:, width:]
    query_unit, query_scale, key_unit, key_scale, values = project(inputs, weight_qkv, 2, head_dim)
    values_ext = with_rims(values)
    occ_local = occupancy(key_unit, hyperplanes, 2.0**BITS / all_tokens)
    gathered = attend(query_unit, key_unit, values, own_ids, own_ids, head_dim)
    group_kv = []
    for x_far, ids_far in zip(group_x, group_ids):
        key_far, scale_far, value_far = project(x_far, weight_kv, 1, head_dim)
        group_kv.append((key_far, scale_far, value_far))
        gathered = attend(
            query_unit, key_far, value_far, own_ids, ids_far, head_dim, seed=gathered
        )
    mixed = mix(gathered, values_ext, own_ids, ids_ext, conv_taps, head_dim)

    attn_out = tp_sum(nn(mixed, out_weight).astype(BF16))
    first_norm, first_back = jax.vjp(
        layer_norm, inputs.astype(F32) + attn_out, attn_gain, attn_shift
    )
    first_low = first_norm.astype(BF16)
    hidden = nn(first_low, up_weight)
    active = jax.nn.gelu(hidden, approximate=False).astype(BF16)
    ffn_out = tp_sum(nn(active, down_weight).astype(BF16))
    result, second_back = jax.vjp(layer_norm, first_norm + ffn_out, ffn_gain, ffn_shift)
    output = result.astype(BF16)
    grad_second, grad_ffn_gain, grad_ffn_shift = second_back(cotangent.astype(F32))
    grad_ffn = grad_second.astype(BF16)
    grad_active = nt(grad_ffn, down_weight)
    unused_gelu, gelu_back = jax.vjp(partial(jax.nn.gelu, approximate=False), hidden)
    grad_hidden = gelu_back(grad_active)[0].astype(BF16)
    grad_first = grad_second + tp_sum(nt(grad_hidden, up_weight).astype(BF16))
    grad_residual, grad_attn_gain, grad_attn_shift = first_back(grad_first)
    grad_attn = grad_residual.astype(BF16)
    grad_mixed = nt(grad_attn, out_weight).astype(BF16)

    grad_down = tn(active, grad_ffn)
    grad_up = tn(first_low, grad_hidden)
    grad_out = tn(mixed, grad_attn)
    dense = jnp.concatenate(
        [grad_down.reshape(-1, depth), grad_up.reshape(-1, depth), grad_out.reshape(-1, depth)]
    ).astype(BF16)
    dense = lax.psum(dense, "seq")

    grad_rows = back_norm(gathered, grad_mixed, head_dim)
    grad_ext = with_rims(grad_mixed)

    grad_query_turned = None
    kv_weight_grad = None
    homes = None
    for distances, x_far, ids_far, kv_far in reversed(
        list(zip(groups, group_x, group_ids, group_kv))
    ):
        key_far, scale_far, value_far = kv_far
        dk, dv, grad_query_turned = back_attend(
            query_unit,
            grad_rows,
            key_far,
            value_far,
            own_ids,
            ids_far,
            head_dim,
            seed=grad_query_turned,
        )
        need = (
            (ids_far[CHUNK - 1 :: CHUNK] >= own_ids[0]) & (ids_far[::CHUNK] <= own_ids[-1])
        ).astype(jnp.int32)
        dx, dw = back_project(
            x_far, weight_kv, [(key_far, scale_far, dk)], 0, [dv], need, head_dim
        )
        kv_weight_grad = dw if kv_weight_grad is None else kv_weight_grad + dw
        count = len(distances) * half
        both = tp_half_sum(dx[:count], dx[count:])
        for index, distance in enumerate(distances):
            home = shifted(both[index * half : (index + 1) * half], "seq", -distance)
            home = home.astype(F32)
            homes = home if homes is None else homes + home

    dk, dv, grad_query_turned = back_attend(
        query_unit,
        grad_rows,
        key_unit,
        values,
        own_ids,
        own_ids,
        head_dim,
        seed=grad_query_turned,
    )
    grad_conv_values, grad_taps = back_conv(
        values_ext, grad_ext, own_ids, ids_ext, conv_taps, head_dim
    )
    need = jnp.ones((tokens // CHUNK,), jnp.int32)
    dx, dw = back_project(
        inputs,
        weight_qkv,
        [(query_unit, query_scale, grad_query_turned), (key_unit, key_scale, dk)],
        1,
        [dv, grad_conv_values],
        need,
        head_dim,
    )
    mine = lax.dynamic_slice_in_dim(dx, my_side * half, half, 0)
    other = lax.dynamic_slice_in_dim(dx, (1 - my_side) * half, half, 0)
    mine_total = (
        lax.dynamic_slice_in_dim(grad_residual, my_side * half, half, 0)
        + homes
        + tp_half_sum(mine, other).astype(F32)
    )
    other_total = swapped(mine_total, "tp")
    lower = jnp.where(my_side == 0, mine_total, other_total)
    upper = jnp.where(my_side == 0, other_total, mine_total)
    grad_inputs = jnp.concatenate([lower, upper], axis=0)

    qkv = jnp.concatenate([dw[:, :width], dw[:, width:] + kv_weight_grad], axis=1).astype(BF16)
    qkv = lax.psum(qkv, "seq").astype(F32)
    small = lax.psum(
        (grad_taps, grad_attn_gain, grad_attn_shift, grad_ffn_gain, grad_ffn_shift), "seq"
    )
    occ = lax.psum(occ_local, "seq")
    dense = dense.astype(F32)
    ff = down_weight.shape[0]
    return (
        output,
        grad_inputs,
        qkv[:, :width],
        qkv[:, width : 2 * width],
        qkv[:, 2 * width :],
        dense[2 * ff :],
        dense[ff : 2 * ff].reshape(up_weight.shape),
        dense[:ff],
        small[0],
        small[1],
        small[2],
        small[3],
        small[4],
        occ,
    )


def tp_half_sum(mine, other):
    return (mine.astype(F32) + swapped(other, "tp").astype(F32)).astype(BF16)


def solution(mesh):
    return jax.shard_map(
        body,
        mesh=mesh,
        in_specs=(
            P("seq", None),
            P("seq", None),
            P(None, "tp"),
            P(None, "tp"),
            P(None, "tp"),
            P("tp", None),
            P(None, "tp"),
            P("tp", None),
            P("tp", None),
            P(),
            P(),
            P(),
            P(),
            P(),
            P(),
        ),
        out_specs=(
            P("seq", None),
            P("seq", None),
            P(None, "tp"),
            P(None, "tp"),
            P(None, "tp"),
            P("tp", None),
            P(None, "tp"),
            P("tp", None),
            P("tp", None),
            P(),
            P(),
            P(),
            P(),
            P("tp", None, None),
        ),
        check_vma=False,
    )
```

```python
from functools import partial
import math

import jax
import jax.numpy as jnp
from jax import lax
from jax.experimental import pallas as pl
from jax.experimental.pallas import tpu as pltpu
from jax.sharding import PartitionSpec as P

TAU = 8
BITS = 8
CONV = 33
MOST = 4096
RIM = (CONV - 1) // 2

EPS_UNIT = 1e-06
EPS_LAYER = 1e-05
SHARP = 4.0
CLIP_EDGE = 0.999

CHUNK = 512
Q_TILE = 512
Q_TILE_BACK = 256
PAIR = 128
STRIP = 128
FAR_ID = 1 << 20

LIGHT = pl.CostEstimate(flops=1 << 20, bytes_accessed=1 << 16, transcendentals=0)

F32 = jnp.float32
BF16 = jnp.bfloat16

ARC = (
    0.49999961256980896,
    -0.06828052550554276,
    0.027964841574430466,
    -0.014291195198893547,
    0.006136968266218901,
    -0.001371906721033156,
)


def params(**kwargs):
    return pltpu.CompilerParams(vmem_limit_bytes=56 << 20, **kwargs)


def nn(left, right):
    return lax.dot_general(left, right, (((1,), (0,)), ((), ())), preferred_element_type=F32)


def nt(left, right):
    return lax.dot_general(left, right, (((1,), (1,)), ((), ())), preferred_element_type=F32)


def tn(left, right):
    return lax.dot_general(left, right, (((0,), (0,)), ((), ())), preferred_element_type=F32)


def head_masks(head_dim):
    lanes = lax.broadcasted_iota(jnp.int32, (1, PAIR), 1)
    first = (lanes < head_dim).astype(F32)
    return first.astype(BF16), (1.0 - first).astype(BF16)


def head_sum(rows, head_dim):
    here = lax.broadcasted_iota(jnp.int32, (PAIR, PAIR), 0) // head_dim
    there = lax.broadcasted_iota(jnp.int32, (PAIR, PAIR), 1) // head_dim
    ones = (here == there).astype(F32).astype(BF16)
    sums = []
    for start in range(0, rows.shape[1], PAIR):
        part = rows[:, start : start + PAIR]
        high = part.astype(BF16)
        low = (part - high.astype(F32)).astype(BF16)
        sums.append(nn(high, ones) + nn(low, ones))
    return jnp.concatenate(sums, axis=1)


def pick_half(mine_refs, other_ref, kept):
    step = pl.program_id(0)
    for index, ref in enumerate(mine_refs):

        @pl.when(step == index)
        def _():
            kept[...] = ref[...]

    @pl.when(step >= len(mine_refs))
    def _():
        kept[...] = other_ref[...]


def other_spec(count, shape):
    return pl.BlockSpec(shape, lambda i, t: (jnp.maximum(i - count, 0), 0))


def half_specs(count, shape):
    return [pl.BlockSpec(shape, lambda i, t: (0, 0))] * count + [other_spec(count, shape)]


def project_kernel(units, count, head_dim, table, *refs):
    if count:
        mine_refs, other_ref, w_ref = refs[:count], refs[count], refs[count + 1]
        out_refs, kept = refs[count + 2 : -1], refs[-1]
        pick_half(mine_refs, other_ref, kept)
    else:
        kept, w_ref = refs[:2]
        out_refs = refs[2:]
    width = out_refs[-1].shape[1]
    needed = table[pl.num_programs(0) + pl.program_id(0)] > 0

    @pl.when(needed)
    def _():
        whole = nn(kept[...], w_ref[...])
        for index in range(units):
            part = whole[:, index * width : (index + 1) * width]
            scale = lax.rsqrt(head_sum(part * part, head_dim) * (1.0 / head_dim) + EPS_UNIT)
            scale = scale * (1.0 / math.sqrt(head_dim))
            out_refs[2 * index][...] = (part * scale).astype(BF16)
            out_refs[2 * index + 1][...] = scale
        out_refs[-1][...] = whole[:, units * width :].astype(BF16)


def project(table, halves, weight, units, head_dim):
    depth = halves[0].shape[1]
    rows = sum(h.shape[0] for h in halves)
    count = len(halves) - 1
    width = weight.shape[1] // (units + 1)
    row_spec = pl.BlockSpec((CHUNK, width), lambda i, t: (t[i], 0))
    spare = CHUNK if count else 0
    if count:
        x_specs = half_specs(count, (CHUNK, depth))
    else:
        x_specs = [pl.BlockSpec((CHUNK, depth), lambda i, t: (i, 0))]
    unit_shapes = [
        jax.ShapeDtypeStruct((rows + spare, width), BF16),
        jax.ShapeDtypeStruct((rows + spare, width), F32),
    ]
    return pl.pallas_call(
        partial(project_kernel, units, count, head_dim),
        grid_spec=pltpu.PrefetchScalarGridSpec(
            num_scalar_prefetch=1,
            grid=(rows // CHUNK,),
            in_specs=x_specs + [pl.BlockSpec(weight.shape, lambda i, t: (0, 0))],
            out_specs=[row_spec] * (2 * units + 1),
            scratch_shapes=[pltpu.VMEM((CHUNK, depth), BF16)] if count else [],
        ),
        out_shape=unit_shapes * units + [jax.ShapeDtypeStruct((rows + spare, width), BF16)],
        compiler_params=params(),
        cost_estimate=pl.CostEstimate(
            flops=4 * rows * depth * weight.shape[1], bytes_accessed=rows * depth, transcendentals=0
        ),
        name="project",
    )(table, *halves, weight)


def collide_parts(scores):
    size = jnp.minimum(jnp.abs(scores), CLIP_EDGE)
    rest = 1.0 - size
    root = lax.rsqrt(rest)
    poly = ARC[5]
    for factor in ARC[4::-1]:
        poly = poly * size + factor
    angle = (rest * root) * poly
    return size, root, jnp.where(scores < 0.0, angle, 1.0 - angle)


def tile_facts(table, tiles_q, tiles_k, qi, kt, base):
    q_low, q_high = table[qi], table[tiles_q + qi]
    k_low, k_high = table[base + kt], table[base + tiles_k + kt]
    needed = (k_high >= q_low) & (k_low <= q_high)
    whole = (q_low == q_high) & (k_low == k_high)
    return needed, whole


def id_column(row, lanes):
    column = jnp.broadcast_to(row, (PAIR, row.shape[1])).T
    return jnp.concatenate([column] * (lanes // PAIR), axis=1)


def attend_kernel(head_dim, groups, seeded, table, q_ref, qrow_ref, *rest):
    out_ref = rest[-1]
    tiles_q = q_ref.shape[0] // Q_TILE
    masks = head_masks(head_dim)
    if seeded:
        out_ref[...] = rest[-2][...]
    else:
        out_ref[...] = jnp.zeros_like(out_ref)

    base = 2 * tiles_q
    for group in range(groups):
        k_ref, v_ref, krow_ref = rest[3 * group : 3 * group + 3]
        tiles_k = k_ref.shape[0] // CHUNK
        attend_group(
            head_dim, masks, base, tiles_q, tiles_k, table, q_ref, qrow_ref, k_ref, v_ref, krow_ref, out_ref
        )
        base += 2 * tiles_k


def attend_group(
    head_dim, masks, base, tiles_q, tiles_k, table, q_ref, qrow_ref, k_ref, v_ref, krow_ref, out_ref
):
    def q_loop(qi, carry):
        rows = pl.ds(pl.multiple_of(qi * Q_TILE, Q_TILE), Q_TILE)

        def k_loop(kt, inner):
            needed, whole = tile_facts(table, tiles_q, tiles_k, qi, kt, base)

            def part(same):
                cols = pl.ds(pl.multiple_of(kt * CHUNK, CHUNK), CHUNK)
                q, k, v = q_ref[rows, :], k_ref[cols, :], v_ref[cols, :]
                total = None
                for mask in masks:
                    chance = collide_parts(nt(q * mask, k))[2]
                    chance = chance * chance
                    chance = chance * chance
                    chance = chance * chance
                    if same is not None:
                        chance = jnp.where(same, chance, 0.0)
                    term = nn(chance.astype(BF16), v * mask)
                    total = term if total is None else total + term
                out_ref[rows, :] += total

            @pl.when(needed & whole)
            def _():
                part(None)

            @pl.when(needed & jnp.logical_not(whole))
            def _():
                part(id_column(qrow_ref[pl.ds(qi, 1), :], CHUNK) == krow_ref[pl.ds(kt, 1), :])

            return inner

        return lax.fori_loop(0, tiles_k, k_loop, carry)

    lax.fori_loop(0, tiles_q, q_loop, 0)


def attend(table, q, own_ids, sources, head_dim, seed=None):
    tokens, width = q.shape
    q_spec = pl.BlockSpec((tokens, PAIR), lambda p, t: (0, p))
    qrow = own_ids.reshape(-1, Q_TILE)
    operands = [q, qrow]
    specs = [q_spec, pl.BlockSpec(qrow.shape, lambda p, t: (0, 0))]
    rows = 0
    for k, v, ids in sources:
        krow = ids.reshape(-1, CHUNK)
        k_spec = pl.BlockSpec((ids.shape[0], PAIR), lambda p, t: (0, p))
        operands += [k, v, krow]
        specs += [k_spec, k_spec, pl.BlockSpec(krow.shape, lambda p, t: (0, 0))]
        rows += ids.shape[0]
    if seed is not None:
        operands.append(seed)
        specs.append(q_spec)
    return pl.pallas_call(
        partial(attend_kernel, head_dim, len(sources), seed is not None),
        grid_spec=pltpu.PrefetchScalarGridSpec(
            num_scalar_prefetch=1, grid=(width // PAIR,), in_specs=specs, out_specs=q_spec
        ),
        out_shape=jax.ShapeDtypeStruct((tokens, width), F32),
        compiler_params=params(),
        cost_estimate=pl.CostEstimate(
            flops=32 * tokens * rows * width, bytes_accessed=rows * width * 4, transcendentals=0
        ),
        name="attend",
    )(table, *operands)


def back_attend_kernel(
    head_dim, seeded, table, q_ref, g_ref, k_ref, v_ref, qrow_ref, krow_ref, *rest
):
    dk_ref, dv_ref, dq_ref, acc_k, acc_v = rest[-5:]
    tiles_q, tiles_k = q_ref.shape[0] // Q_TILE_BACK, k_ref.shape[0] // CHUNK
    masks = head_masks(head_dim)
    if seeded:
        dq_ref[...] = rest[0][...]
    else:
        dq_ref[...] = jnp.zeros_like(dq_ref)

    def k_loop(kt, carry):
        cols = pl.ds(pl.multiple_of(kt * CHUNK, CHUNK), CHUNK)
        low, high = table[0], table[2 * tiles_q - 1]
        touched = (table[2 * tiles_q + tiles_k + kt] >= low) & (table[2 * tiles_q + kt] <= high)

        def q_loop(qi, inner):
            needed, whole = tile_facts(table, tiles_q, tiles_k, qi, kt, 2 * tiles_q)

            def part(same):
                rows = pl.ds(pl.multiple_of(qi * Q_TILE_BACK, Q_TILE_BACK), Q_TILE_BACK)
                q, g, k, v = q_ref[rows, :], g_ref[rows, :], k_ref[cols, :], v_ref[cols, :]
                k_turned = k.T
                sum_k, sum_v = None, None
                for index, mask in enumerate(masks):
                    q_half, g_half = q * mask, g * mask
                    scores = nt(k, q_half)
                    size, root, chance = collide_parts(scores)
                    second = chance * chance
                    fourth = second * second
                    weights = fourth * fourth
                    slope = (fourth * second) * (chance * (root * lax.rsqrt(1.0 + size)))
                    inside = jnp.abs(scores) <= CLIP_EDGE
                    if same is not None:
                        inside = inside & same
                        weights = jnp.where(same, weights, 0.0)
                    slope = jnp.where(inside, nt(v, g_half) * slope, 0.0).astype(BF16)
                    term_v = nn(weights.astype(BF16), g_half)
                    term_k = nn(slope, q_half)
                    sum_v = term_v if sum_v is None else sum_v + term_v
                    sum_k = term_k if sum_k is None else sum_k + term_k
                    half = slice(index * head_dim, (index + 1) * head_dim)
                    dq_ref[half, rows] += nn(k_turned[half, :], slope)
                acc_v[...] += sum_v
                acc_k[...] += sum_k

            @pl.when(needed & whole)
            def _():
                part(None)

            @pl.when(needed & jnp.logical_not(whole))
            def _():
                ids = id_column(krow_ref[pl.ds(kt, 1), :], Q_TILE_BACK)
                part(ids == qrow_ref[pl.ds(qi, 1), :])

            return inner

        @pl.when(touched)
        def _():
            acc_k[...] = jnp.zeros_like(acc_k)
            acc_v[...] = jnp.zeros_like(acc_v)
            lax.fori_loop(0, tiles_q, q_loop, 0)
            dk_ref[cols, :] = acc_k[...].astype(BF16)
            dv_ref[cols, :] = acc_v[...].astype(BF16)

        @pl.when(jnp.logical_not(touched))
        def _():
            dk_ref[cols, :] = jnp.zeros((CHUNK, PAIR), BF16)
            dv_ref[cols, :] = jnp.zeros((CHUNK, PAIR), BF16)

        return carry

    lax.fori_loop(0, tiles_k, k_loop, 0)


def back_attend(table, q, g, k, v, own_ids, key_ids, head_dim, seed=None, cost=LIGHT):
    tokens, width = q.shape
    far = key_ids.shape[0]
    qrow, krow = own_ids.reshape(-1, Q_TILE_BACK), key_ids.reshape(-1, CHUNK)
    q_spec = pl.BlockSpec((tokens, PAIR), lambda p, t: (0, p))
    k_spec = pl.BlockSpec((far, PAIR), lambda p, t: (0, p))
    dq_spec = pl.BlockSpec((PAIR, tokens), lambda p, t: (p, 0))
    specs = [
        q_spec,
        q_spec,
        k_spec,
        k_spec,
        pl.BlockSpec(qrow.shape, lambda p, t: (0, 0)),
        pl.BlockSpec(krow.shape, lambda p, t: (0, 0)),
    ]
    operands = [q, g, k, v, qrow, krow]
    if seed is not None:
        operands.append(seed)
        specs.append(dq_spec)
    return pl.pallas_call(
        partial(back_attend_kernel, head_dim, seed is not None),
        grid_spec=pltpu.PrefetchScalarGridSpec(
            num_scalar_prefetch=1,
            grid=(width // PAIR,),
            in_specs=specs,
            out_specs=[k_spec, k_spec, dq_spec],
            scratch_shapes=[pltpu.VMEM((CHUNK, PAIR), F32), pltpu.VMEM((CHUNK, PAIR), F32)],
        ),
        out_shape=[
            jax.ShapeDtypeStruct((far, width), BF16),
            jax.ShapeDtypeStruct((far, width), BF16),
            jax.ShapeDtypeStruct((width, tokens), F32),
        ],
        compiler_params=params(),
        cost_estimate=cost,
        name="back_attend",
    )(table, *operands)


def back_project_kernel(units, turned, terms, rims, count, head_dim, table, *refs):
    mine_refs, other_ref, w_ref = refs[:count], refs[count], refs[count + 1]
    dx_mine, dx_other, dw_ref, kept, sum_ref = refs[-5:]
    refs = refs[count + 2 : -5]
    step = pl.program_id(0)
    place, needed = table[step], table[pl.num_programs(0) + step] > 0

    @pl.when(step == 0)
    def _():
        dw_ref[...] = jnp.zeros_like(dw_ref)

    def store(value):
        @pl.when(step < count)
        def _():
            dx_mine[...] = value

        @pl.when(step >= count)
        def _():
            dx_other[...] = value

    @pl.when(needed)
    def _():
        pick_half(mine_refs, other_ref, kept)
        grads = []
        for index in range(units):
            unit_ref, scale_ref, grad_ref = refs[3 * index : 3 * index + 3]
            grad = grad_ref[...].astype(F32)
            if index < turned:
                grad = grad.T
            unit = unit_ref[...].astype(F32)
            inner = head_sum(grad * unit, head_dim)
            grads.append(
                ((TAU / math.pi) * scale_ref[...] * (grad - unit * inner)).astype(BF16)
            )
        value_refs = refs[3 * units : 3 * units + terms]
        value = value_refs[0][...].astype(F32)
        for extra in value_refs[1:]:
            value = value + extra[...].astype(F32)
        if rims is not None:
            rim_ref = refs[-1]
            sum_ref[...] = value

            @pl.when(place == rims)
            def _():
                sum_ref[CHUNK - STRIP :, :] += rim_ref[:STRIP, :]

            @pl.when(place == rims + 1)
            def _():
                sum_ref[:STRIP, :] += rim_ref[STRIP:, :]

            value = sum_ref[...]
        grads.append(value.astype(BF16))
        joined = jnp.concatenate(grads, axis=1)
        store(nt(joined, w_ref[...]).astype(BF16))
        dw_ref[...] += tn(kept[...], joined)

    @pl.when(jnp.logical_not(needed))
    def _():
        store(jnp.zeros(dx_mine.shape, BF16))


def back_project(table, halves, weight, parts, turned, values, head_dim, rims=None, rim=None):
    depth = halves[0].shape[1]
    count = len(halves) - 1
    width = values[0].shape[1]
    row_spec = pl.BlockSpec((CHUNK, width), lambda i, t: (t[4 * count + i], 0))
    weight_spec = pl.BlockSpec(weight.shape, lambda i, t: (0, 0))
    wide_specs = [
        pl.BlockSpec((CHUNK, depth), lambda i, t: (jnp.minimum(i, count - 1), 0)),
        other_spec(count, (CHUNK, depth)),
    ]
    specs = half_specs(count, (CHUNK, depth)) + [weight_spec]
    operands = [*halves, weight]
    for index, (unit, scale, grad) in enumerate(parts):
        operands += [unit, scale, grad]
        specs += [row_spec, row_spec]
        specs.append(
            pl.BlockSpec((width, CHUNK), lambda i, t: (0, t[4 * count + i]))
            if index < turned
            else row_spec
        )
    operands += values
    specs += [row_spec] * len(values)
    if rim is not None:
        operands.append(rim)
        specs.append(pl.BlockSpec(rim.shape, lambda i, t: (0, 0)))
    return pl.pallas_call(
        partial(back_project_kernel, len(parts), turned, len(values), rims, count, head_dim),
        grid_spec=pltpu.PrefetchScalarGridSpec(
            num_scalar_prefetch=1,
            grid=(2 * count,),
            in_specs=specs,
            out_specs=wide_specs + [weight_spec],
            scratch_shapes=[pltpu.VMEM((CHUNK, depth), BF16), pltpu.VMEM((CHUNK, width), F32)],
        ),
        out_shape=[
            jax.ShapeDtypeStruct((count * CHUNK, depth), BF16),
            jax.ShapeDtypeStruct((count * CHUNK, depth), BF16),
            jax.ShapeDtypeStruct(weight.shape, F32),
        ],
        compiler_params=params(),
        cost_estimate=LIGHT,
        name="back_project",
    )(table, *operands)


def band_windows(ids_ext, strips):
    start = STRIP // 2
    return jnp.stack([ids_ext[start + row : start + row + 2 * STRIP] for row in range(0, strips * STRIP, STRIP)])


def lane_taps(conv_taps, mirrored):
    front = STRIP // 2 - RIM
    heads = conv_taps.shape[0]
    taps = conv_taps[:, ::-1] if mirrored else conv_taps
    return jnp.pad(taps, ((0, -heads % 8), (front, 2 * STRIP - front - CONV)))


def fill_bands(taps_ref, bands, heads):
    for head in range(heads):
        row = jnp.broadcast_to(taps_ref[head : head + 1, :], (STRIP, 2 * STRIP))
        bands[head] = pltpu.roll(row, 0, 1, stride=1, stride_axis=0)


def band_product(band, same, window):
    band = jnp.where(same, band, 0.0)
    high = band.astype(BF16)
    low = (band - high.astype(F32)).astype(BF16)
    return nn(high, window) + nn(low, window)


def fill_extended(kept, edge, centre_ref, rim_ref):
    rows = centre_ref.shape[0]
    kept[...] = jnp.zeros_like(kept)
    kept[edge : edge + rows, :] = centre_ref[...]
    if rim_ref is not None:
        kept[edge - RIM : edge, :] = rim_ref[:RIM, :]
        kept[edge + rows : edge + rows + RIM, :] = rim_ref[RIM:, :]


def mix_kernel(head_dim, g_ref, col_ref, v_ref, rim_ref, row_ref, taps_ref, out_ref, bands, kept):
    heads = g_ref.shape[1] // head_dim
    step = pl.program_id(0)

    @pl.when(step == 0)
    def _():
        fill_bands(taps_ref, bands, heads)
        fill_extended(kept, STRIP, v_ref, rim_ref)

    masks = head_masks(head_dim)
    window = kept[pl.ds(pl.multiple_of(step * STRIP + STRIP // 2, STRIP // 2), 2 * STRIP), :]
    ids = col_ref[...]
    same = jnp.concatenate([ids, ids], axis=1) == row_ref[pl.ds(step, 1), :]
    pieces = []
    for pair in range(heads // 2):
        values = window[:, pair * PAIR : (pair + 1) * PAIR]
        total = None
        for index, mask in enumerate(masks):
            term = band_product(bands[2 * pair + index], same, values * mask)
            total = term if total is None else total + term
        pieces.append(total)
    gathered = g_ref[...]
    scale = lax.rsqrt(head_sum(gathered * gathered, head_dim) * (1.0 / head_dim) + EPS_UNIT)
    out_ref[...] = (gathered * scale + jnp.concatenate(pieces, axis=1)).astype(BF16)


def mix(gathered, values, rim, ids_ext, col, conv_taps, head_dim):
    tokens, width = gathered.shape
    heads = width // head_dim
    strips = tokens // STRIP
    row = band_windows(ids_ext[STRIP:], strips)
    taps = lane_taps(conv_taps, False)
    row_spec = pl.BlockSpec((STRIP, width), lambda i: (i, 0))
    whole = [values, rim, row, taps]
    return pl.pallas_call(
        partial(mix_kernel, head_dim),
        grid=(strips,),
        in_specs=[row_spec, pl.BlockSpec((STRIP, PAIR), lambda i: (i + 2, 0))]
        + [pl.BlockSpec(a.shape, lambda i: (0, 0)) for a in whole],
        out_specs=row_spec,
        out_shape=jax.ShapeDtypeStruct((tokens, width), BF16),
        scratch_shapes=[
            pltpu.VMEM((heads, STRIP, 2 * STRIP), F32),
            pltpu.VMEM((tokens + 2 * STRIP, width), BF16),
        ],
        compiler_params=params(),
        cost_estimate=LIGHT,
        name="mix",
    )(gathered, col, *whole)


def back_norm_kernel(head_dim, g_ref, m_ref, out_ref):
    gathered, grad = g_ref[...], m_ref[...].astype(F32)
    scale = lax.rsqrt(head_sum(gathered * gathered, head_dim) * (1.0 / head_dim) + EPS_UNIT)
    mean = head_sum(grad * gathered, head_dim) * (1.0 / head_dim)
    out_ref[...] = (scale * (grad - (scale * scale) * gathered * mean)).astype(BF16)


def back_norm(gathered, grad_mixed, head_dim):
    tokens, width = gathered.shape
    row_spec = pl.BlockSpec((CHUNK, width), lambda i: (i, 0))
    return pl.pallas_call(
        partial(back_norm_kernel, head_dim),
        grid=(tokens // CHUNK,),
        in_specs=[row_spec, row_spec],
        out_specs=row_spec,
        out_shape=jax.ShapeDtypeStruct((tokens, width), BF16),
        compiler_params=params(),
        cost_estimate=LIGHT,
        name="back_norm",
    )(gathered, grad_mixed)


def back_conv_kernel(
    head_dim, col_ref, v_ref, rim_ref, m_ref, row_ref, taps_ref, dv_ref, tap_ref, bands, sums, kept_v, kept_m
):
    heads = dv_ref.shape[1] // head_dim
    step, steps = pl.program_id(0), pl.num_programs(0)

    @pl.when(step == 0)
    def _():
        fill_bands(taps_ref, bands, heads)
        fill_extended(kept_v, 2 * STRIP, v_ref, rim_ref)
        fill_extended(kept_m, 2 * STRIP, m_ref, None)
        sums[...] = jnp.zeros_like(sums)

    masks = head_masks(head_dim)
    around = pl.ds(pl.multiple_of(step * STRIP + STRIP // 2, STRIP // 2), 2 * STRIP)
    centre = pl.ds(pl.multiple_of(step * STRIP + STRIP, STRIP), STRIP)
    ids = col_ref[...]
    same = jnp.concatenate([ids, ids], axis=1) == row_ref[pl.ds(step, 1), :]
    pieces = []
    for pair in range(heads // 2):
        cols = slice(pair * PAIR, (pair + 1) * PAIR)
        grads, values, here = kept_m[around, cols], kept_v[around, cols], kept_m[centre, cols]
        total = None
        for index, mask in enumerate(masks):
            head = 2 * pair + index
            term = band_product(bands[head], same, grads * mask)
            total = term if total is None else total + term
            sums[head] += jnp.where(same, nt(here * mask, values), 0.0)
        pieces.append(total)
    dv_ref[...] = jnp.concatenate(pieces, axis=1)

    @pl.when(step == steps - 1)
    def _():
        tap_ref[...] = jnp.zeros_like(tap_ref)
        places = [lax.broadcasted_iota(jnp.int32, (STRIP, STRIP), d) for d in (0, 1)]
        flip = (places[0] + places[1] == STRIP - 1).astype(F32).astype(BF16)
        for head in range(heads):
            total = sums[head]
            high = total.astype(BF16)
            low = (total - high.astype(F32)).astype(BF16)
            turned = pltpu.roll(
                nn(flip, high) + nn(flip, low), STRIP + 1, 1, stride=1, stride_axis=0
            )
            tap_ref[head : head + 1, :] = jnp.sum(turned, axis=0, keepdims=True)


def back_conv(values, rim, grad_mixed, ids_ext, col, conv_taps, head_dim):
    tokens, width = values.shape
    heads = width // head_dim
    strips = tokens // STRIP + 2
    row = band_windows(ids_ext, strips)
    taps = lane_taps(conv_taps, True)
    front = STRIP // 2 - RIM
    whole = [values, rim, grad_mixed, row, taps]
    grad_values, tap_sums = pl.pallas_call(
        partial(back_conv_kernel, head_dim),
        grid=(strips,),
        in_specs=[pl.BlockSpec((STRIP, PAIR), lambda i: (i + 1, 0))]
        + [pl.BlockSpec(a.shape, lambda i: (0, 0)) for a in whole],
        out_specs=[
            pl.BlockSpec((STRIP, width), lambda i: (i, 0)),
            pl.BlockSpec(taps.shape, lambda i: (0, 0)),
        ],
        out_shape=[
            jax.ShapeDtypeStruct((strips * STRIP, width), F32),
            jax.ShapeDtypeStruct(taps.shape, F32),
        ],
        scratch_shapes=[
            pltpu.VMEM((heads, STRIP, 2 * STRIP), F32),
            pltpu.VMEM((heads, STRIP, 2 * STRIP), F32),
            pltpu.VMEM((tokens + 4 * STRIP, width), BF16),
            pltpu.VMEM((tokens + 4 * STRIP, width), BF16),
        ],
        compiler_params=params(),
        cost_estimate=LIGHT,
        name="back_conv",
    )(col, *whole)
    return grad_values, tap_sums[:heads, front : front + CONV]


def occupancy_kernel(hashes, k_ref, w_ref, out_ref, counts):
    combos = 4
    lanes = hashes * combos
    side = combos * combos
    wide = hashes * side

    @pl.when(pl.program_id(1) == 0)
    def _():
        counts[...] = jnp.zeros_like(counts)

    source = lax.broadcasted_iota(jnp.int32, (lanes, wide), 0)
    target = lax.broadcasted_iota(jnp.int32, (lanes, wide), 1)
    same_hash = (source // combos) == (target // side)
    picks = []
    for divisor in (1, combos):
        chosen = same_hash & ((source % combos) == ((target // divisor) % combos))
        picks.append(chosen.astype(F32).astype(BF16))
    keys = k_ref[...]
    for index in range(2):
        signed = nn(keys, w_ref[index])
        halves = []
        for half in range(2):
            product = None
            for pick in range(2):
                start = (half * 2 + pick) * 2 * lanes
                one = 1.0 + jnp.exp(-signed[:, start : start + lanes])
                two = 1.0 + jnp.exp(-signed[:, start + lanes : start + 2 * lanes])
                spread = nn((1.0 / (one * two)).astype(BF16), picks[pick])
                product = spread if product is None else product * spread
            halves.append(product.astype(BF16))
        low, high = halves
        for start in range(0, wide, PAIR):
            block = slice(start, start + PAIR)
            counts[index, block, :] += tn(high[:, block], low[:, block])

    @pl.when(pl.program_id(1) == pl.num_programs(1) - 1)
    def _():
        row = lax.broadcasted_iota(jnp.int32, (wide, PAIR), 0)
        lane = lax.broadcasted_iota(jnp.int32, (wide, PAIR), 1)
        diagonal = ((row % PAIR) // side) == (lane // side)
        fold = [lax.broadcasted_iota(jnp.int32, (PAIR, side * side), d) for d in (0, 1)]
        fold = ((fold[0] % side) == (fold[1] % side)).astype(F32).astype(BF16)
        spot = [lax.broadcasted_iota(jnp.int32, (wide, side * side), d) for d in (0, 1)]
        kept = (spot[0] % side) == (spot[1] // side)
        home = [lax.broadcasted_iota(jnp.int32, (hashes, wide), d) for d in (0, 1)]
        home = (home[0] == home[1] // side).astype(F32).astype(BF16)
        for index in range(2):
            left = jnp.where(diagonal, counts[index], 0.0)
            total = None
            for _ in range(3):
                piece = left.astype(BF16)
                left = left - piece.astype(F32)
                spread = jnp.where(kept, nn(piece, fold), 0.0).astype(BF16)
                term = nn(home, spread)
                total = term if total is None else total + term
            out_ref[index] = total


def occupancy(key_unit, hyperplanes, scale):
    tokens, width = key_unit.shape
    hashes, bits, head_dim = hyperplanes.shape
    pairs = width // PAIR
    wide = hashes * 16
    planes = SHARP * hyperplanes.astype(F32)
    columns = []
    for group in range(bits // 2):
        for bit in range(2):
            signs = 2.0 * ((jnp.arange(4) // (2**bit)) % 2).astype(F32) - 1.0
            plane = planes[:, 2 * group + bit, :]
            columns.append((plane.T[:, :, None] * signs).reshape(head_dim, hashes * 4))
    weight = jnp.concatenate(columns, axis=1).astype(BF16)
    blank = jnp.zeros_like(weight)
    weights = jnp.stack(
        [jnp.concatenate([weight, blank], axis=0), jnp.concatenate([blank, weight], axis=0)]
    )
    counts = pl.pallas_call(
        partial(occupancy_kernel, hashes),
        grid=(pairs, tokens // CHUNK),
        in_specs=[
            pl.BlockSpec((CHUNK, PAIR), lambda p, t: (t, p)),
            pl.BlockSpec(weights.shape, lambda p, t: (0, 0, 0)),
        ],
        out_specs=pl.BlockSpec((2, hashes, 256), lambda p, t: (p, 0, 0)),
        out_shape=jax.ShapeDtypeStruct((2 * pairs, hashes, 256), F32),
        scratch_shapes=[pltpu.VMEM((2, wide, PAIR), F32)],
        compiler_params=params(),
        cost_estimate=pl.CostEstimate(
            flops=tokens * width * 32000, bytes_accessed=tokens * width * 4, transcendentals=0
        ),
        name="occupancy",
    )(key_unit, weights)
    return counts * scale


PLANE = 4


def sum_plan(n, rows):
    unit = 16 * n
    units = -(-rows // unit)
    first = -(-2 * units // 3)
    streams = [(0, first * unit, True)]
    if units > first:
        streams.append((first * unit, (units - first) * unit, False))
    return units * unit, streams


def sum_kernel(n, streams, split, *refs):
    count = len(streams)
    table_ref, misc_ref = refs[:2]
    outs, misc_out = refs[2 : 2 + split], refs[2 + split]
    scratch = refs[3 + split :]
    send, recv = scratch[-2:]
    me = lax.axis_index("seq")
    groups = n // PLANE
    near_me, far_me = lax.rem(me, PLANE), me // PLANE

    def device(plane_first, one, two):
        return {"seq": two * PLANE + one if plane_first else one * PLANE + two}

    barrier = pltpu.get_barrier_semaphore()
    for step in range(1, PLANE):
        pl.semaphore_signal(
            barrier, 1, device_id=device(True, lax.rem(near_me + step, PLANE), far_me)
        )
    for step in range(1, groups):
        pl.semaphore_signal(
            barrier, 1, device_id=device(True, near_me, lax.rem(far_me + step, groups))
        )
    pl.semaphore_wait(barrier, PLANE - 1 + groups - 1)

    facts = []
    for index, (base, rows, plane_first) in enumerate(streams):
        sizes = (PLANE, groups) if plane_first else (groups, PLANE)
        mine = (near_me, far_me) if plane_first else (far_me, near_me)
        buffers = scratch[5 * index : 5 * index + 5]
        source = misc_ref if index == count - 1 else table_ref
        block, chunk = rows // sizes[0], rows // n
        facts.append((index, source, base, plane_first, sizes, mine, block, chunk, buffers))

    def at(start, number):
        return pl.ds(pl.multiple_of(start, 8), number)

    def start_all(phase):
        started = []
        for index, source, base, plane_first, sizes, mine, block, chunk, buffers in facts:
            got_one, part, got_two, merged, full = buffers
            side = 0 if phase in (0, 3) else 1
            for step in range(1, sizes[side]):
                to = lax.rem(mine[side] + step, sizes[side])
                if phase == 0:
                    src, dst = source.at[at(base + to * block, block), :], got_one.at[step - 1]
                elif phase == 1:
                    src, dst = part.at[at(to * chunk, chunk), :], got_two.at[step - 1]
                elif phase == 2:
                    src = dst = merged.at[at(mine[1] * chunk, chunk), :]
                else:
                    src, dst = merged, full.at[at(mine[0] * block, block), :]
                pair = (to, mine[1]) if side == 0 else (mine[0], to)
                copy = pltpu.make_async_remote_copy(
                    src_ref=src,
                    dst_ref=dst,
                    send_sem=send.at[index, phase, step - 1],
                    recv_sem=recv.at[index, phase, step - 1],
                    device_id=device(plane_first, *pair),
                    device_id_type=pl.DeviceIdType.MESH,
                )
                copy.start()
                started.append(copy)
        return started

    def wait_all(started):
        for copy in started:
            copy.wait()

    wait_all(start_all(0))
    for index, source, base, plane_first, sizes, mine, block, chunk, buffers in facts:
        got_one, part, got_two, merged, full = buffers

        def add(piece, carry):
            rows = at(piece * chunk, chunk)
            total = source[at(base + mine[0] * block + piece * chunk, chunk), :].astype(F32)
            for step in range(sizes[0] - 1):
                total = total + got_one[step, rows, :].astype(F32)
            part[rows, :] = total.astype(part.dtype)
            return carry

        lax.fori_loop(0, sizes[1], add, 0)
    wait_all(start_all(1))
    for index, source, base, plane_first, sizes, mine, block, chunk, buffers in facts:
        got_one, part, got_two, merged, full = buffers
        rows = at(mine[1] * chunk, chunk)
        total = part[rows, :].astype(F32)
        for step in range(sizes[1] - 1):
            total = total + got_two[step].astype(F32)
        merged[rows, :] = total.astype(merged.dtype)
    wait_all(start_all(2))
    started = start_all(3)
    for index, source, base, plane_first, sizes, mine, block, chunk, buffers in facts:
        merged, full = buffers[3:]
        full[at(mine[0] * block, block), :] = merged[...]
    wait_all(started)
    for index, source, base, plane_first, sizes, mine, block, chunk, buffers in facts:
        full = buffers[4]

        def put(piece, carry):
            rows = at(piece * chunk, chunk)
            if index == count - 1:
                misc_out[rows, :] = full[rows, :]
            else:
                there = at(base + piece * chunk, chunk)
                for part_index, out in enumerate(outs):
                    width = out.shape[1]
                    lanes = slice(part_index * width, (part_index + 1) * width)
                    out[there, :] = full[rows, lanes].astype(F32)
            return carry

        lax.fori_loop(0, n, put, 0)


def sum_over_seq(table, misc, split):
    n = lax.axis_size("seq")
    rows, width = table.shape
    padded, streams = sum_plan(n, rows)
    if padded > rows:
        table = jnp.pad(table, ((0, padded - rows), (0, 0)))
    lanes = -(-misc.size // (8 * n * PAIR)) * PAIR
    misc_table = jnp.pad(misc, (0, 8 * n * lanes - misc.size)).reshape(8 * n, lanes)
    streams = streams + [(0, 8 * n, True)]
    scratch = []
    for index, (_, stream_rows, plane_first) in enumerate(streams):
        last = index == len(streams) - 1
        kind, lane_count = (F32, lanes) if last else (BF16, width)
        one, two = (PLANE, n // PLANE) if plane_first else (n // PLANE, PLANE)
        block, chunk = stream_rows // one, stream_rows // n
        scratch += [
            pltpu.VMEM((one - 1, block, lane_count), kind),
            pltpu.VMEM((block, lane_count), kind),
            pltpu.VMEM((two - 1, chunk, lane_count), kind),
            pltpu.VMEM((block, lane_count), kind),
            pltpu.VMEM((stream_rows, lane_count), kind),
        ]
    partners = max(PLANE, n // PLANE) - 1
    sems = pltpu.SemaphoreType.DMA((len(streams), 4, partners))
    in_vmem = pl.BlockSpec(memory_space=pltpu.VMEM)
    shapes = [jax.ShapeDtypeStruct((padded, width // split), F32)] * split
    *sums, misc_sum = pl.pallas_call(
        partial(sum_kernel, n, streams, split),
        in_specs=[in_vmem, in_vmem],
        out_specs=[in_vmem] * (split + 1),
        out_shape=shapes + [jax.ShapeDtypeStruct(misc_table.shape, F32)],
        scratch_shapes=scratch + [sems, sems],
        compiler_params=params(collective_id=0, has_side_effects=True),
        cost_estimate=pl.CostEstimate(flops=1 << 36, bytes_accessed=1 << 24, transcendentals=0),
        name="sum_over_seq",
    )(table, misc_table)
    return [total[:rows] for total in sums], misc_sum.reshape(-1)[: misc.size]


def doc_ids(lengths, positions, all_tokens):
    doc_ends = jnp.cumsum(lengths)
    doc_index = jnp.sum((doc_ends[None, :] <= positions[:, None]).astype(jnp.int32), axis=1)
    doc_index = jnp.where(positions < 0, -1, doc_index)
    return jnp.where(positions >= all_tokens, FAR_ID, doc_index)


def shifted(block, axis, distance):
    count = lax.axis_size(axis)
    route = [(i, i + distance) for i in range(count) if 0 <= i + distance < count]
    return lax.ppermute(block, axis, route)


def swapped(block, axis):
    return lax.ppermute(block, axis, [(0, 1), (1, 0)])


def tp_sum(partial_low):
    return partial_low.astype(F32) + swapped(partial_low, "tp").astype(F32)


def after(value, *others):
    return lax.optimization_barrier((value, *others))[0]


def layer_norm(vectors, gain_row, shift_row):
    center = vectors - jnp.mean(vectors, axis=-1, keepdims=True)
    spread = jnp.mean(center * center, axis=-1, keepdims=True)
    return center * lax.rsqrt(spread + EPS_LAYER) * gain_row + shift_row


def body(
    inputs,
    cotangent,
    query_weight,
    key_weight,
    value_weight,
    out_weight,
    up_weight,
    down_weight,
    conv_taps,
    attn_gain,
    attn_shift,
    ffn_gain,
    ffn_shift,
    hyperplanes,
    lengths,
):
    tokens, depth = inputs.shape
    head_dim = hyperplanes.shape[2]
    width = query_weight.shape[1]
    half = tokens // 2
    my_index = lax.axis_index("seq")
    my_side = lax.axis_index("tp")
    all_tokens = tokens * lax.axis_size("seq")
    far_reach = (MOST + tokens - 2) // tokens
    close = far_reach // 2
    near = list(range(close, 0, -1)) + list(range(-1, -close - 1, -1))
    far = list(range(far_reach, close, -1)) + list(range(-close - 1, -far_reach - 1, -1))
    groups = [near, far]
    first_token = my_index * tokens

    mine_rows = lax.dynamic_slice_in_dim(inputs, my_side * half, half, 0)
    near_mine = [shifted(mine_rows, "seq", d) for d in near]

    def ids_at(positions):
        return doc_ids(lengths, positions, all_tokens)

    def span(start, count, step=1):
        return start + step * jnp.arange(count, dtype=jnp.int32)

    ids_ext = ids_at(span(first_token - 2 * STRIP, tokens + 4 * STRIP))
    ids_col = jnp.broadcast_to(ids_ext[:, None], (ids_ext.shape[0], PAIR))
    own_ids = ids_at(span(first_token, tokens))
    q_count = tokens // Q_TILE_BACK
    k_starts = [
        jnp.concatenate([span(first_token - d * tokens, tokens // CHUNK, CHUNK) for d in part])
        for part in groups + [[0]]
    ]
    k_counts = [starts.shape[0] for starts in k_starts]
    q_starts = span(first_token, q_count, Q_TILE_BACK)
    ends = ids_at(
        jnp.concatenate(
            [q_starts, q_starts + Q_TILE_BACK - 1]
            + [starts + extra for starts in k_starts for extra in (0, CHUNK - 1)]
        )
    )
    q_low, q_high = ends[:q_count], ends[q_count : 2 * q_count]
    ratio = Q_TILE // Q_TILE_BACK
    q_ends = [q_low[::ratio], q_high[ratio - 1 :: ratio]]
    tables, back_tables, chunk_tables, fill_tables, needs, group_ids = [], [], [], [], [], []
    spot = 2 * q_count
    for starts, count in zip(k_starts, k_counts):
        pieces = ends[spot : spot + 2 * count]
        spot += 2 * count
        tables.append(pieces)
        back_tables.append(jnp.concatenate([q_low, q_high, pieces]))
        need = ((pieces[count:] >= q_low[0]) & (pieces[:count] <= q_high[-1])).astype(jnp.int32)
        need = need.reshape(-1, 2)
        places = span(0, count).reshape(-1, 2)
        ordered = []
        for pair in (places, need):
            mine = jnp.where(my_side == 0, pair[:, 0], pair[:, 1])
            other = jnp.where(my_side == 0, pair[:, 1], pair[:, 0])
            ordered += [mine, other]
        place = jnp.concatenate(ordered[:2])
        wanted = jnp.concatenate(ordered[2:])
        chunk_tables.append(jnp.concatenate([place, wanted, place * wanted]))
        fill_tables.append(jnp.concatenate([jnp.where(wanted > 0, place, count), wanted]))
        needs.append(need)
        group_ids.append(
            ids_at((starts[:, None] + jnp.arange(CHUNK, dtype=jnp.int32)).reshape(-1))
        )
    near_at, far_at, own_at = range(3)

    weight_qkv = jnp.concatenate([query_weight, key_weight, value_weight], axis=1)
    weight_kv = weight_qkv[:, width:]
    plain_table = jnp.array(list(range(tokens // CHUNK)) + [1] * (tokens // CHUNK), jnp.int32)
    query_unit, query_scale, key_unit, key_scale, values = project(
        plain_table, [inputs], weight_qkv, 2, head_dim
    )
    gathered = attend(
        jnp.concatenate([*q_ends, tables[own_at]]),
        query_unit,
        own_ids,
        [(key_unit, values, own_ids)],
        head_dim,
    )

    def other_half(mine):
        return jnp.concatenate([swapped(term, "tp") for term in mine], axis=0)

    *near_mine, late_rows = after((*near_mine, mine_rows), gathered)
    far_mine = [shifted(late_rows, "seq", d) for d in far]
    near_other = other_half(near_mine)
    occ_local = occupancy(after(key_unit, *near_mine), hyperplanes, 2.0**BITS / all_tokens)
    near_x = [*near_mine, after(near_other, occ_local)]
    near_kv = project(fill_tables[near_at], near_x, weight_kv, 1, head_dim)
    *far_mine, query_late = after((*far_mine, query_unit), *near_kv)
    far_other = other_half(far_mine)
    gathered = attend(
        jnp.concatenate([*q_ends, tables[near_at]]),
        query_late,
        own_ids,
        [(near_kv[0], near_kv[2], group_ids[near_at])],
        head_dim,
        seed=gathered,
    )
    far_x = [*far_mine, after(far_other, gathered)]
    far_kv = project(fill_tables[far_at], far_x, weight_kv, 1, head_dim)
    gathered = attend(
        jnp.concatenate([*q_ends, tables[far_at]]),
        query_unit,
        own_ids,
        [(far_kv[0], far_kv[2], group_ids[far_at])],
        head_dim,
        seed=gathered,
    )
    group_x, group_kv = [near_x, far_x], [near_kv, far_kv]
    edge = close * tokens
    sides = needs[near_at].reshape(-1)[edge // CHUNK - 1 : edge // CHUNK + 1]
    values_rim = jnp.where(
        jnp.repeat(sides, RIM)[:, None] > 0, group_kv[near_at][2][edge - RIM : edge + RIM], 0
    )
    mixed = mix(gathered, values, values_rim, ids_ext, ids_col, conv_taps, head_dim)

    attn_out = tp_sum(nn(mixed, out_weight).astype(BF16))
    first_norm, first_back = jax.vjp(
        layer_norm, inputs.astype(F32) + attn_out, attn_gain, attn_shift
    )
    first_low = first_norm.astype(BF16)
    hidden = nn(first_low, up_weight)
    active = jax.nn.gelu(hidden, approximate=False).astype(BF16)
    ffn_out = tp_sum(nn(active, down_weight).astype(BF16))
    result, second_back = jax.vjp(layer_norm, first_norm + ffn_out, ffn_gain, ffn_shift)
    output = result.astype(BF16)
    grad_second, grad_ffn_gain, grad_ffn_shift = second_back(cotangent.astype(F32))
    grad_ffn = grad_second.astype(BF16)
    grad_active = nt(grad_ffn, down_weight)
    unused_gelu, gelu_back = jax.vjp(partial(jax.nn.gelu, approximate=False), hidden)
    grad_hidden = gelu_back(grad_active)[0].astype(BF16)
    grad_first = grad_second + tp_sum(nt(grad_hidden, up_weight).astype(BF16))
    grad_residual, grad_attn_gain, grad_attn_shift = first_back(grad_first)
    grad_attn = grad_residual.astype(BF16)
    grad_mixed = nt(grad_attn, out_weight).astype(BF16)

    grad_down = tn(active, grad_ffn).astype(BF16)
    grad_up = tn(first_low, grad_hidden).astype(BF16)
    grad_out = tn(mixed, grad_attn).astype(BF16)
    down_out = jnp.concatenate([grad_down, grad_out], axis=0)
    grad_up_low, down_out_low = grad_up, down_out
    grad_up, down_out = lax.psum((grad_up_low, down_out_low), "seq")

    grad_rows = back_norm(gathered, after(grad_mixed, grad_up_low, down_out_low), head_dim)

    def back_scores(index, grad_rows, seed):
        key_far, _, value_far = group_kv[index]
        return back_attend(
            back_tables[index],
            query_unit,
            grad_rows,
            key_far,
            value_far,
            own_ids,
            group_ids[index],
            head_dim,
            seed=seed,
        )

    def back_inputs(index, dk, dv, **rims):
        key_far, scale_far, _ = group_kv[index]
        parts = [(key_far, scale_far, dk)]
        return back_project(
            chunk_tables[index], group_x[index], weight_kv, parts, 0, [dv], head_dim, **rims
        )

    def send_home(distances, dx_mine, came):
        both = [
            (
                dx_mine[i * half : (i + 1) * half].astype(F32)
                + came[i * half : (i + 1) * half].astype(F32)
            ).astype(BF16)
            for i in range(len(distances))
        ]
        return both, [shifted(term, "seq", -d) for term, d in zip(both, distances)]

    dk, dv, turned = back_scores(far_at, grad_rows, None)
    far_dx, dx_other, far_dw = back_inputs(far_at, dk, dv)
    far_came = swapped(dx_other, "tp")
    grad_conv_values, grad_taps = back_conv(
        values, values_rim, after(grad_mixed, far_dx), ids_ext, ids_col, conv_taps, head_dim
    )
    rim = jnp.concatenate([grad_conv_values[:STRIP], grad_conv_values[-STRIP:]], axis=0)
    dk, dv, turned = back_scores(near_at, after(grad_rows, grad_conv_values), turned)
    near_dx, dx_other, near_dw = back_inputs(
        near_at, dk, dv, rims=close * (tokens // CHUNK) - 1, rim=rim
    )
    near_came = swapped(dx_other, "tp")
    far_came, grad_up, down_out = after((far_came, grad_up, down_out), near_dx)
    terms, far_homes = send_home(far, far_dx, far_came)
    dk, dv, turned = back_attend(
        back_tables[own_at],
        query_unit,
        after(grad_rows, *terms),
        key_unit,
        values,
        own_ids,
        own_ids,
        head_dim,
        seed=turned,
        cost=pl.CostEstimate(flops=1 << 35, bytes_accessed=1 << 20, transcendentals=0),
    )
    terms, near_homes = send_home(near, near_dx, after(near_came, dk))
    dk, far_homes = after((dk, far_homes), *terms)
    own_mine = mine_rows
    own_other = lax.dynamic_slice_in_dim(inputs, (1 - my_side) * half, half, 0)
    dx_mine, dx_other, dw = back_project(
        chunk_tables[own_at],
        [own_mine, own_other],
        weight_qkv,
        [(query_unit, query_scale, turned), (key_unit, key_scale, dk)],
        1,
        [dv, grad_conv_values[STRIP:-STRIP]],
        head_dim,
    )

    qkv = jnp.concatenate([dw[:, :width], dw[:, width:] + near_dw + far_dw], axis=1).astype(BF16)
    misc = [
        occ_local,
        grad_taps,
        grad_attn_gain,
        grad_attn_shift,
        grad_ffn_gain,
        grad_ffn_shift,
    ]
    packed = jnp.concatenate([term.reshape(-1) for term in misc])
    qkv, packed = sum_over_seq(qkv, packed, 3)

    came = swapped(dx_other, "tp")
    near_homes = after(tuple(near_homes), packed)
    total = (
        lax.dynamic_slice_in_dim(grad_residual, my_side * half, half, 0)
        + dx_mine.astype(F32)
        + came.astype(F32)
    )
    for home in (*far_homes, *near_homes):
        total = total + home.astype(F32)
    other_total = swapped(total, "tp")
    lower = jnp.where(my_side == 0, total, other_total)
    upper = jnp.where(my_side == 0, other_total, total)
    grad_inputs = jnp.concatenate([lower, upper], axis=0)

    unpacked, at = [], 0
    for term in misc:
        unpacked.append(packed[at : at + term.size].reshape(term.shape))
        at += term.size
    down_out = down_out.astype(F32)
    ff = down_weight.shape[0]
    return (
        output,
        grad_inputs,
        *qkv,
        down_out[ff:],
        grad_up.astype(F32),
        down_out[:ff],
        *unpacked[1:],
        unpacked[0],
    )


def solution(mesh):
    return jax.shard_map(
        body,
        mesh=mesh,
        in_specs=(
            P("seq", None),
            P("seq", None),
            P(None, "tp"),
            P(None, "tp"),
            P(None, "tp"),
            P("tp", None),
            P(None, "tp"),
            P("tp", None),
            P("tp", None),
            P(),
            P(),
            P(),
            P(),
            P(),
            P(),
        ),
        out_specs=(
            P("seq", None),
            P("seq", None),
            P(None, "tp"),
            P(None, "tp"),
            P(None, "tp"),
            P("tp", None),
            P(None, "tp"),
            P("tp", None),
            P("tp", None),
            P(),
            P(),
            P(),
            P(),
            P("tp", None, None),
        ),
        check_vma=False,
    )
```

```python
from functools import partial
import math

import jax
import jax.numpy as jnp
from jax import lax
from jax.experimental import pallas as pl
from jax.experimental.pallas import tpu as pltpu
from jax.sharding import PartitionSpec as P

TAU = 8
BITS = 8
CONV = 33
MOST = 4096
RIM = (CONV - 1) // 2

EPS_UNIT = 1e-06
EPS_LAYER = 1e-05
SHARP = 4.0
CLIP_EDGE = 0.999

CHUNK = 512
Q_TILE = 512
Q_TILE_BACK = 256
PAIR = 128
STRIP = 128
FAR_ID = 1 << 20

LIGHT = pl.CostEstimate(flops=1 << 20, bytes_accessed=1 << 16, transcendentals=0)

F32 = jnp.float32
BF16 = jnp.bfloat16

ARC = (
    0.49999961256980896,
    -0.06828052550554276,
    0.027964841574430466,
    -0.014291195198893547,
    0.006136968266218901,
    -0.001371906721033156,
)


def params(**kwargs):
    return pltpu.CompilerParams(vmem_limit_bytes=56 << 20, **kwargs)


def nn(left, right):
    return lax.dot_general(left, right, (((1,), (0,)), ((), ())), preferred_element_type=F32)


def nt(left, right):
    return lax.dot_general(left, right, (((1,), (1,)), ((), ())), preferred_element_type=F32)


def tn(left, right):
    return lax.dot_general(left, right, (((0,), (0,)), ((), ())), preferred_element_type=F32)


def head_masks(head_dim):
    lanes = lax.broadcasted_iota(jnp.int32, (1, PAIR), 1)
    first = (lanes < head_dim).astype(F32)
    return first.astype(BF16), (1.0 - first).astype(BF16)


def head_sum(rows, head_dim):
    here = lax.broadcasted_iota(jnp.int32, (PAIR, PAIR), 0) // head_dim
    there = lax.broadcasted_iota(jnp.int32, (PAIR, PAIR), 1) // head_dim
    ones = (here == there).astype(F32).astype(BF16)
    sums = []
    for start in range(0, rows.shape[1], PAIR):
        part = rows[:, start : start + PAIR]
        high = part.astype(BF16)
        low = (part - high.astype(F32)).astype(BF16)
        sums.append(nn(high, ones) + nn(low, ones))
    return jnp.concatenate(sums, axis=1)


def pick_half(mine_refs, other_ref, kept):
    step = pl.program_id(0)
    for index, ref in enumerate(mine_refs):

        @pl.when(step == index)
        def _():
            kept[...] = ref[...]

    @pl.when(step >= len(mine_refs))
    def _():
        kept[...] = other_ref[...]


def other_spec(count, shape):
    return pl.BlockSpec(shape, lambda i, t: (jnp.maximum(i - count, 0), 0))


def half_specs(count, shape):
    return [pl.BlockSpec(shape, lambda i, t: (0, 0))] * count + [other_spec(count, shape)]


def project_kernel(units, count, joined, head_dim, table, *refs):
    if count:
        mine_refs, other_ref, w_ref = refs[:count], refs[count], refs[count + 1]
        out_refs, kept = refs[count + 2 + joined : -1], refs[-1]
        pick_half(mine_refs, other_ref, kept)
    else:
        kept, w_ref = refs[:2]
        out_refs = refs[2:]
    width = out_refs[-1].shape[1]
    needed = table[pl.num_programs(0) + pl.program_id(0)] > 0

    @pl.when(needed)
    def _():
        whole = nn(kept[...], w_ref[...])
        for index in range(units):
            part = whole[:, index * width : (index + 1) * width]
            scale = lax.rsqrt(head_sum(part * part, head_dim) * (1.0 / head_dim) + EPS_UNIT)
            scale = scale * (1.0 / math.sqrt(head_dim))
            out_refs[2 * index][...] = (part * scale).astype(BF16)
            out_refs[2 * index + 1][...] = scale
        out_refs[-1][...] = whole[:, units * width :].astype(BF16)


def project(table, halves, weight, units, head_dim, chunks=None, into=()):
    depth = halves[0].shape[1]
    rows = sum(h.shape[0] for h in halves)
    count = len(halves) - 1
    width = weight.shape[1] // (units + 1)
    row_spec = pl.BlockSpec((CHUNK, width), lambda i, t: (t[i], 0))
    held = (chunks + 1) * CHUNK if count else rows
    if count:
        x_specs = half_specs(count, (CHUNK, depth))
    else:
        x_specs = [pl.BlockSpec((CHUNK, depth), lambda i, t: (i, 0))]
    unit_shapes = [
        jax.ShapeDtypeStruct((held, width), BF16),
        jax.ShapeDtypeStruct((held, width), F32),
    ]
    return pl.pallas_call(
        partial(project_kernel, units, count, len(into), head_dim),
        grid_spec=pltpu.PrefetchScalarGridSpec(
            num_scalar_prefetch=1,
            grid=(rows // CHUNK,),
            in_specs=x_specs
            + [pl.BlockSpec(weight.shape, lambda i, t: (0, 0))]
            + [pl.BlockSpec(memory_space=pl.ANY)] * len(into),
            out_specs=[row_spec] * (2 * units + 1),
            scratch_shapes=[pltpu.VMEM((CHUNK, depth), BF16)] if count else [],
        ),
        out_shape=unit_shapes * units + [jax.ShapeDtypeStruct((held, width), BF16)],
        input_output_aliases={len(halves) + 2 + i: i for i in range(len(into))},
        compiler_params=params(),
        cost_estimate=pl.CostEstimate(
            flops=4 * rows * depth * weight.shape[1], bytes_accessed=rows * depth, transcendentals=0
        ),
        name="project",
    )(table, *halves, weight, *into)


def collide(scores):
    size = jnp.minimum(jnp.abs(scores), CLIP_EDGE)
    rest = 1.0 - size
    poly = ARC[5]
    for factor in ARC[4::-1]:
        poly = poly * size + factor
    angle = (rest * lax.rsqrt(rest)) * poly
    return jnp.where(scores < 0.0, angle, 1.0 - angle)


def tile_facts(table, tiles_q, tiles_k, qi, kt):
    q_low, q_high = table[qi], table[tiles_q + qi]
    k_low, k_high = table[2 * tiles_q + kt], table[2 * tiles_q + tiles_k + kt]
    needed = (k_high >= q_low) & (k_low <= q_high)
    whole = (q_low == q_high) & (k_low == k_high)
    return needed, whole


def tile_table(q_low, q_high, k_low, k_high, first, last):
    need = (k_high[first:last] >= q_low[0]) & (k_low[first:last] <= q_high[-1])
    count = jnp.sum(need.astype(jnp.int32))
    steps = jnp.arange(last - first, dtype=jnp.int32)
    place = jnp.cumsum(need.astype(jnp.int32)) - 1
    wanted = jnp.minimum(steps, jnp.maximum(count - 1, 0))
    chosen = need[None, :] & (place[None, :] == wanted[:, None])
    order = jnp.sum(jnp.where(chosen, steps[None, :], 0), axis=1) + first
    return jnp.concatenate([q_low, q_high, k_low, k_high, order, count[None]])


def id_column(row, lanes):
    column = jnp.broadcast_to(row, (PAIR, row.shape[1])).T
    return jnp.concatenate([column] * (lanes // PAIR), axis=1)


def attend_kernel(
    head_dim, tiles_k, seeded, table, q_ref, qrow_ref, krow_ref, k_ref, v_ref, *rest
):
    out_ref, w_ref = rest[-2:]
    tiles_q = q_ref.shape[0] // Q_TILE
    step, steps = pl.program_id(1), pl.num_programs(1)
    order = 2 * (tiles_q + tiles_k)
    masks = head_masks(head_dim)

    @pl.when(step == 0)
    def _():
        if seeded:
            out_ref[...] = rest[0][...]
        else:
            out_ref[...] = jnp.zeros_like(out_ref)

    @pl.when(step < table[order + steps])
    def _():
        kt = table[order + step]

        def q_loop(qi, carry):
            rows = pl.ds(pl.multiple_of(qi * Q_TILE, Q_TILE), Q_TILE)
            needed, whole = tile_facts(table, tiles_q, tiles_k, qi, kt)

            def part(same):
                q, k = q_ref[rows, :], k_ref[...]
                v_turned = v_ref[...].T
                for index, mask in enumerate(masks):
                    chance = collide(nt(k, q * mask))
                    chance = chance * chance
                    chance = chance * chance
                    chance = chance * chance
                    if same is not None:
                        chance = jnp.where(same, chance, 0.0)
                    weights = chance.astype(BF16)
                    w_ref[index, :, rows] = weights
                    half = slice(index * head_dim, (index + 1) * head_dim)
                    out_ref[half, rows] += nn(v_turned[half, :], weights)

            @pl.when(needed & whole)
            def _():
                part(None)

            @pl.when(needed & jnp.logical_not(whole))
            def _():
                part(id_column(krow_ref[pl.ds(kt, 1), :], Q_TILE) == qrow_ref[pl.ds(qi, 1), :])

            @pl.when(jnp.logical_not(needed))
            def _():
                w_ref[:, :, rows] = jnp.zeros((2, CHUNK, Q_TILE), BF16)

            return carry

        lax.fori_loop(0, tiles_q, q_loop, 0)


def attend(table, q, k, v, own_ids, key_ids, head_dim, seed=None):
    tokens, width = q.shape
    tiles_k = key_ids.shape[0] // CHUNK
    order = 2 * (tokens // Q_TILE + tiles_k)
    qrow, krow = own_ids.reshape(-1, Q_TILE), key_ids.reshape(-1, CHUNK)
    k_spec = pl.BlockSpec((CHUNK, PAIR), lambda p, j, t: (t[order + j], p))
    turned_spec = pl.BlockSpec((PAIR, tokens), lambda p, j, t: (p, 0))
    operands = [q, qrow, krow, k, v]
    specs = [
        pl.BlockSpec((tokens, PAIR), lambda p, j, t: (0, p)),
        pl.BlockSpec(qrow.shape, lambda p, j, t: (0, 0)),
        pl.BlockSpec(krow.shape, lambda p, j, t: (0, 0)),
        k_spec,
        k_spec,
    ]
    if seed is not None:
        operands.append(seed)
        specs.append(turned_spec)
    return pl.pallas_call(
        partial(attend_kernel, head_dim, tiles_k, seed is not None),
        grid_spec=pltpu.PrefetchScalarGridSpec(
            num_scalar_prefetch=1,
            grid=(width // PAIR, tiles_k),
            in_specs=specs,
            out_specs=[
                turned_spec,
                pl.BlockSpec((2, CHUNK, tokens), lambda p, j, t: (p, t[order + j], 0)),
            ],
        ),
        out_shape=[
            jax.ShapeDtypeStruct((width, tokens), F32),
            jax.ShapeDtypeStruct((width // head_dim, tiles_k * CHUNK, tokens), BF16),
        ],
        compiler_params=params(),
        cost_estimate=pl.CostEstimate(
            flops=32 * tokens * tiles_k * CHUNK * width,
            bytes_accessed=tokens * width * 4,
            transcendentals=0,
        ),
        name="attend",
    )(table, *operands)


def back_attend_kernel(
    head_dim, tiles_k, seeded, table, q_ref, g_ref, k_ref, v_ref, w_ref, *rest
):
    dk_ref, dv_ref, dq_ref, acc_k, acc_v = rest[-5:]
    tiles_q = q_ref.shape[0] // Q_TILE_BACK
    step, steps = pl.program_id(1), pl.num_programs(1)
    order = 2 * (tiles_q + tiles_k)
    masks = head_masks(head_dim)

    @pl.when(step == 0)
    def _():
        if seeded:
            dq_ref[...] = rest[0][...]
        else:
            dq_ref[...] = jnp.zeros_like(dq_ref)

    @pl.when(step < table[order + steps])
    def _():
        kt = table[order + step]
        acc_k[...] = jnp.zeros_like(acc_k)
        acc_v[...] = jnp.zeros_like(acc_v)

        def q_loop(qi, carry):
            needed, _ = tile_facts(table, tiles_q, tiles_k, qi, kt)

            @pl.when(needed)
            def _():
                rows = pl.ds(pl.multiple_of(qi * Q_TILE_BACK, Q_TILE_BACK), Q_TILE_BACK)
                q, g, k, v = q_ref[rows, :], g_ref[rows, :], k_ref[...], v_ref[...]
                k_turned = k.T
                sum_k, sum_v = None, None
                for index, mask in enumerate(masks):
                    q_half, g_half = q * mask, g * mask
                    scores = nt(k, q_half)
                    weights = w_ref[index, :, rows]
                    power = jnp.exp(((TAU - 1) / TAU) * jnp.log(weights.astype(F32)))
                    square = scores * scores
                    slope = nt(v, g_half) * (power * lax.rsqrt(1.0 - square))
                    slope = jnp.where(square <= CLIP_EDGE * CLIP_EDGE, slope, 0.0).astype(BF16)
                    term_v = nn(weights, g_half)
                    term_k = nn(slope, q_half)
                    sum_v = term_v if sum_v is None else sum_v + term_v
                    sum_k = term_k if sum_k is None else sum_k + term_k
                    half = slice(index * head_dim, (index + 1) * head_dim)
                    dq_ref[half, rows] += nn(k_turned[half, :], slope)
                acc_v[...] += sum_v
                acc_k[...] += sum_k

            return carry

        lax.fori_loop(0, tiles_q, q_loop, 0)
        dk_ref[...] = acc_k[...].astype(BF16)
        dv_ref[...] = acc_v[...].astype(BF16)


def back_attend(table, steps, first, tiles_k, q, g, k, v, weights, head_dim, seed=None, cost=LIGHT):
    tokens, width = q.shape
    order = 2 * (tokens // Q_TILE_BACK + tiles_k)
    q_spec = pl.BlockSpec((tokens, PAIR), lambda p, j, t: (0, p))
    k_spec = pl.BlockSpec((CHUNK, PAIR), lambda p, j, t: (t[order + j], p))
    dk_spec = pl.BlockSpec((CHUNK, PAIR), lambda p, j, t: (t[order + j] - first, p))
    dq_spec = pl.BlockSpec((PAIR, tokens), lambda p, j, t: (p, 0))
    specs = [
        q_spec,
        q_spec,
        k_spec,
        k_spec,
        pl.BlockSpec((2, CHUNK, tokens), lambda p, j, t: (p, t[order + j], 0)),
    ]
    operands = [q, g, k, v, weights]
    if seed is not None:
        operands.append(seed)
        specs.append(dq_spec)
    return pl.pallas_call(
        partial(back_attend_kernel, head_dim, tiles_k, seed is not None),
        grid_spec=pltpu.PrefetchScalarGridSpec(
            num_scalar_prefetch=1,
            grid=(width // PAIR, steps),
            in_specs=specs,
            out_specs=[dk_spec, dk_spec, dq_spec],
            scratch_shapes=[pltpu.VMEM((CHUNK, PAIR), F32), pltpu.VMEM((CHUNK, PAIR), F32)],
        ),
        out_shape=[
            jax.ShapeDtypeStruct((steps * CHUNK, width), BF16),
            jax.ShapeDtypeStruct((steps * CHUNK, width), BF16),
            jax.ShapeDtypeStruct((width, tokens), F32),
        ],
        compiler_params=params(),
        cost_estimate=cost,
        name="back_attend",
    )(table, *operands)


def back_project_kernel(units, turned, terms, rims, count, head_dim, table, *refs):
    mine_refs, other_ref, w_ref = refs[:count], refs[count], refs[count + 1]
    dx_mine, dx_other, dw_ref, kept, sum_ref = refs[-5:]
    refs = refs[count + 2 : -5]
    step = pl.program_id(0)
    place, needed = table[step], table[pl.num_programs(0) + step] > 0

    @pl.when(step == 0)
    def _():
        dw_ref[...] = jnp.zeros_like(dw_ref)

    def store(value):
        @pl.when(step < count)
        def _():
            dx_mine[...] = value

        @pl.when(step >= count)
        def _():
            dx_other[...] = value

    @pl.when(needed)
    def _():
        pick_half(mine_refs, other_ref, kept)
        grads = []
        for index in range(units):
            unit_ref, scale_ref, grad_ref = refs[3 * index : 3 * index + 3]
            grad = grad_ref[...].astype(F32)
            if index < turned:
                grad = grad.T
            unit = unit_ref[...].astype(F32)
            inner = head_sum(grad * unit, head_dim)
            grads.append(
                ((TAU / math.pi) * scale_ref[...] * (grad - unit * inner)).astype(BF16)
            )
        value_refs = refs[3 * units : 3 * units + terms]
        value = value_refs[0][...].astype(F32)
        for extra in value_refs[1:]:
            value = value + extra[...].astype(F32)
        if rims is not None:
            rim_ref = refs[-1]
            sum_ref[...] = value

            @pl.when(place == rims)
            def _():
                sum_ref[CHUNK - STRIP :, :] += rim_ref[:STRIP, :]

            @pl.when(place == rims + 1)
            def _():
                sum_ref[:STRIP, :] += rim_ref[STRIP:, :]

            value = sum_ref[...]
        grads.append(value.astype(BF16))
        joined = jnp.concatenate(grads, axis=1)
        store(nt(joined, w_ref[...]).astype(BF16))
        dw_ref[...] += tn(kept[...], joined)

    @pl.when(jnp.logical_not(needed))
    def _():
        store(jnp.zeros(dx_mine.shape, BF16))


def back_project(table, halves, weight, parts, turned, values, head_dim, first=0, rims=None, rim=None):
    depth = halves[0].shape[1]
    count = len(halves) - 1
    width = values[0].shape[1]
    row_spec = pl.BlockSpec((CHUNK, width), lambda i, t: (t[4 * count + i], 0))
    unit_spec = pl.BlockSpec((CHUNK, width), lambda i, t: (t[4 * count + i] + first, 0))
    weight_spec = pl.BlockSpec(weight.shape, lambda i, t: (0, 0))
    wide_specs = [
        pl.BlockSpec((CHUNK, depth), lambda i, t: (jnp.minimum(i, count - 1), 0)),
        other_spec(count, (CHUNK, depth)),
    ]
    specs = half_specs(count, (CHUNK, depth)) + [weight_spec]
    operands = [*halves, weight]
    for index, (unit, scale, grad) in enumerate(parts):
        operands += [unit, scale, grad]
        specs += [unit_spec, unit_spec]
        specs.append(
            pl.BlockSpec((width, CHUNK), lambda i, t: (0, t[4 * count + i]))
            if index < turned
            else row_spec
        )
    operands += values
    specs += [row_spec] * len(values)
    if rim is not None:
        operands.append(rim)
        specs.append(pl.BlockSpec(rim.shape, lambda i, t: (0, 0)))
    return pl.pallas_call(
        partial(back_project_kernel, len(parts), turned, len(values), rims, count, head_dim),
        grid_spec=pltpu.PrefetchScalarGridSpec(
            num_scalar_prefetch=1,
            grid=(2 * count,),
            in_specs=specs,
            out_specs=wide_specs + [weight_spec],
            scratch_shapes=[pltpu.VMEM((CHUNK, depth), BF16), pltpu.VMEM((CHUNK, width), F32)],
        ),
        out_shape=[
            jax.ShapeDtypeStruct((count * CHUNK, depth), BF16),
            jax.ShapeDtypeStruct((count * CHUNK, depth), BF16),
            jax.ShapeDtypeStruct(weight.shape, F32),
        ],
        compiler_params=params(),
        cost_estimate=LIGHT,
        name="back_project",
    )(table, *operands)


def band_windows(ids_ext, strips):
    start = STRIP // 2
    return jnp.stack([ids_ext[start + row : start + row + 2 * STRIP] for row in range(0, strips * STRIP, STRIP)])


def lane_taps(conv_taps, mirrored):
    front = STRIP // 2 - RIM
    heads = conv_taps.shape[0]
    taps = conv_taps[:, ::-1] if mirrored else conv_taps
    return jnp.pad(taps, ((0, -heads % 8), (front, 2 * STRIP - front - CONV)))


def fill_bands(taps_ref, bands, heads):
    for head in range(heads):
        row = jnp.broadcast_to(taps_ref[head : head + 1, :], (STRIP, 2 * STRIP))
        bands[head] = pltpu.roll(row, 0, 1, stride=1, stride_axis=0)


def band_product(band, same, window):
    band = jnp.where(same, band, 0.0)
    high = band.astype(BF16)
    low = (band - high.astype(F32)).astype(BF16)
    return nn(high, window) + nn(low, window)


def fill_extended(kept, edge, centre_ref, rim_ref):
    rows = centre_ref.shape[0]
    kept[...] = jnp.zeros_like(kept)
    kept[edge : edge + rows, :] = centre_ref[...]
    if rim_ref is not None:
        kept[edge - RIM : edge, :] = rim_ref[:RIM, :]
        kept[edge + rows : edge + rows + RIM, :] = rim_ref[RIM:, :]


def mix_kernel(head_dim, g_ref, col_ref, v_ref, rim_ref, row_ref, taps_ref, out_ref, bands, kept):
    heads = g_ref.shape[0] // head_dim
    step = pl.program_id(0)

    @pl.when(step == 0)
    def _():
        fill_bands(taps_ref, bands, heads)
        fill_extended(kept, STRIP, v_ref, rim_ref)

    masks = head_masks(head_dim)
    window = kept[pl.ds(pl.multiple_of(step * STRIP + STRIP // 2, STRIP // 2), 2 * STRIP), :]
    ids = col_ref[...]
    same = jnp.concatenate([ids, ids], axis=1) == row_ref[pl.ds(step, 1), :]
    pieces = []
    for pair in range(heads // 2):
        values = window[:, pair * PAIR : (pair + 1) * PAIR]
        total = None
        for index, mask in enumerate(masks):
            term = band_product(bands[2 * pair + index], same, values * mask)
            total = term if total is None else total + term
        pieces.append(total)
    gathered = g_ref[...].T
    scale = lax.rsqrt(head_sum(gathered * gathered, head_dim) * (1.0 / head_dim) + EPS_UNIT)
    out_ref[...] = (gathered * scale + jnp.concatenate(pieces, axis=1)).astype(BF16)


def mix(gathered, values, rim, ids_ext, col, conv_taps, head_dim):
    width, tokens = gathered.shape
    heads = width // head_dim
    strips = tokens // STRIP
    row = band_windows(ids_ext[STRIP:], strips)
    taps = lane_taps(conv_taps, False)
    row_spec = pl.BlockSpec((STRIP, width), lambda i: (i, 0))
    whole = [values, rim, row, taps]
    return pl.pallas_call(
        partial(mix_kernel, head_dim),
        grid=(strips,),
        in_specs=[
            pl.BlockSpec((width, STRIP), lambda i: (0, i)),
            pl.BlockSpec((STRIP, PAIR), lambda i: (i + 2, 0)),
        ]
        + [pl.BlockSpec(a.shape, lambda i: (0, 0)) for a in whole],
        out_specs=row_spec,
        out_shape=jax.ShapeDtypeStruct((tokens, width), BF16),
        scratch_shapes=[
            pltpu.VMEM((heads, STRIP, 2 * STRIP), F32),
            pltpu.VMEM((tokens + 2 * STRIP, width), BF16),
        ],
        compiler_params=params(),
        cost_estimate=LIGHT,
        name="mix",
    )(gathered, col, *whole)


def back_norm_kernel(head_dim, g_ref, m_ref, out_ref):
    gathered, grad = g_ref[...].T, m_ref[...].astype(F32)
    scale = lax.rsqrt(head_sum(gathered * gathered, head_dim) * (1.0 / head_dim) + EPS_UNIT)
    mean = head_sum(grad * gathered, head_dim) * (1.0 / head_dim)
    out_ref[...] = (scale * (grad - (scale * scale) * gathered * mean)).astype(BF16)


def back_norm(gathered, grad_mixed, head_dim):
    width, tokens = gathered.shape
    row_spec = pl.BlockSpec((CHUNK, width), lambda i: (i, 0))
    return pl.pallas_call(
        partial(back_norm_kernel, head_dim),
        grid=(tokens // CHUNK,),
        in_specs=[pl.BlockSpec((width, CHUNK), lambda i: (0, i)), row_spec],
        out_specs=row_spec,
        out_shape=jax.ShapeDtypeStruct((tokens, width), BF16),
        compiler_params=params(),
        cost_estimate=LIGHT,
        name="back_norm",
    )(gathered, grad_mixed)


def back_conv_kernel(
    head_dim, col_ref, v_ref, rim_ref, m_ref, row_ref, taps_ref, dv_ref, tap_ref, bands, sums, kept_v, kept_m
):
    heads = dv_ref.shape[1] // head_dim
    step, steps = pl.program_id(0), pl.num_programs(0)

    @pl.when(step == 0)
    def _():
        fill_bands(taps_ref, bands, heads)
        fill_extended(kept_v, 2 * STRIP, v_ref, rim_ref)
        fill_extended(kept_m, 2 * STRIP, m_ref, None)
        sums[...] = jnp.zeros_like(sums)

    masks = head_masks(head_dim)
    around = pl.ds(pl.multiple_of(step * STRIP + STRIP // 2, STRIP // 2), 2 * STRIP)
    centre = pl.ds(pl.multiple_of(step * STRIP + STRIP, STRIP), STRIP)
    ids = col_ref[...]
    same = jnp.concatenate([ids, ids], axis=1) == row_ref[pl.ds(step, 1), :]
    pieces = []
    for pair in range(heads // 2):
        cols = slice(pair * PAIR, (pair + 1) * PAIR)
        grads, values, here = kept_m[around, cols], kept_v[around, cols], kept_m[centre, cols]
        total = None
        for index, mask in enumerate(masks):
            head = 2 * pair + index
            term = band_product(bands[head], same, grads * mask)
            total = term if total is None else total + term
            sums[head] += jnp.where(same, nt(here * mask, values), 0.0)
        pieces.append(total)
    dv_ref[...] = jnp.concatenate(pieces, axis=1)

    @pl.when(step == steps - 1)
    def _():
        tap_ref[...] = jnp.zeros_like(tap_ref)
        places = [lax.broadcasted_iota(jnp.int32, (STRIP, STRIP), d) for d in (0, 1)]
        flip = (places[0] + places[1] == STRIP - 1).astype(F32).astype(BF16)
        for head in range(heads):
            total = sums[head]
            high = total.astype(BF16)
            low = (total - high.astype(F32)).astype(BF16)
            turned = pltpu.roll(
                nn(flip, high) + nn(flip, low), STRIP + 1, 1, stride=1, stride_axis=0
            )
            tap_ref[head : head + 1, :] = jnp.sum(turned, axis=0, keepdims=True)


def back_conv(values, rim, grad_mixed, ids_ext, col, conv_taps, head_dim):
    tokens, width = values.shape
    heads = width // head_dim
    strips = tokens // STRIP + 2
    row = band_windows(ids_ext, strips)
    taps = lane_taps(conv_taps, True)
    front = STRIP // 2 - RIM
    whole = [values, rim, grad_mixed, row, taps]
    grad_values, tap_sums = pl.pallas_call(
        partial(back_conv_kernel, head_dim),
        grid=(strips,),
        in_specs=[pl.BlockSpec((STRIP, PAIR), lambda i: (i + 1, 0))]
        + [pl.BlockSpec(a.shape, lambda i: (0, 0)) for a in whole],
        out_specs=[
            pl.BlockSpec((STRIP, width), lambda i: (i, 0)),
            pl.BlockSpec(taps.shape, lambda i: (0, 0)),
        ],
        out_shape=[
            jax.ShapeDtypeStruct((strips * STRIP, width), F32),
            jax.ShapeDtypeStruct(taps.shape, F32),
        ],
        scratch_shapes=[
            pltpu.VMEM((heads, STRIP, 2 * STRIP), F32),
            pltpu.VMEM((heads, STRIP, 2 * STRIP), F32),
            pltpu.VMEM((tokens + 4 * STRIP, width), BF16),
            pltpu.VMEM((tokens + 4 * STRIP, width), BF16),
        ],
        compiler_params=params(),
        cost_estimate=LIGHT,
        name="back_conv",
    )(col, *whole)
    return grad_values, tap_sums[:heads, front : front + CONV]


def occupancy_kernel(hashes, k_ref, w_ref, out_ref, counts):
    combos = 4
    lanes = hashes * combos
    side = combos * combos
    wide = hashes * side

    @pl.when(pl.program_id(1) == 0)
    def _():
        counts[...] = jnp.zeros_like(counts)

    source = lax.broadcasted_iota(jnp.int32, (lanes, wide), 0)
    target = lax.broadcasted_iota(jnp.int32, (lanes, wide), 1)
    same_hash = (source // combos) == (target // side)
    picks = []
    for divisor in (1, combos):
        chosen = same_hash & ((source % combos) == ((target // divisor) % combos))
        picks.append(chosen.astype(F32).astype(BF16))
    keys = k_ref[...]
    for index in range(2):
        signed = nn(keys, w_ref[index])
        halves = []
        for half in range(2):
            product = None
            for pick in range(2):
                start = (half * 2 + pick) * 2 * lanes
                one = 1.0 + jnp.exp(-signed[:, start : start + lanes])
                two = 1.0 + jnp.exp(-signed[:, start + lanes : start + 2 * lanes])
                spread = nn((1.0 / (one * two)).astype(BF16), picks[pick])
                product = spread if product is None else product * spread
            halves.append(product.astype(BF16))
        low, high = halves
        for start in range(0, wide, PAIR):
            block = slice(start, start + PAIR)
            counts[index, block, :] += tn(high[:, block], low[:, block])

    @pl.when(pl.program_id(1) == pl.num_programs(1) - 1)
    def _():
        row = lax.broadcasted_iota(jnp.int32, (wide, PAIR), 0)
        lane = lax.broadcasted_iota(jnp.int32, (wide, PAIR), 1)
        diagonal = ((row % PAIR) // side) == (lane // side)
        fold = [lax.broadcasted_iota(jnp.int32, (PAIR, side * side), d) for d in (0, 1)]
        fold = ((fold[0] % side) == (fold[1] % side)).astype(F32).astype(BF16)
        spot = [lax.broadcasted_iota(jnp.int32, (wide, side * side), d) for d in (0, 1)]
        kept = (spot[0] % side) == (spot[1] // side)
        home = [lax.broadcasted_iota(jnp.int32, (hashes, wide), d) for d in (0, 1)]
        home = (home[0] == home[1] // side).astype(F32).astype(BF16)
        for index in range(2):
            left = jnp.where(diagonal, counts[index], 0.0)
            total = None
            for _ in range(3):
                piece = left.astype(BF16)
                left = left - piece.astype(F32)
                spread = jnp.where(kept, nn(piece, fold), 0.0).astype(BF16)
                term = nn(home, spread)
                total = term if total is None else total + term
            out_ref[index] = total


def occupancy(key_unit, hyperplanes, scale):
    tokens, width = key_unit.shape
    hashes, bits, head_dim = hyperplanes.shape
    pairs = width // PAIR
    wide = hashes * 16
    planes = SHARP * hyperplanes.astype(F32)
    columns = []
    for group in range(bits // 2):
        for bit in range(2):
            signs = 2.0 * ((jnp.arange(4) // (2**bit)) % 2).astype(F32) - 1.0
            plane = planes[:, 2 * group + bit, :]
            columns.append((plane.T[:, :, None] * signs).reshape(head_dim, hashes * 4))
    weight = jnp.concatenate(columns, axis=1).astype(BF16)
    blank = jnp.zeros_like(weight)
    weights = jnp.stack(
        [jnp.concatenate([weight, blank], axis=0), jnp.concatenate([blank, weight], axis=0)]
    )
    counts = pl.pallas_call(
        partial(occupancy_kernel, hashes),
        grid=(pairs, tokens // CHUNK),
        in_specs=[
            pl.BlockSpec((CHUNK, PAIR), lambda p, t: (t, p)),
            pl.BlockSpec(weights.shape, lambda p, t: (0, 0, 0)),
        ],
        out_specs=pl.BlockSpec((2, hashes, 256), lambda p, t: (p, 0, 0)),
        out_shape=jax.ShapeDtypeStruct((2 * pairs, hashes, 256), F32),
        scratch_shapes=[pltpu.VMEM((2, wide, PAIR), F32)],
        compiler_params=params(),
        cost_estimate=pl.CostEstimate(
            flops=tokens * width * 32000, bytes_accessed=tokens * width * 4, transcendentals=0
        ),
        name="occupancy",
    )(key_unit, weights)
    return counts * scale


BELL_STEP = 0.3275911
BELL = (0.254829592, -0.284496736, 1.421413741, -1.453152027, 1.061405429)


def feed_kernel(x_ref, up_ref, down_ref, out_ref, active_ref, slope_ref):
    hidden = nn(x_ref[...], up_ref[...])
    size = jnp.abs(hidden)
    step = 1.0 / (1.0 + (BELL_STEP / math.sqrt(2.0)) * size)
    poly = BELL[4]
    for factor in BELL[3::-1]:
        poly = poly * step + factor
    bell = jnp.exp(-0.5 * (hidden * hidden))
    tail = (0.5 * step) * (poly * bell)
    phi = jnp.where(hidden < 0.0, tail, 1.0 - tail)
    active = (hidden * phi).astype(BF16)
    active_ref[...] = active
    slope_ref[...] = (phi + hidden * (bell * (1.0 / math.sqrt(2.0 * math.pi)))).astype(BF16)
    out_ref[...] = nn(active, down_ref[...]).astype(BF16)


def feed(x, up_weight, down_weight):
    tokens, depth = x.shape
    hidden = up_weight.shape[1]
    rows = 256
    wide = pl.BlockSpec((rows, hidden), lambda i: (i, 0))
    narrow = pl.BlockSpec((rows, depth), lambda i: (i, 0))
    return pl.pallas_call(
        feed_kernel,
        grid=(tokens // rows,),
        in_specs=[
            narrow,
            pl.BlockSpec(up_weight.shape, lambda i: (0, 0)),
            pl.BlockSpec(down_weight.shape, lambda i: (0, 0)),
        ],
        out_specs=[narrow, wide, wide],
        out_shape=[
            jax.ShapeDtypeStruct((tokens, depth), BF16),
            jax.ShapeDtypeStruct((tokens, hidden), BF16),
            jax.ShapeDtypeStruct((tokens, hidden), BF16),
        ],
        compiler_params=params(),
        cost_estimate=LIGHT,
        name="feed",
    )(x, up_weight, down_weight)


PLANE = 4


def sum_plan(n, rows):
    unit = 16 * n
    units = -(-rows // unit)
    first = -(-2 * units // 3)
    streams = [(0, first * unit, True)]
    if units > first:
        streams.append((first * unit, (units - first) * unit, False))
    return units * unit, streams


def sum_kernel(n, streams, split, *refs):
    count = len(streams)
    table_ref, misc_ref = refs[:2]
    outs, misc_out = refs[2 : 2 + split], refs[2 + split]
    scratch = refs[3 + split :]
    send, recv = scratch[-2:]
    me = lax.axis_index("seq")
    groups = n // PLANE
    near_me, far_me = lax.rem(me, PLANE), me // PLANE

    def device(plane_first, one, two):
        return {"seq": two * PLANE + one if plane_first else one * PLANE + two}

    barrier = pltpu.get_barrier_semaphore()
    for step in range(1, PLANE):
        pl.semaphore_signal(
            barrier, 1, device_id=device(True, lax.rem(near_me + step, PLANE), far_me)
        )
    for step in range(1, groups):
        pl.semaphore_signal(
            barrier, 1, device_id=device(True, near_me, lax.rem(far_me + step, groups))
        )
    pl.semaphore_wait(barrier, PLANE - 1 + groups - 1)

    facts = []
    for index, (base, rows, plane_first) in enumerate(streams):
        sizes = (PLANE, groups) if plane_first else (groups, PLANE)
        mine = (near_me, far_me) if plane_first else (far_me, near_me)
        buffers = scratch[5 * index : 5 * index + 5]
        source = misc_ref if index == count - 1 else table_ref
        block, chunk = rows // sizes[0], rows // n
        facts.append((index, source, base, plane_first, sizes, mine, block, chunk, buffers))

    def at(start, number):
        return pl.ds(pl.multiple_of(start, 8), number)

    def start_all(phase):
        started = []
        for index, source, base, plane_first, sizes, mine, block, chunk, buffers in facts:
            got_one, part, got_two, merged, full = buffers
            side = 0 if phase in (0, 3) else 1
            for step in range(1, sizes[side]):
                to = lax.rem(mine[side] + step, sizes[side])
                if phase == 0:
                    src, dst = source.at[at(base + to * block, block), :], got_one.at[step - 1]
                elif phase == 1:
                    src, dst = part.at[at(to * chunk, chunk), :], got_two.at[step - 1]
                elif phase == 2:
                    src = dst = merged.at[at(mine[1] * chunk, chunk), :]
                else:
                    src, dst = merged, full.at[at(mine[0] * block, block), :]
                pair = (to, mine[1]) if side == 0 else (mine[0], to)
                copy = pltpu.make_async_remote_copy(
                    src_ref=src,
                    dst_ref=dst,
                    send_sem=send.at[index, phase, step - 1],
                    recv_sem=recv.at[index, phase, step - 1],
                    device_id=device(plane_first, *pair),
                    device_id_type=pl.DeviceIdType.MESH,
                )
                copy.start()
                started.append(copy)
        return started

    def wait_all(started):
        for copy in started:
            copy.wait()

    wait_all(start_all(0))
    for index, source, base, plane_first, sizes, mine, block, chunk, buffers in facts:
        got_one, part, got_two, merged, full = buffers

        def add(piece, carry):
            rows = at(piece * chunk, chunk)
            total = source[at(base + mine[0] * block + piece * chunk, chunk), :].astype(F32)
            for step in range(sizes[0] - 1):
                total = total + got_one[step, rows, :].astype(F32)
            part[rows, :] = total.astype(part.dtype)
            return carry

        lax.fori_loop(0, sizes[1], add, 0)
    wait_all(start_all(1))
    for index, source, base, plane_first, sizes, mine, block, chunk, buffers in facts:
        got_one, part, got_two, merged, full = buffers
        rows = at(mine[1] * chunk, chunk)
        total = part[rows, :].astype(F32)
        for step in range(sizes[1] - 1):
            total = total + got_two[step].astype(F32)
        merged[rows, :] = total.astype(merged.dtype)
    wait_all(start_all(2))
    started = start_all(3)
    for index, source, base, plane_first, sizes, mine, block, chunk, buffers in facts:
        merged, full = buffers[3:]
        full[at(mine[0] * block, block), :] = merged[...]
    wait_all(started)
    for index, source, base, plane_first, sizes, mine, block, chunk, buffers in facts:
        full = buffers[4]

        def put(piece, carry):
            rows = at(piece * chunk, chunk)
            if index == count - 1:
                misc_out[rows, :] = full[rows, :]
            else:
                there = at(base + piece * chunk, chunk)
                for part_index, out in enumerate(outs):
                    width = out.shape[1]
                    lanes = slice(part_index * width, (part_index + 1) * width)
                    out[there, :] = full[rows, lanes].astype(F32)
            return carry

        lax.fori_loop(0, n, put, 0)


def sum_over_seq(table, misc, split):
    n = lax.axis_size("seq")
    rows, width = table.shape
    padded, streams = sum_plan(n, rows)
    if padded > rows:
        table = jnp.pad(table, ((0, padded - rows), (0, 0)))
    lanes = -(-misc.size // (8 * n * PAIR)) * PAIR
    misc_table = jnp.pad(misc, (0, 8 * n * lanes - misc.size)).reshape(8 * n, lanes)
    streams = streams + [(0, 8 * n, True)]
    scratch = []
    for index, (_, stream_rows, plane_first) in enumerate(streams):
        last = index == len(streams) - 1
        kind, lane_count = (F32, lanes) if last else (BF16, width)
        one, two = (PLANE, n // PLANE) if plane_first else (n // PLANE, PLANE)
        block, chunk = stream_rows // one, stream_rows // n
        scratch += [
            pltpu.VMEM((one - 1, block, lane_count), kind),
            pltpu.VMEM((block, lane_count), kind),
            pltpu.VMEM((two - 1, chunk, lane_count), kind),
            pltpu.VMEM((block, lane_count), kind),
            pltpu.VMEM((stream_rows, lane_count), kind),
        ]
    partners = max(PLANE, n // PLANE) - 1
    sems = pltpu.SemaphoreType.DMA((len(streams), 4, partners))
    in_vmem = pl.BlockSpec(memory_space=pltpu.VMEM)
    shapes = [jax.ShapeDtypeStruct((padded, width // split), F32)] * split
    *sums, misc_sum = pl.pallas_call(
        partial(sum_kernel, n, streams, split),
        in_specs=[in_vmem, in_vmem],
        out_specs=[in_vmem] * (split + 1),
        out_shape=shapes + [jax.ShapeDtypeStruct(misc_table.shape, F32)],
        scratch_shapes=scratch + [sems, sems],
        compiler_params=params(collective_id=0, has_side_effects=True),
        cost_estimate=pl.CostEstimate(flops=1 << 36, bytes_accessed=1 << 24, transcendentals=0),
        name="sum_over_seq",
    )(table, misc_table)
    return [total[:rows] for total in sums], misc_sum.reshape(-1)[: misc.size]


def doc_ids(lengths, positions, all_tokens):
    doc_ends = jnp.cumsum(lengths)
    doc_index = jnp.sum((doc_ends[None, :] <= positions[:, None]).astype(jnp.int32), axis=1)
    doc_index = jnp.where(positions < 0, -1, doc_index)
    return jnp.where(positions >= all_tokens, FAR_ID, doc_index)


def shifted(block, axis, distance):
    count = lax.axis_size(axis)
    route = [(i, i + distance) for i in range(count) if 0 <= i + distance < count]
    return lax.ppermute(block, axis, route)


def swapped(block, axis):
    return lax.ppermute(block, axis, [(0, 1), (1, 0)])


def tp_sum(partial_low):
    return partial_low.astype(F32) + swapped(partial_low, "tp").astype(F32)


def after(value, *others):
    return lax.optimization_barrier((value, *others))[0]


def layer_norm(vectors, gain_row, shift_row):
    center = vectors - jnp.mean(vectors, axis=-1, keepdims=True)
    spread = jnp.mean(center * center, axis=-1, keepdims=True)
    return center * lax.rsqrt(spread + EPS_LAYER) * gain_row + shift_row


def body(
    inputs,
    cotangent,
    query_weight,
    key_weight,
    value_weight,
    out_weight,
    up_weight,
    down_weight,
    conv_taps,
    attn_gain,
    attn_shift,
    ffn_gain,
    ffn_shift,
    hyperplanes,
    lengths,
):
    tokens, depth = inputs.shape
    head_dim = hyperplanes.shape[2]
    width = query_weight.shape[1]
    half = tokens // 2
    my_index = lax.axis_index("seq")
    my_side = lax.axis_index("tp")
    all_tokens = tokens * lax.axis_size("seq")
    far_reach = (MOST + tokens - 2) // tokens
    close = far_reach // 2
    near = list(range(close, 0, -1)) + list(range(-1, -close - 1, -1))
    far = list(range(far_reach, close, -1)) + list(range(-close - 1, -far_reach - 1, -1))
    groups = [near, far]
    first_token = my_index * tokens

    mine_rows = lax.dynamic_slice_in_dim(inputs, my_side * half, half, 0)
    near_mine = [shifted(mine_rows, "seq", d) for d in near]

    def ids_at(positions):
        return doc_ids(lengths, positions, all_tokens)

    def span(start, count, step=1):
        return start + step * jnp.arange(count, dtype=jnp.int32)

    ids_ext = ids_at(span(first_token - 2 * STRIP, tokens + 4 * STRIP))
    ids_col = jnp.broadcast_to(ids_ext[:, None], (ids_ext.shape[0], PAIR))
    own_ids = ids_at(span(first_token, tokens))
    q_count = tokens // Q_TILE_BACK
    k_starts = [
        jnp.concatenate([span(first_token - d * tokens, tokens // CHUNK, CHUNK) for d in part])
        for part in groups + [[0]]
    ]
    k_counts = [starts.shape[0] for starts in k_starts]
    q_starts = span(first_token, q_count, Q_TILE_BACK)
    ends = ids_at(
        jnp.concatenate(
            [q_starts, q_starts + Q_TILE_BACK - 1]
            + [starts + extra for starts in k_starts for extra in (0, CHUNK - 1)]
        )
    )
    q_low, q_high = ends[:q_count], ends[q_count : 2 * q_count]
    ratio = Q_TILE // Q_TILE_BACK
    q_ends = (q_low[::ratio], q_high[ratio - 1 :: ratio])
    k_ends, chunk_tables, fill_tables, needs, group_ids = [], [], [], [], []
    spot, window = 2 * q_count, k_counts[0] + k_counts[1]
    for index, (starts, count) in enumerate(zip(k_starts, k_counts)):
        low, high = ends[spot : spot + count], ends[spot + count : spot + 2 * count]
        spot += 2 * count
        k_ends.append((low, high))
        need = ((high >= q_low[0]) & (low <= q_high[-1])).astype(jnp.int32).reshape(-1, 2)
        places = span(0, count).reshape(-1, 2)
        ordered = []
        for pair in (places, need):
            mine = jnp.where(my_side == 0, pair[:, 0], pair[:, 1])
            other = jnp.where(my_side == 0, pair[:, 1], pair[:, 0])
            ordered += [mine, other]
        place = jnp.concatenate(ordered[:2])
        wanted = jnp.concatenate(ordered[2:])
        chunk_tables.append(jnp.concatenate([place, wanted, place * wanted]))
        base = k_counts[0] if index == 1 else 0
        fill_tables.append(
            jnp.concatenate([jnp.where(wanted > 0, place + base, window), wanted])
        )
        needs.append(need)
        group_ids.append(
            ids_at((starts[:, None] + jnp.arange(CHUNK, dtype=jnp.int32)).reshape(-1))
        )
    window_ends = [jnp.concatenate(both) for both in zip(k_ends[0], k_ends[1])]
    window_ids = jnp.concatenate(group_ids[:2])
    split = k_counts[0]
    window_table = tile_table(*q_ends, *window_ends, 0, window)
    own_table = tile_table(*q_ends, *k_ends[2], 0, k_counts[2])
    near_table = tile_table(q_low, q_high, *window_ends, 0, split)
    far_table = tile_table(q_low, q_high, *window_ends, split, window)
    own_back_table = tile_table(q_low, q_high, *k_ends[2], 0, k_counts[2])
    near_at, far_at, own_at = range(3)

    weight_qkv = jnp.concatenate([query_weight, key_weight, value_weight], axis=1)
    weight_kv = weight_qkv[:, width:]
    plain_table = jnp.array(list(range(tokens // CHUNK)) + [1] * (tokens // CHUNK), jnp.int32)
    query_unit, query_scale, key_unit, key_scale, values = project(
        plain_table, [inputs], weight_qkv, 2, head_dim
    )
    gathered, own_weights = attend(
        own_table, query_unit, key_unit, values, own_ids, own_ids, head_dim
    )

    def other_half(mine):
        return jnp.concatenate([swapped(term, "tp") for term in mine], axis=0)

    *near_mine, late_rows = after((*near_mine, mine_rows), gathered)
    far_mine = [shifted(late_rows if i else mine_rows, "seq", d) for i, d in enumerate(far)]
    near_x = [*near_mine, other_half(near_mine)]
    near_kv = project(fill_tables[near_at], near_x, weight_kv, 1, head_dim, window)
    far_mine = after(tuple(far_mine), *near_kv)
    far_x = [*far_mine, other_half(far_mine)]
    key_win, scale_win, value_win = project(
        fill_tables[far_at], far_x, weight_kv, 1, head_dim, window, near_kv
    )
    group_x = [near_x, far_x]
    gathered, far_weights = attend(
        window_table,
        query_unit,
        key_win,
        value_win,
        own_ids,
        window_ids,
        head_dim,
        seed=gathered,
    )
    edge = close * tokens
    sides = needs[near_at].reshape(-1)[edge // CHUNK - 1 : edge // CHUNK + 1]
    values_rim = jnp.where(
        jnp.repeat(sides, RIM)[:, None] > 0, value_win[edge - RIM : edge + RIM], 0
    )
    mixed = mix(gathered, values, values_rim, ids_ext, ids_col, conv_taps, head_dim)

    attn_out = tp_sum(nn(mixed, out_weight).astype(BF16))
    first_norm, first_back = jax.vjp(
        layer_norm, inputs.astype(F32) + attn_out, attn_gain, attn_shift
    )
    first_low = first_norm.astype(BF16)
    partial_out, active, slope = feed(first_low, up_weight, down_weight)
    ffn_out = tp_sum(partial_out)
    result, second_back = jax.vjp(layer_norm, first_norm + ffn_out, ffn_gain, ffn_shift)
    output = result.astype(BF16)
    grad_second, grad_ffn_gain, grad_ffn_shift = second_back(cotangent.astype(F32))
    grad_ffn = grad_second.astype(BF16)
    grad_hidden = (nt(grad_ffn, down_weight) * slope.astype(F32)).astype(BF16)
    grad_first = grad_second + tp_sum(nt(grad_hidden, up_weight).astype(BF16))
    grad_residual, grad_attn_gain, grad_attn_shift = first_back(grad_first)
    grad_attn = grad_residual.astype(BF16)
    grad_mixed = nt(grad_attn, out_weight).astype(BF16)

    grad_down = tn(active, grad_ffn).astype(BF16)
    grad_up = tn(first_low, grad_hidden).astype(BF16)
    grad_out = tn(mixed, grad_attn).astype(BF16)
    down_out = jnp.concatenate([grad_down, grad_out], axis=0)
    grad_up_low, down_out_low = grad_up, down_out
    grad_up, down_out = lax.psum((grad_up_low, down_out_low), "seq")

    grad_rows = back_norm(gathered, after(grad_mixed, grad_up_low, down_out_low), head_dim)

    def back_scores(table, first, grad_rows, seed):
        return back_attend(
            table,
            split,
            first,
            window,
            query_unit,
            grad_rows,
            key_win,
            value_win,
            far_weights,
            head_dim,
            seed=seed,
        )

    def back_inputs(index, dk, dv, **rims):
        return back_project(
            chunk_tables[index],
            group_x[index],
            weight_kv,
            [(key_win, scale_win, dk)],
            0,
            [dv],
            head_dim,
            first=split * index,
            **rims,
        )

    def send_home(distances, dx_mine, came):
        both = [
            (
                dx_mine[i * half : (i + 1) * half].astype(F32)
                + came[i * half : (i + 1) * half].astype(F32)
            ).astype(BF16)
            for i in range(len(distances))
        ]
        return both, [shifted(term, "seq", -d) for term, d in zip(both, distances)]

    dk, dv, turned = back_scores(far_table, split, grad_rows, None)
    far_dx, dx_other, far_dw = back_inputs(far_at, dk, dv)
    far_came = swapped(dx_other, "tp")
    grad_conv_values, grad_taps = back_conv(
        values, values_rim, after(grad_mixed, far_dx), ids_ext, ids_col, conv_taps, head_dim
    )
    rim = jnp.concatenate([grad_conv_values[:STRIP], grad_conv_values[-STRIP:]], axis=0)
    dk, dv, turned = back_scores(
        near_table, 0, after(grad_rows, grad_conv_values), turned
    )
    near_dx, dx_other, near_dw = back_inputs(
        near_at, dk, dv, rims=close * (tokens // CHUNK) - 1, rim=rim
    )
    near_came = swapped(dx_other, "tp")
    far_came, grad_up, down_out = after((far_came, grad_up, down_out), near_dx)
    terms, far_homes = send_home(far, far_dx, far_came)
    dk, dv, turned = back_attend(
        own_back_table,
        k_counts[own_at],
        0,
        k_counts[own_at],
        query_unit,
        after(grad_rows, *terms),
        key_unit,
        values,
        own_weights,
        head_dim,
        seed=turned,
        cost=pl.CostEstimate(flops=1 << 35, bytes_accessed=1 << 20, transcendentals=0),
    )
    terms, near_homes = send_home(near, near_dx, after(near_came, dk))
    dk, key_late, far_homes = after((dk, key_unit, far_homes), *terms)
    own_mine = mine_rows
    own_other = lax.dynamic_slice_in_dim(inputs, (1 - my_side) * half, half, 0)
    dx_mine, dx_other, dw = back_project(
        chunk_tables[own_at],
        [own_mine, own_other],
        weight_qkv,
        [(query_unit, query_scale, turned), (key_unit, key_scale, dk)],
        1,
        [dv, grad_conv_values[STRIP:-STRIP]],
        head_dim,
    )

    occ_local = occupancy(after(key_late, dw), hyperplanes, 2.0**BITS / all_tokens)
    near_homes = after(tuple(near_homes), occ_local)
    qkv = jnp.concatenate([dw[:, :width], dw[:, width:] + near_dw + far_dw], axis=1).astype(BF16)
    misc = [
        occ_local,
        grad_taps,
        grad_attn_gain,
        grad_attn_shift,
        grad_ffn_gain,
        grad_ffn_shift,
    ]
    packed = jnp.concatenate([term.reshape(-1) for term in misc])
    qkv, packed = sum_over_seq(qkv, packed, 3)

    came = swapped(dx_other, "tp")
    total = (
        lax.dynamic_slice_in_dim(grad_residual, my_side * half, half, 0)
        + dx_mine.astype(F32)
        + came.astype(F32)
    )
    for home in (*far_homes, *near_homes):
        total = total + home.astype(F32)
    other_total = swapped(total, "tp")
    lower = jnp.where(my_side == 0, total, other_total)
    upper = jnp.where(my_side == 0, other_total, total)
    grad_inputs = jnp.concatenate([lower, upper], axis=0)

    unpacked, at = [], 0
    for term in misc:
        unpacked.append(packed[at : at + term.size].reshape(term.shape))
        at += term.size
    down_out = down_out.astype(F32)
    ff = down_weight.shape[0]
    return (
        output,
        grad_inputs,
        *qkv,
        down_out[ff:],
        grad_up.astype(F32),
        down_out[:ff],
        *unpacked[1:],
        unpacked[0],
    )


def solution(mesh):
    return jax.shard_map(
        body,
        mesh=mesh,
        in_specs=(
            P("seq", None),
            P("seq", None),
            P(None, "tp"),
            P(None, "tp"),
            P(None, "tp"),
            P("tp", None),
            P(None, "tp"),
            P("tp", None),
            P("tp", None),
            P(),
            P(),
            P(),
            P(),
            P(),
            P(),
        ),
        out_specs=(
            P("seq", None),
            P("seq", None),
            P(None, "tp"),
            P(None, "tp"),
            P(None, "tp"),
            P("tp", None),
            P(None, "tp"),
            P("tp", None),
            P("tp", None),
            P(),
            P(),
            P(),
            P(),
            P("tp", None, None),
        ),
        check_vma=False,
    )
```

```python
from functools import partial
import math

import jax
import jax.numpy as jnp
from jax import lax
from jax.experimental import pallas as pl
from jax.experimental.pallas import tpu as pltpu
from jax.sharding import PartitionSpec as P

TAU = 8
BITS = 8
CONV = 33
MOST = 4096
RIM = (CONV - 1) // 2

EPS_UNIT = 1e-06
EPS_LAYER = 1e-05
SHARP = 4.0
CLIP_EDGE = 0.999

CHUNK = 512
Q_TILE = 512
Q_TILE_BACK = 256
PAIR = 128
STRIP = 128
FAR_ID = 1 << 20

LIGHT = pl.CostEstimate(flops=1 << 20, bytes_accessed=1 << 16, transcendentals=0)

F32 = jnp.float32
BF16 = jnp.bfloat16

ARC = (
    0.49999961256980896,
    -0.06828052550554276,
    0.027964841574430466,
    -0.014291195198893547,
    0.006136968266218901,
    -0.001371906721033156,
)


def params(**kwargs):
    return pltpu.CompilerParams(vmem_limit_bytes=56 << 20, **kwargs)


def nn(left, right):
    return lax.dot_general(left, right, (((1,), (0,)), ((), ())), preferred_element_type=F32)


def nt(left, right):
    return lax.dot_general(left, right, (((1,), (1,)), ((), ())), preferred_element_type=F32)


def tn(left, right):
    return lax.dot_general(left, right, (((0,), (0,)), ((), ())), preferred_element_type=F32)


def head_masks(head_dim):
    lanes = lax.broadcasted_iota(jnp.int32, (1, PAIR), 1)
    first = (lanes < head_dim).astype(F32)
    return first.astype(BF16), (1.0 - first).astype(BF16)


def head_sum(rows, head_dim):
    here = lax.broadcasted_iota(jnp.int32, (PAIR, PAIR), 0) // head_dim
    there = lax.broadcasted_iota(jnp.int32, (PAIR, PAIR), 1) // head_dim
    ones = (here == there).astype(F32).astype(BF16)
    sums = []
    for start in range(0, rows.shape[1], PAIR):
        part = rows[:, start : start + PAIR]
        high = part.astype(BF16)
        low = (part - high.astype(F32)).astype(BF16)
        sums.append(nn(high, ones) + nn(low, ones))
    return jnp.concatenate(sums, axis=1)


def pick_half(mine_refs, other_ref, kept):
    step = pl.program_id(0)
    for index, ref in enumerate(mine_refs):

        @pl.when(step == index)
        def _():
            kept[...] = ref[...]

    @pl.when(step >= len(mine_refs))
    def _():
        kept[...] = other_ref[...]


def other_spec(count, shape):
    return pl.BlockSpec(shape, lambda i, t: (jnp.maximum(i - count, 0), 0))


def half_specs(count, shape):
    return [pl.BlockSpec(shape, lambda i, t: (0, 0))] * count + [other_spec(count, shape)]


def project_kernel(units, count, head_dim, table, *refs):
    if count:
        mine_refs, other_ref, w_ref = refs[:count], refs[count], refs[count + 1]
        out_refs, kept = refs[count + 2 : -1], refs[-1]
        pick_half(mine_refs, other_ref, kept)
    else:
        kept, w_ref = refs[:2]
        out_refs = refs[2:]
    width = out_refs[-1].shape[1]
    needed = table[pl.num_programs(0) + pl.program_id(0)] > 0

    @pl.when(needed)
    def _():
        whole = nn(kept[...], w_ref[...])
        for index in range(units):
            part = whole[:, index * width : (index + 1) * width]
            scale = lax.rsqrt(head_sum(part * part, head_dim) * (1.0 / head_dim) + EPS_UNIT)
            scale = scale * (1.0 / math.sqrt(head_dim))
            out_refs[2 * index][...] = (part * scale).astype(BF16)
            out_refs[2 * index + 1][...] = scale
        out_refs[-1][...] = whole[:, units * width :].astype(BF16)


def project(table, halves, weight, units, head_dim, chunks=None):
    depth = halves[0].shape[1]
    rows = sum(h.shape[0] for h in halves)
    count = len(halves) - 1
    width = weight.shape[1] // (units + 1)
    row_spec = pl.BlockSpec((CHUNK, width), lambda i, t: (t[i], 0))
    held = (chunks + 1) * CHUNK if count else rows
    if count:
        x_specs = half_specs(count, (CHUNK, depth))
    else:
        x_specs = [pl.BlockSpec((CHUNK, depth), lambda i, t: (i, 0))]
    unit_shapes = [
        jax.ShapeDtypeStruct((held, width), BF16),
        jax.ShapeDtypeStruct((held, width), F32),
    ]
    return pl.pallas_call(
        partial(project_kernel, units, count, head_dim),
        grid_spec=pltpu.PrefetchScalarGridSpec(
            num_scalar_prefetch=1,
            grid=(rows // CHUNK,),
            in_specs=x_specs + [pl.BlockSpec(weight.shape, lambda i, t: (0, 0))],
            out_specs=[row_spec] * (2 * units + 1),
            scratch_shapes=[pltpu.VMEM((CHUNK, depth), BF16)] if count else [],
        ),
        out_shape=unit_shapes * units + [jax.ShapeDtypeStruct((held, width), BF16)],
        compiler_params=params(),
        cost_estimate=pl.CostEstimate(
            flops=4 * rows * depth * weight.shape[1], bytes_accessed=rows * depth, transcendentals=0
        ),
        name="project",
    )(table, *halves, weight)


def collide(scores):
    size = jnp.minimum(jnp.abs(scores), CLIP_EDGE)
    rest = 1.0 - size
    poly = ARC[5]
    for factor in ARC[4::-1]:
        poly = poly * size + factor
    angle = (rest * lax.rsqrt(rest)) * poly
    return jnp.where(scores < 0.0, angle, 1.0 - angle)


def tile_facts(table, tiles_q, tiles_k, qi, kt):
    q_low, q_high = table[qi], table[tiles_q + qi]
    k_low, k_high = table[2 * tiles_q + kt], table[2 * tiles_q + tiles_k + kt]
    needed = (k_high >= q_low) & (k_low <= q_high)
    whole = (q_low == q_high) & (k_low == k_high)
    return needed, whole


def id_column(row, lanes):
    column = jnp.broadcast_to(row, (PAIR, row.shape[1])).T
    return jnp.concatenate([column] * (lanes // PAIR), axis=1)


def attend_kernel(
    head_dim, tiles_k, seeded, table, q_ref, qrow_ref, krow_ref, k_ref, v_ref, *rest
):
    out_ref, w_ref = rest[-2:]
    tiles_q = q_ref.shape[0] // Q_TILE
    step, steps = pl.program_id(1), pl.num_programs(1)
    order = 2 * (tiles_q + tiles_k)
    masks = head_masks(head_dim)

    @pl.when(step == 0)
    def _():
        if seeded:
            out_ref[...] = rest[0][...]
        else:
            out_ref[...] = jnp.zeros_like(out_ref)

    @pl.when(step < table[order + steps])
    def _():
        kt = table[order + step]

        def q_loop(qi, carry):
            rows = pl.ds(pl.multiple_of(qi * Q_TILE, Q_TILE), Q_TILE)
            needed, whole = tile_facts(table, tiles_q, tiles_k, qi, kt)

            def part(same):
                q, k = q_ref[rows, :], k_ref[...]
                v_turned = v_ref[...].T
                for index, mask in enumerate(masks):
                    chance = collide(nt(k, q * mask))
                    chance = chance * chance
                    chance = chance * chance
                    chance = chance * chance
                    if same is not None:
                        chance = jnp.where(same, chance, 0.0)
                    weights = chance.astype(BF16)
                    w_ref[index, :, rows] = weights
                    half = slice(index * head_dim, (index + 1) * head_dim)
                    out_ref[half, rows] += nn(v_turned[half, :], weights)

            @pl.when(needed & whole)
            def _():
                part(None)

            @pl.when(needed & jnp.logical_not(whole))
            def _():
                part(id_column(krow_ref[pl.ds(kt, 1), :], Q_TILE) == qrow_ref[pl.ds(qi, 1), :])

            @pl.when(jnp.logical_not(needed))
            def _():
                w_ref[:, :, rows] = jnp.zeros((2, CHUNK, Q_TILE), BF16)

            return carry

        lax.fori_loop(0, tiles_q, q_loop, 0)


def attend(table, q, k, v, qrow, krow, head_dim, seed=None):
    tokens, width = q.shape
    tiles_k = krow.shape[0]
    order = 2 * (tokens // Q_TILE + tiles_k)
    k_spec = pl.BlockSpec((CHUNK, PAIR), lambda p, j, t: (t[order + j], p))
    turned_spec = pl.BlockSpec((PAIR, tokens), lambda p, j, t: (p, 0))
    operands = [q, qrow, krow, k, v]
    specs = [
        pl.BlockSpec((tokens, PAIR), lambda p, j, t: (0, p)),
        pl.BlockSpec(qrow.shape, lambda p, j, t: (0, 0)),
        pl.BlockSpec(krow.shape, lambda p, j, t: (0, 0)),
        k_spec,
        k_spec,
    ]
    if seed is not None:
        operands.append(seed)
        specs.append(turned_spec)
    return pl.pallas_call(
        partial(attend_kernel, head_dim, tiles_k, seed is not None),
        grid_spec=pltpu.PrefetchScalarGridSpec(
            num_scalar_prefetch=1,
            grid=(width // PAIR, tiles_k),
            in_specs=specs,
            out_specs=[
                turned_spec,
                pl.BlockSpec((2, CHUNK, tokens), lambda p, j, t: (p, t[order + j], 0)),
            ],
        ),
        out_shape=[
            jax.ShapeDtypeStruct((width, tokens), F32),
            jax.ShapeDtypeStruct((width // head_dim, tiles_k * CHUNK, tokens), BF16),
        ],
        compiler_params=params(),
        cost_estimate=pl.CostEstimate(
            flops=32 * tokens * tiles_k * CHUNK * width,
            bytes_accessed=tokens * width * 4,
            transcendentals=0,
        ),
        name="attend",
    )(table, *operands)


def back_attend_kernel(
    head_dim, tiles_k, seeded, table, q_ref, g_ref, k_ref, v_ref, w_ref, *rest
):
    dk_ref, dv_ref, dq_ref, acc_k, acc_v = rest[-5:]
    tiles_q = q_ref.shape[0] // Q_TILE_BACK
    step, steps = pl.program_id(1), pl.num_programs(1)
    order = 2 * (tiles_q + tiles_k)
    masks = head_masks(head_dim)

    @pl.when(step == 0)
    def _():
        if seeded:
            dq_ref[...] = rest[0][...]
        else:
            dq_ref[...] = jnp.zeros_like(dq_ref)

    @pl.when(step < table[order + steps])
    def _():
        kt = table[order + step]
        acc_k[...] = jnp.zeros_like(acc_k)
        acc_v[...] = jnp.zeros_like(acc_v)

        def q_loop(qi, carry):
            needed, _ = tile_facts(table, tiles_q, tiles_k, qi, kt)

            @pl.when(needed)
            def _():
                rows = pl.ds(pl.multiple_of(qi * Q_TILE_BACK, Q_TILE_BACK), Q_TILE_BACK)
                q, g, k, v = q_ref[rows, :], g_ref[rows, :], k_ref[...], v_ref[...]
                k_turned = k.T
                sum_k, sum_v = None, None
                for index, mask in enumerate(masks):
                    q_half, g_half = q * mask, g * mask
                    scores = nt(k, q_half)
                    weights = w_ref[index, :, rows]
                    power = jnp.exp(((TAU - 1) / TAU) * jnp.log(weights.astype(F32)))
                    square = scores * scores
                    slope = nt(v, g_half) * (power * lax.rsqrt(1.0 - square))
                    slope = jnp.where(square <= CLIP_EDGE * CLIP_EDGE, slope, 0.0).astype(BF16)
                    term_v = nn(weights, g_half)
                    term_k = nn(slope, q_half)
                    sum_v = term_v if sum_v is None else sum_v + term_v
                    sum_k = term_k if sum_k is None else sum_k + term_k
                    half = slice(index * head_dim, (index + 1) * head_dim)
                    dq_ref[half, rows] += nn(k_turned[half, :], slope)
                acc_v[...] += sum_v
                acc_k[...] += sum_k

            return carry

        lax.fori_loop(0, tiles_q, q_loop, 0)
        dk_ref[...] = acc_k[...].astype(BF16)
        dv_ref[...] = acc_v[...].astype(BF16)


def back_attend(table, tiles_k, q, g, k, v, weights, head_dim, seed=None, cost=LIGHT):
    tokens, width = q.shape
    order = 2 * (tokens // Q_TILE_BACK + tiles_k)
    q_spec = pl.BlockSpec((tokens, PAIR), lambda p, j, t: (0, p))
    k_spec = pl.BlockSpec((CHUNK, PAIR), lambda p, j, t: (t[order + j], p))
    dq_spec = pl.BlockSpec((PAIR, tokens), lambda p, j, t: (p, 0))
    specs = [
        q_spec,
        q_spec,
        k_spec,
        k_spec,
        pl.BlockSpec((2, CHUNK, tokens), lambda p, j, t: (p, t[order + j], 0)),
    ]
    operands = [q, g, k, v, weights]
    if seed is not None:
        operands.append(seed)
        specs.append(dq_spec)
    return pl.pallas_call(
        partial(back_attend_kernel, head_dim, tiles_k, seed is not None),
        grid_spec=pltpu.PrefetchScalarGridSpec(
            num_scalar_prefetch=1,
            grid=(width // PAIR, tiles_k),
            in_specs=specs,
            out_specs=[k_spec, k_spec, dq_spec],
            scratch_shapes=[pltpu.VMEM((CHUNK, PAIR), F32), pltpu.VMEM((CHUNK, PAIR), F32)],
        ),
        out_shape=[
            jax.ShapeDtypeStruct((tiles_k * CHUNK, width), BF16),
            jax.ShapeDtypeStruct((tiles_k * CHUNK, width), BF16),
            jax.ShapeDtypeStruct((width, tokens), F32),
        ],
        compiler_params=params(),
        cost_estimate=cost,
        name="back_attend",
    )(table, *operands)


def back_project_kernel(units, turned, terms, rims, count, head_dim, table, *refs):
    mine_refs, other_ref, w_ref = refs[:count], refs[count], refs[count + 1]
    dx_mine, dx_other, dw_ref, kept, sum_ref = refs[-5:]
    refs = refs[count + 2 : -5]
    step = pl.program_id(0)
    place, needed = table[step], table[pl.num_programs(0) + step] > 0

    @pl.when(step == 0)
    def _():
        dw_ref[...] = jnp.zeros_like(dw_ref)

    def store(value):
        @pl.when(step < count)
        def _():
            dx_mine[...] = value

        @pl.when(step >= count)
        def _():
            dx_other[...] = value

    @pl.when(needed)
    def _():
        pick_half(mine_refs, other_ref, kept)
        grads = []
        for index in range(units):
            unit_ref, scale_ref, grad_ref = refs[3 * index : 3 * index + 3]
            grad = grad_ref[...].astype(F32)
            if index < turned:
                grad = grad.T
            unit = unit_ref[...].astype(F32)
            inner = head_sum(grad * unit, head_dim)
            grads.append(
                ((TAU / math.pi) * scale_ref[...] * (grad - unit * inner)).astype(BF16)
            )
        value_refs = refs[3 * units : 3 * units + terms]
        value = value_refs[0][...].astype(F32)
        for extra in value_refs[1:]:
            value = value + extra[...].astype(F32)
        if rims is not None:
            rim_ref = refs[-1]
            sum_ref[...] = value

            @pl.when(place == rims)
            def _():
                sum_ref[CHUNK - STRIP :, :] += rim_ref[:STRIP, :]

            @pl.when(place == rims + 1)
            def _():
                sum_ref[:STRIP, :] += rim_ref[STRIP:, :]

            value = sum_ref[...]
        grads.append(value.astype(BF16))
        joined = jnp.concatenate(grads, axis=1)
        store(nt(joined, w_ref[...]).astype(BF16))
        dw_ref[...] += tn(kept[...], joined)

    @pl.when(jnp.logical_not(needed))
    def _():
        store(jnp.zeros(dx_mine.shape, BF16))


def back_project(table, halves, weight, parts, turned, values, head_dim, rims=None, rim=None):
    depth = halves[0].shape[1]
    count = len(halves) - 1
    width = values[0].shape[1]
    row_spec = pl.BlockSpec((CHUNK, width), lambda i, t: (t[4 * count + i], 0))
    weight_spec = pl.BlockSpec(weight.shape, lambda i, t: (0, 0))
    wide_specs = [
        pl.BlockSpec((CHUNK, depth), lambda i, t: (jnp.minimum(i, count - 1), 0)),
        other_spec(count, (CHUNK, depth)),
    ]
    specs = half_specs(count, (CHUNK, depth)) + [weight_spec]
    operands = [*halves, weight]
    for index, (unit, scale, grad) in enumerate(parts):
        operands += [unit, scale, grad]
        specs += [row_spec, row_spec]
        specs.append(
            pl.BlockSpec((width, CHUNK), lambda i, t: (0, t[4 * count + i]))
            if index < turned
            else row_spec
        )
    operands += values
    specs += [row_spec] * len(values)
    if rim is not None:
        operands.append(rim)
        specs.append(pl.BlockSpec(rim.shape, lambda i, t: (0, 0)))
    return pl.pallas_call(
        partial(back_project_kernel, len(parts), turned, len(values), rims, count, head_dim),
        grid_spec=pltpu.PrefetchScalarGridSpec(
            num_scalar_prefetch=1,
            grid=(2 * count,),
            in_specs=specs,
            out_specs=wide_specs + [weight_spec],
            scratch_shapes=[pltpu.VMEM((CHUNK, depth), BF16), pltpu.VMEM((CHUNK, width), F32)],
        ),
        out_shape=[
            jax.ShapeDtypeStruct((count * CHUNK, depth), BF16),
            jax.ShapeDtypeStruct((count * CHUNK, depth), BF16),
            jax.ShapeDtypeStruct(weight.shape, F32),
        ],
        compiler_params=params(),
        cost_estimate=LIGHT,
        name="back_project",
    )(table, *operands)


def lane_taps(conv_taps, mirrored):
    front = STRIP // 2 - RIM
    heads = conv_taps.shape[0]
    taps = conv_taps[:, ::-1] if mirrored else conv_taps
    return jnp.pad(taps, ((0, -heads % 8), (front, 2 * STRIP - front - CONV)))


def fill_bands(taps_ref, bands, heads):
    for head in range(heads):
        row = jnp.broadcast_to(taps_ref[head : head + 1, :], (STRIP, 2 * STRIP))
        bands[head] = pltpu.roll(row, 0, 1, stride=1, stride_axis=0)


def band_product(band, same, window):
    band = jnp.where(same, band, 0.0)
    high = band.astype(BF16)
    low = (band - high.astype(F32)).astype(BF16)
    return nn(high, window) + nn(low, window)


def fill_extended(kept, edge, centre_ref, rim_ref):
    rows = centre_ref.shape[0]
    kept[...] = jnp.zeros_like(kept)
    kept[edge : edge + rows, :] = centre_ref[...]
    if rim_ref is not None:
        kept[edge - RIM : edge, :] = rim_ref[:RIM, :]
        kept[edge + rows : edge + rows + RIM, :] = rim_ref[RIM:, :]


def mix_kernel(head_dim, g_ref, col_ref, v_ref, rim_ref, row_ref, taps_ref, out_ref, bands, kept):
    heads = g_ref.shape[0] // head_dim
    step = pl.program_id(0)

    @pl.when(step == 0)
    def _():
        fill_bands(taps_ref, bands, heads)
        fill_extended(kept, STRIP, v_ref, rim_ref)

    masks = head_masks(head_dim)
    window = kept[pl.ds(pl.multiple_of(step * STRIP + STRIP // 2, STRIP // 2), 2 * STRIP), :]
    ids = col_ref[...]
    same = jnp.concatenate([ids, ids], axis=1) == row_ref[pl.ds(step, 1), :]
    pieces = []
    for pair in range(heads // 2):
        values = window[:, pair * PAIR : (pair + 1) * PAIR]
        total = None
        for index, mask in enumerate(masks):
            term = band_product(bands[2 * pair + index], same, values * mask)
            total = term if total is None else total + term
        pieces.append(total)
    gathered = g_ref[...].T
    scale = lax.rsqrt(head_sum(gathered * gathered, head_dim) * (1.0 / head_dim) + EPS_UNIT)
    out_ref[...] = (gathered * scale + jnp.concatenate(pieces, axis=1)).astype(BF16)


def mix(gathered, values, rim, row, col, conv_taps, head_dim):
    width, tokens = gathered.shape
    heads = width // head_dim
    strips = tokens // STRIP
    taps = lane_taps(conv_taps, False)
    row_spec = pl.BlockSpec((STRIP, width), lambda i: (i, 0))
    whole = [values, rim, row, taps]
    return pl.pallas_call(
        partial(mix_kernel, head_dim),
        grid=(strips,),
        in_specs=[
            pl.BlockSpec((width, STRIP), lambda i: (0, i)),
            pl.BlockSpec((STRIP, PAIR), lambda i: (i + 2, 0)),
        ]
        + [pl.BlockSpec(a.shape, lambda i: (0, 0)) for a in whole],
        out_specs=row_spec,
        out_shape=jax.ShapeDtypeStruct((tokens, width), BF16),
        scratch_shapes=[
            pltpu.VMEM((heads, STRIP, 2 * STRIP), F32),
            pltpu.VMEM((tokens + 2 * STRIP, width), BF16),
        ],
        compiler_params=params(),
        cost_estimate=LIGHT,
        name="mix",
    )(gathered, col, *whole)


def back_norm_kernel(head_dim, g_ref, m_ref, out_ref):
    gathered, grad = g_ref[...].T, m_ref[...].astype(F32)
    scale = lax.rsqrt(head_sum(gathered * gathered, head_dim) * (1.0 / head_dim) + EPS_UNIT)
    mean = head_sum(grad * gathered, head_dim) * (1.0 / head_dim)
    out_ref[...] = (scale * (grad - (scale * scale) * gathered * mean)).astype(BF16)


def back_norm(gathered, grad_mixed, head_dim):
    width, tokens = gathered.shape
    row_spec = pl.BlockSpec((CHUNK, width), lambda i: (i, 0))
    return pl.pallas_call(
        partial(back_norm_kernel, head_dim),
        grid=(tokens // CHUNK,),
        in_specs=[pl.BlockSpec((width, CHUNK), lambda i: (0, i)), row_spec],
        out_specs=row_spec,
        out_shape=jax.ShapeDtypeStruct((tokens, width), BF16),
        compiler_params=params(),
        cost_estimate=LIGHT,
        name="back_norm",
    )(gathered, grad_mixed)


def back_conv_kernel(
    head_dim, col_ref, v_ref, rim_ref, m_ref, row_ref, taps_ref, dv_ref, tap_ref, bands, sums, kept_v, kept_m
):
    heads = dv_ref.shape[1] // head_dim
    step, steps = pl.program_id(0), pl.num_programs(0)

    @pl.when(step == 0)
    def _():
        fill_bands(taps_ref, bands, heads)
        fill_extended(kept_v, 2 * STRIP, v_ref, rim_ref)
        fill_extended(kept_m, 2 * STRIP, m_ref, None)
        sums[...] = jnp.zeros_like(sums)

    masks = head_masks(head_dim)
    around = pl.ds(pl.multiple_of(step * STRIP + STRIP // 2, STRIP // 2), 2 * STRIP)
    centre = pl.ds(pl.multiple_of(step * STRIP + STRIP, STRIP), STRIP)
    ids = col_ref[...]
    same = jnp.concatenate([ids, ids], axis=1) == row_ref[pl.ds(step, 1), :]
    pieces = []
    for pair in range(heads // 2):
        cols = slice(pair * PAIR, (pair + 1) * PAIR)
        grads, values, here = kept_m[around, cols], kept_v[around, cols], kept_m[centre, cols]
        total = None
        for index, mask in enumerate(masks):
            head = 2 * pair + index
            term = band_product(bands[head], same, grads * mask)
            total = term if total is None else total + term
            sums[head] += jnp.where(same, nt(here * mask, values), 0.0)
        pieces.append(total)
    dv_ref[...] = jnp.concatenate(pieces, axis=1)

    @pl.when(step == steps - 1)
    def _():
        tap_ref[...] = jnp.zeros_like(tap_ref)
        places = [lax.broadcasted_iota(jnp.int32, (STRIP, STRIP), d) for d in (0, 1)]
        flip = (places[0] + places[1] == STRIP - 1).astype(F32).astype(BF16)
        for head in range(heads):
            total = sums[head]
            high = total.astype(BF16)
            low = (total - high.astype(F32)).astype(BF16)
            turned = pltpu.roll(
                nn(flip, high) + nn(flip, low), STRIP + 1, 1, stride=1, stride_axis=0
            )
            tap_ref[head : head + 1, :] = jnp.sum(turned, axis=0, keepdims=True)


def back_conv(values, rim, grad_mixed, row, col, conv_taps, head_dim):
    tokens, width = values.shape
    heads = width // head_dim
    strips = tokens // STRIP + 2
    taps = lane_taps(conv_taps, True)
    front = STRIP // 2 - RIM
    whole = [values, rim, grad_mixed, row, taps]
    grad_values, tap_sums = pl.pallas_call(
        partial(back_conv_kernel, head_dim),
        grid=(strips,),
        in_specs=[pl.BlockSpec((STRIP, PAIR), lambda i: (i + 1, 0))]
        + [pl.BlockSpec(a.shape, lambda i: (0, 0)) for a in whole],
        out_specs=[
            pl.BlockSpec((STRIP, width), lambda i: (i, 0)),
            pl.BlockSpec(taps.shape, lambda i: (0, 0)),
        ],
        out_shape=[
            jax.ShapeDtypeStruct((strips * STRIP, width), F32),
            jax.ShapeDtypeStruct(taps.shape, F32),
        ],
        scratch_shapes=[
            pltpu.VMEM((heads, STRIP, 2 * STRIP), F32),
            pltpu.VMEM((heads, STRIP, 2 * STRIP), F32),
            pltpu.VMEM((tokens + 4 * STRIP, width), BF16),
            pltpu.VMEM((tokens + 4 * STRIP, width), BF16),
        ],
        compiler_params=params(),
        cost_estimate=LIGHT,
        name="back_conv",
    )(col, *whole)
    return grad_values, tap_sums[:heads, front : front + CONV]


def occupancy_kernel(hashes, k_ref, w_ref, out_ref, counts):
    combos = 4
    lanes = hashes * combos
    side = combos * combos
    wide = hashes * side

    @pl.when(pl.program_id(1) == 0)
    def _():
        counts[...] = jnp.zeros_like(counts)

    source = lax.broadcasted_iota(jnp.int32, (lanes, wide), 0)
    target = lax.broadcasted_iota(jnp.int32, (lanes, wide), 1)
    same_hash = (source // combos) == (target // side)
    picks = []
    for divisor in (1, combos):
        chosen = same_hash & ((source % combos) == ((target // divisor) % combos))
        picks.append(chosen.astype(F32).astype(BF16))
    keys = k_ref[...]
    for index in range(2):
        signed = nn(keys, w_ref[index])
        halves = []
        for half in range(2):
            product = None
            for pick in range(2):
                start = (half * 2 + pick) * 2 * lanes
                one = 1.0 + jnp.exp(-signed[:, start : start + lanes])
                two = 1.0 + jnp.exp(-signed[:, start + lanes : start + 2 * lanes])
                spread = nn((1.0 / (one * two)).astype(BF16), picks[pick])
                product = spread if product is None else product * spread
            halves.append(product.astype(BF16))
        low, high = halves
        for start in range(0, wide, PAIR):
            block = slice(start, start + PAIR)
            counts[index, block, :] += tn(high[:, block], low[:, block])

    @pl.when(pl.program_id(1) == pl.num_programs(1) - 1)
    def _():
        row = lax.broadcasted_iota(jnp.int32, (wide, PAIR), 0)
        lane = lax.broadcasted_iota(jnp.int32, (wide, PAIR), 1)
        diagonal = ((row % PAIR) // side) == (lane // side)
        fold = [lax.broadcasted_iota(jnp.int32, (PAIR, side * side), d) for d in (0, 1)]
        fold = ((fold[0] % side) == (fold[1] % side)).astype(F32).astype(BF16)
        spot = [lax.broadcasted_iota(jnp.int32, (wide, side * side), d) for d in (0, 1)]
        kept = (spot[0] % side) == (spot[1] // side)
        home = [lax.broadcasted_iota(jnp.int32, (hashes, wide), d) for d in (0, 1)]
        home = (home[0] == home[1] // side).astype(F32).astype(BF16)
        for index in range(2):
            left = jnp.where(diagonal, counts[index], 0.0)
            total = None
            for _ in range(3):
                piece = left.astype(BF16)
                left = left - piece.astype(F32)
                spread = jnp.where(kept, nn(piece, fold), 0.0).astype(BF16)
                term = nn(home, spread)
                total = term if total is None else total + term
            out_ref[index] = total


def occupancy(key_unit, hyperplanes, scale):
    tokens, width = key_unit.shape
    hashes, bits, head_dim = hyperplanes.shape
    pairs = width // PAIR
    wide = hashes * 16
    planes = SHARP * hyperplanes.astype(F32)
    columns = []
    for group in range(bits // 2):
        for bit in range(2):
            signs = 2.0 * ((jnp.arange(4) // (2**bit)) % 2).astype(F32) - 1.0
            plane = planes[:, 2 * group + bit, :]
            columns.append((plane.T[:, :, None] * signs).reshape(head_dim, hashes * 4))
    weight = jnp.concatenate(columns, axis=1).astype(BF16)
    blank = jnp.zeros_like(weight)
    weights = jnp.stack(
        [jnp.concatenate([weight, blank], axis=0), jnp.concatenate([blank, weight], axis=0)]
    )
    counts = pl.pallas_call(
        partial(occupancy_kernel, hashes),
        grid=(pairs, tokens // CHUNK),
        in_specs=[
            pl.BlockSpec((CHUNK, PAIR), lambda p, t: (t, p)),
            pl.BlockSpec(weights.shape, lambda p, t: (0, 0, 0)),
        ],
        out_specs=pl.BlockSpec((2, hashes, 256), lambda p, t: (p, 0, 0)),
        out_shape=jax.ShapeDtypeStruct((2 * pairs, hashes, 256), F32),
        scratch_shapes=[pltpu.VMEM((2, wide, PAIR), F32)],
        compiler_params=params(),
        cost_estimate=pl.CostEstimate(
            flops=tokens * width * 32000, bytes_accessed=tokens * width * 4, transcendentals=0
        ),
        name="occupancy",
    )(key_unit, weights)
    return counts * scale


BELL_STEP = 0.3275911
BELL = (0.254829592, -0.284496736, 1.421413741, -1.453152027, 1.061405429)


def feed_kernel(x_ref, up_ref, down_ref, out_ref, active_ref, slope_ref):
    hidden = nn(x_ref[...], up_ref[...])
    size = jnp.abs(hidden)
    step = 1.0 / (1.0 + (BELL_STEP / math.sqrt(2.0)) * size)
    poly = BELL[4]
    for factor in BELL[3::-1]:
        poly = poly * step + factor
    bell = jnp.exp(-0.5 * (hidden * hidden))
    tail = (0.5 * step) * (poly * bell)
    phi = jnp.where(hidden < 0.0, tail, 1.0 - tail)
    active = (hidden * phi).astype(BF16)
    active_ref[...] = active
    slope_ref[...] = (phi + hidden * (bell * (1.0 / math.sqrt(2.0 * math.pi)))).astype(BF16)
    out_ref[...] = nn(active, down_ref[...]).astype(BF16)


def feed(x, up_weight, down_weight):
    tokens, depth = x.shape
    hidden = up_weight.shape[1]
    rows = 256
    wide = pl.BlockSpec((rows, hidden), lambda i: (i, 0))
    narrow = pl.BlockSpec((rows, depth), lambda i: (i, 0))
    return pl.pallas_call(
        feed_kernel,
        grid=(tokens // rows,),
        in_specs=[
            narrow,
            pl.BlockSpec(up_weight.shape, lambda i: (0, 0)),
            pl.BlockSpec(down_weight.shape, lambda i: (0, 0)),
        ],
        out_specs=[narrow, wide, wide],
        out_shape=[
            jax.ShapeDtypeStruct((tokens, depth), BF16),
            jax.ShapeDtypeStruct((tokens, hidden), BF16),
            jax.ShapeDtypeStruct((tokens, hidden), BF16),
        ],
        compiler_params=params(),
        cost_estimate=LIGHT,
        name="feed",
    )(x, up_weight, down_weight)


PLANE = 4


def sum_plan(n, rows):
    unit = 16 * n
    units = -(-rows // unit)
    first = -(-2 * units // 3)
    streams = [(0, first * unit, True)]
    if units > first:
        streams.append((first * unit, (units - first) * unit, False))
    return units * unit, streams


def sum_kernel(n, streams, split, *refs):
    count = len(streams)
    table_ref, misc_ref = refs[:2]
    outs, misc_out = refs[2 : 2 + split], refs[2 + split]
    scratch = refs[3 + split :]
    send, recv = scratch[-2:]
    me = lax.axis_index("seq")
    groups = n // PLANE
    near_me, far_me = lax.rem(me, PLANE), me // PLANE

    def device(plane_first, one, two):
        return {"seq": two * PLANE + one if plane_first else one * PLANE + two}

    barrier = pltpu.get_barrier_semaphore()
    for step in range(1, PLANE):
        pl.semaphore_signal(
            barrier, 1, device_id=device(True, lax.rem(near_me + step, PLANE), far_me)
        )
    for step in range(1, groups):
        pl.semaphore_signal(
            barrier, 1, device_id=device(True, near_me, lax.rem(far_me + step, groups))
        )
    pl.semaphore_wait(barrier, PLANE - 1 + groups - 1)

    facts = []
    for index, (base, rows, plane_first) in enumerate(streams):
        sizes = (PLANE, groups) if plane_first else (groups, PLANE)
        mine = (near_me, far_me) if plane_first else (far_me, near_me)
        buffers = scratch[5 * index : 5 * index + 5]
        source = misc_ref if index == count - 1 else table_ref
        block, chunk = rows // sizes[0], rows // n
        facts.append((index, source, base, plane_first, sizes, mine, block, chunk, buffers))

    def at(start, number):
        return pl.ds(pl.multiple_of(start, 8), number)

    def start_all(phase):
        started = []
        for index, source, base, plane_first, sizes, mine, block, chunk, buffers in facts:
            got_one, part, got_two, merged, full = buffers
            side = 0 if phase in (0, 3) else 1
            for step in range(1, sizes[side]):
                to = lax.rem(mine[side] + step, sizes[side])
                if phase == 0:
                    src, dst = source.at[at(base + to * block, block), :], got_one.at[step - 1]
                elif phase == 1:
                    src, dst = part.at[at(to * chunk, chunk), :], got_two.at[step - 1]
                elif phase == 2:
                    src = dst = merged.at[at(mine[1] * chunk, chunk), :]
                else:
                    src, dst = merged, full.at[at(mine[0] * block, block), :]
                pair = (to, mine[1]) if side == 0 else (mine[0], to)
                copy = pltpu.make_async_remote_copy(
                    src_ref=src,
                    dst_ref=dst,
                    send_sem=send.at[index, phase, step - 1],
                    recv_sem=recv.at[index, phase, step - 1],
                    device_id=device(plane_first, *pair),
                    device_id_type=pl.DeviceIdType.MESH,
                )
                copy.start()
                started.append(copy)
        return started

    def wait_all(started):
        for copy in started:
            copy.wait()

    wait_all(start_all(0))
    for index, source, base, plane_first, sizes, mine, block, chunk, buffers in facts:
        got_one, part, got_two, merged, full = buffers

        def add(piece, carry):
            rows = at(piece * chunk, chunk)
            total = source[at(base + mine[0] * block + piece * chunk, chunk), :].astype(F32)
            for step in range(sizes[0] - 1):
                total = total + got_one[step, rows, :].astype(F32)
            part[rows, :] = total.astype(part.dtype)
            return carry

        lax.fori_loop(0, sizes[1], add, 0)
    wait_all(start_all(1))
    for index, source, base, plane_first, sizes, mine, block, chunk, buffers in facts:
        got_one, part, got_two, merged, full = buffers
        rows = at(mine[1] * chunk, chunk)
        total = part[rows, :].astype(F32)
        for step in range(sizes[1] - 1):
            total = total + got_two[step].astype(F32)
        merged[rows, :] = total.astype(merged.dtype)
    wait_all(start_all(2))
    started = start_all(3)
    for index, source, base, plane_first, sizes, mine, block, chunk, buffers in facts:
        merged, full = buffers[3:]
        full[at(mine[0] * block, block), :] = merged[...]
    wait_all(started)
    for index, source, base, plane_first, sizes, mine, block, chunk, buffers in facts:
        full = buffers[4]

        def put(piece, carry):
            rows = at(piece * chunk, chunk)
            if index == count - 1:
                misc_out[rows, :] = full[rows, :]
            else:
                there = at(base + piece * chunk, chunk)
                for part_index, out in enumerate(outs):
                    width = out.shape[1]
                    lanes = slice(part_index * width, (part_index + 1) * width)
                    out[there, :] = full[rows, lanes].astype(F32)
            return carry

        lax.fori_loop(0, n, put, 0)


def sum_over_seq(table, misc, split):
    n = lax.axis_size("seq")
    rows, width = table.shape
    padded, streams = sum_plan(n, rows)
    if padded > rows:
        table = jnp.pad(table, ((0, padded - rows), (0, 0)))
    lanes = -(-misc.size // (8 * n * PAIR)) * PAIR
    misc_table = jnp.pad(misc, (0, 8 * n * lanes - misc.size)).reshape(8 * n, lanes)
    streams = streams + [(0, 8 * n, True)]
    scratch = []
    for index, (_, stream_rows, plane_first) in enumerate(streams):
        last = index == len(streams) - 1
        kind, lane_count = (F32, lanes) if last else (BF16, width)
        one, two = (PLANE, n // PLANE) if plane_first else (n // PLANE, PLANE)
        block, chunk = stream_rows // one, stream_rows // n
        scratch += [
            pltpu.VMEM((one - 1, block, lane_count), kind),
            pltpu.VMEM((block, lane_count), kind),
            pltpu.VMEM((two - 1, chunk, lane_count), kind),
            pltpu.VMEM((block, lane_count), kind),
            pltpu.VMEM((stream_rows, lane_count), kind),
        ]
    partners = max(PLANE, n // PLANE) - 1
    sems = pltpu.SemaphoreType.DMA((len(streams), 4, partners))
    in_vmem = pl.BlockSpec(memory_space=pltpu.VMEM)
    shapes = [jax.ShapeDtypeStruct((padded, width // split), F32)] * split
    *sums, misc_sum = pl.pallas_call(
        partial(sum_kernel, n, streams, split),
        in_specs=[in_vmem, in_vmem],
        out_specs=[in_vmem] * (split + 1),
        out_shape=shapes + [jax.ShapeDtypeStruct(misc_table.shape, F32)],
        scratch_shapes=scratch + [sems, sems],
        compiler_params=params(collective_id=0, has_side_effects=True),
        cost_estimate=pl.CostEstimate(flops=1 << 36, bytes_accessed=1 << 24, transcendentals=0),
        name="sum_over_seq",
    )(table, misc_table)
    return [total[:rows] for total in sums], misc_sum.reshape(-1)[: misc.size]


def plan_kernel(tokens, groups, length_ref, *refs):
    outs, end_ref = refs[:-1], refs[-1]
    docs = length_ref.shape[0]
    my_index, my_side = lax.axis_index("seq"), lax.axis_index("tp")
    all_tokens = tokens * lax.axis_size("seq")
    first = my_index * tokens
    half = tokens // CHUNK

    def add(doc, total):
        total = total + length_ref[doc]
        end_ref[doc] = total
        return total

    lax.fori_loop(0, docs, add, jnp.int32(0))

    q_count = tokens // Q_TILE_BACK
    spots = [first + i * Q_TILE_BACK for i in range(q_count)]
    spots += [spot + Q_TILE_BACK - 1 for spot in spots]
    starts = []
    for distances in groups:
        starts.append([first - d * tokens + h * CHUNK for d in distances for h in range(half)])
        spots += starts[-1] + [start + CHUNK - 1 for start in starts[-1]]

    def count_ends(doc, found):
        end = end_ref[doc]
        return [f + (end <= spot).astype(jnp.int32) for f, spot in zip(found, spots)]

    found = lax.fori_loop(0, docs, count_ends, [jnp.int32(0)] * len(spots))
    found = [
        jnp.where(spot < 0, -1, jnp.where(spot >= all_tokens, FAR_ID, f))
        for f, spot in zip(found, spots)
    ]
    q_low, q_high = found[:q_count], found[q_count : 2 * q_count]
    ratio = Q_TILE // Q_TILE_BACK
    at, rest = 2 * q_count, list(outs)
    for group in starts:
        number = len(group)
        low, high = found[at : at + number], found[at + number : at + 2 * number]
        at += 2 * number
        need = [
            ((h >= q_low[0]) & (l <= q_high[-1])).astype(jnp.int32) for l, h in zip(low, high)
        ]
        ends = [
            [*q_low[::ratio], *q_high[ratio - 1 :: ratio], *low, *high],
            [*q_low, *q_high, *low, *high],
        ]
        for values in ends:
            table = rest.pop(0)
            for i, value in enumerate(values):
                table[i] = value
            base, last, taken = len(values), jnp.int32(0), jnp.int32(0)
            for i in range(number):
                table[base + i] = jnp.int32(0)
            for i in range(number):
                spot = jnp.where(need[i] > 0, taken, number - 1)
                kept = table[base + spot]
                table[base + spot] = jnp.where(need[i] > 0, i, kept)
                last = jnp.where(need[i] > 0, i, last)
                taken = taken + need[i]
            for i in range(number):
                table[base + i] = jnp.where(i < taken, table[base + i], last)
            table[base + number] = taken
        chunk_table, fill_table = rest.pop(0), rest.pop(0)
        for i in range(number):
            block, side = i % (number // 2), i // (number // 2)
            place = 2 * block + jnp.where(my_side == 0, side, 1 - side)
            one, two = need[2 * block + side], need[2 * block + 1 - side]
            wanted = jnp.where(my_side == 0, one, two)
            chunk_table[i] = place
            chunk_table[number + i] = wanted
            chunk_table[2 * number + i] = place * wanted
            fill_table[i] = jnp.where(wanted > 0, place, number)
            fill_table[number + i] = wanted
        need_ref = rest.pop(0)
        for i in range(number):
            need_ref[i] = need[i]

    def ids_of(positions):
        def step(doc, total):
            return total + (end_ref[doc] <= positions).astype(jnp.int32)

        total = lax.fori_loop(0, docs, step, jnp.zeros_like(positions))
        total = jnp.where(positions < 0, -1, total)
        return jnp.where(positions >= all_tokens, FAR_ID, total)

    def rows_of(bases, lanes):
        row = lax.broadcasted_iota(jnp.int32, (len(bases), lanes), 0)
        positions = lax.broadcasted_iota(jnp.int32, (len(bases), lanes), 1)
        for i, base in enumerate(bases):
            positions = positions + jnp.where(row == i, base, 0)
        return ids_of(positions)

    for group in starts:
        rest.pop(0)[...] = rows_of(group, CHUNK)
    rest.pop(0)[...] = rows_of([first + i * Q_TILE for i in range(tokens // Q_TILE)], Q_TILE)
    strips = tokens // STRIP
    for extra in (0, 1):
        bases = [first + i * STRIP - STRIP // 2 for i in range(-extra, strips + extra)]
        rest.pop(0)[...] = rows_of(bases, 2 * STRIP)
    col_ref = rest.pop(0)

    def fill(strip, carry):
        row = lax.broadcasted_iota(jnp.int32, (STRIP, PAIR), 0)
        rows = pl.ds(pl.multiple_of(strip * STRIP, STRIP), STRIP)
        col_ref[rows, :] = ids_of(row + (first + (strip - 2) * STRIP))
        return carry

    lax.fori_loop(0, strips + 4, fill, 0)


def plan(lengths, tokens, groups):
    half = tokens // CHUNK
    q_tiles, q_back = tokens // Q_TILE, tokens // Q_TILE_BACK
    strips = tokens // STRIP
    sizes, rows = [], []
    for distances in groups:
        number = half * len(distances)
        sizes += [
            2 * q_tiles + 3 * number + 1,
            2 * q_back + 3 * number + 1,
            3 * number,
            2 * number,
            number,
        ]
        rows.append((number, CHUNK))
    rows += [(q_tiles, Q_TILE), (strips, 2 * STRIP), (strips + 2, 2 * STRIP)]
    rows.append(((strips + 4) * STRIP, PAIR))
    smem = pl.BlockSpec(memory_space=pltpu.SMEM)
    vmem = pl.BlockSpec(memory_space=pltpu.VMEM)
    shapes = [(size,) for size in sizes] + rows
    outs = pl.pallas_call(
        partial(plan_kernel, tokens, groups),
        in_specs=[smem],
        out_specs=[smem] * len(sizes) + [vmem] * len(rows),
        out_shape=[jax.ShapeDtypeStruct(shape, jnp.int32) for shape in shapes],
        scratch_shapes=[pltpu.SMEM(lengths.shape, jnp.int32)],
        compiler_params=params(),
        cost_estimate=LIGHT,
        name="plan",
    )(lengths)
    tables = [outs[5 * i : 5 * i + 5] for i in range(len(groups))]
    return [list(column) for column in zip(*tables)], outs[len(sizes) :]


def shifted(block, axis, distance):
    count = lax.axis_size(axis)
    route = [(i, i + distance) for i in range(count) if 0 <= i + distance < count]
    return lax.ppermute(block, axis, route)


def swapped(block, axis):
    return lax.ppermute(block, axis, [(0, 1), (1, 0)])


def tp_sum(partial_low):
    return partial_low.astype(F32) + swapped(partial_low, "tp").astype(F32)


def after(value, *others):
    return lax.optimization_barrier((value, *others))[0]


def layer_norm(vectors, gain_row, shift_row):
    center = vectors - jnp.mean(vectors, axis=-1, keepdims=True)
    spread = jnp.mean(center * center, axis=-1, keepdims=True)
    return center * lax.rsqrt(spread + EPS_LAYER) * gain_row + shift_row


def body(
    inputs,
    cotangent,
    query_weight,
    key_weight,
    value_weight,
    out_weight,
    up_weight,
    down_weight,
    conv_taps,
    attn_gain,
    attn_shift,
    ffn_gain,
    ffn_shift,
    hyperplanes,
    lengths,
):
    tokens, depth = inputs.shape
    head_dim = hyperplanes.shape[2]
    width = query_weight.shape[1]
    half = tokens // 2
    my_side = lax.axis_index("tp")
    all_tokens = tokens * lax.axis_size("seq")
    far_reach = (MOST + tokens - 2) // tokens
    close = far_reach // 2
    near = list(range(close, 0, -1)) + list(range(-1, -close - 1, -1))
    far = list(range(far_reach, close, -1)) + list(range(-close - 1, -far_reach - 1, -1))

    mine_rows = lax.dynamic_slice_in_dim(inputs, my_side * half, half, 0)
    near_mine = [shifted(mine_rows, "seq", d) for d in near]

    near_at, far_at, own_at = range(3)
    k_counts = [tokens // CHUNK * len(distances) for distances in (near, far, [0])]
    (tables, back_tables, chunk_tables, fill_tables, needs), id_rows = plan(
        lengths, tokens, (near, far, [0])
    )
    near_rows, far_rows, own_key_rows, own_rows, mix_row, back_row, ids_col = id_rows

    weight_qkv = jnp.concatenate([query_weight, key_weight, value_weight], axis=1)
    weight_kv = weight_qkv[:, width:]
    plain_table = jnp.array(list(range(tokens // CHUNK)) + [1] * (tokens // CHUNK), jnp.int32)
    query_unit, query_scale, key_unit, key_scale, values = project(
        plain_table, [inputs], weight_qkv, 2, head_dim
    )
    gathered, own_weights = attend(
        tables[own_at], query_unit, key_unit, values, own_rows, own_key_rows, head_dim
    )

    def other_half(mine):
        return jnp.concatenate([swapped(term, "tp") for term in mine], axis=0)

    *near_mine, late_rows = after((*near_mine, mine_rows), gathered)
    far_mine = [shifted(late_rows if i else mine_rows, "seq", d) for i, d in enumerate(far)]
    group_x, group_kv, group_weights = [], [], []
    for index, mine in ((near_at, near_mine), (far_at, far_mine)):
        if index == far_at:
            mine = after(tuple(mine), gathered)
        group_x.append([*mine, other_half(mine)])
        key_far, scale_far, value_far = project(
            fill_tables[index], group_x[index], weight_kv, 1, head_dim, k_counts[index]
        )
        group_kv.append((key_far, scale_far, value_far))
        gathered, weights = attend(
            tables[index],
            query_unit,
            key_far,
            value_far,
            own_rows,
            (near_rows, far_rows)[index],
            head_dim,
            seed=gathered,
        )
        group_weights.append(weights)
    edge = close * tokens
    sides = needs[near_at][edge // CHUNK - 1 : edge // CHUNK + 1]
    values_rim = jnp.where(
        jnp.repeat(sides, RIM)[:, None] > 0, group_kv[near_at][2][edge - RIM : edge + RIM], 0
    )
    mixed = mix(gathered, values, values_rim, mix_row, ids_col, conv_taps, head_dim)

    attn_out = tp_sum(nn(mixed, out_weight).astype(BF16))
    first_norm, first_back = jax.vjp(
        layer_norm, inputs.astype(F32) + attn_out, attn_gain, attn_shift
    )
    first_low = first_norm.astype(BF16)
    partial_out, active, slope = feed(first_low, up_weight, down_weight)
    ffn_out = tp_sum(partial_out)
    result, second_back = jax.vjp(layer_norm, first_norm + ffn_out, ffn_gain, ffn_shift)
    output = result.astype(BF16)
    grad_second, grad_ffn_gain, grad_ffn_shift = second_back(cotangent.astype(F32))
    grad_ffn = grad_second.astype(BF16)
    grad_hidden = (nt(grad_ffn, down_weight) * slope.astype(F32)).astype(BF16)
    grad_first = grad_second + tp_sum(nt(grad_hidden, up_weight).astype(BF16))
    grad_residual, grad_attn_gain, grad_attn_shift = first_back(grad_first)
    grad_attn = grad_residual.astype(BF16)
    grad_mixed = nt(grad_attn, out_weight).astype(BF16)

    grad_down = tn(active, grad_ffn).astype(BF16)
    grad_up = tn(first_low, grad_hidden).astype(BF16)
    grad_out = tn(mixed, grad_attn).astype(BF16)
    down_out = jnp.concatenate([grad_down, grad_out], axis=0)
    grad_up_low, down_out_low = grad_up, down_out
    grad_up, down_out = lax.psum((grad_up_low, down_out_low), "seq")

    grad_rows = back_norm(gathered, after(grad_mixed, grad_up_low, down_out_low), head_dim)

    def back_scores(index, grad_rows, seed):
        key_far, _, value_far = group_kv[index]
        return back_attend(
            back_tables[index],
            k_counts[index],
            query_unit,
            grad_rows,
            key_far,
            value_far,
            group_weights[index],
            head_dim,
            seed=seed,
        )

    def back_inputs(index, dk, dv, **rims):
        key_far, scale_far, _ = group_kv[index]
        parts = [(key_far, scale_far, dk)]
        return back_project(
            chunk_tables[index], group_x[index], weight_kv, parts, 0, [dv], head_dim, **rims
        )

    def send_home(distances, dx_mine, came):
        both = [
            (
                dx_mine[i * half : (i + 1) * half].astype(F32)
                + came[i * half : (i + 1) * half].astype(F32)
            ).astype(BF16)
            for i in range(len(distances))
        ]
        return both, [shifted(term, "seq", -d) for term, d in zip(both, distances)]

    dk, dv, turned = back_scores(far_at, grad_rows, None)
    far_dx, dx_other, far_dw = back_inputs(far_at, dk, dv)
    far_came = swapped(dx_other, "tp")
    grad_conv_values, grad_taps = back_conv(
        values, values_rim, after(grad_mixed, far_dx), back_row, ids_col, conv_taps, head_dim
    )
    rim = jnp.concatenate([grad_conv_values[:STRIP], grad_conv_values[-STRIP:]], axis=0)
    dk, dv, turned = back_scores(near_at, after(grad_rows, grad_conv_values), turned)
    near_dx, dx_other, near_dw = back_inputs(
        near_at, dk, dv, rims=close * (tokens // CHUNK) - 1, rim=rim
    )
    near_came = swapped(dx_other, "tp")
    far_came, grad_up, down_out = after((far_came, grad_up, down_out), near_dx)
    terms, far_homes = send_home(far, far_dx, far_came)
    dk, dv, turned = back_attend(
        back_tables[own_at],
        k_counts[own_at],
        query_unit,
        after(grad_rows, *terms),
        key_unit,
        values,
        own_weights,
        head_dim,
        seed=turned,
        cost=pl.CostEstimate(flops=1 << 35, bytes_accessed=1 << 20, transcendentals=0),
    )
    terms, near_homes = send_home(near, near_dx, after(near_came, dk))
    dk, key_late, far_homes = after((dk, key_unit, far_homes), *terms)
    own_mine = mine_rows
    own_other = lax.dynamic_slice_in_dim(inputs, (1 - my_side) * half, half, 0)
    dx_mine, dx_other, dw = back_project(
        chunk_tables[own_at],
        [own_mine, own_other],
        weight_qkv,
        [(query_unit, query_scale, turned), (key_unit, key_scale, dk)],
        1,
        [dv, grad_conv_values[STRIP:-STRIP]],
        head_dim,
    )

    occ_local = occupancy(after(key_late, dw), hyperplanes, 2.0**BITS / all_tokens)
    near_homes = after(tuple(near_homes), occ_local)
    qkv = jnp.concatenate([dw[:, :width], dw[:, width:] + near_dw + far_dw], axis=1).astype(BF16)
    misc = [
        occ_local,
        grad_taps,
        grad_attn_gain,
        grad_attn_shift,
        grad_ffn_gain,
        grad_ffn_shift,
    ]
    packed = jnp.concatenate([term.reshape(-1) for term in misc])
    qkv, packed = sum_over_seq(qkv, packed, 3)

    came = swapped(dx_other, "tp")
    total = (
        lax.dynamic_slice_in_dim(grad_residual, my_side * half, half, 0)
        + dx_mine.astype(F32)
        + came.astype(F32)
    )
    for home in (*far_homes, *near_homes):
        total = total + home.astype(F32)
    other_total = swapped(total, "tp")
    lower = jnp.where(my_side == 0, total, other_total)
    upper = jnp.where(my_side == 0, other_total, total)
    grad_inputs = jnp.concatenate([lower, upper], axis=0)

    unpacked, at = [], 0
    for term in misc:
        unpacked.append(packed[at : at + term.size].reshape(term.shape))
        at += term.size
    down_out = down_out.astype(F32)
    ff = down_weight.shape[0]
    return (
        output,
        grad_inputs,
        *qkv,
        down_out[ff:],
        grad_up.astype(F32),
        down_out[:ff],
        *unpacked[1:],
        unpacked[0],
    )


def solution(mesh):
    return jax.shard_map(
        body,
        mesh=mesh,
        in_specs=(
            P("seq", None),
            P("seq", None),
            P(None, "tp"),
            P(None, "tp"),
            P(None, "tp"),
            P("tp", None),
            P(None, "tp"),
            P("tp", None),
            P("tp", None),
            P(),
            P(),
            P(),
            P(),
            P(),
            P(),
        ),
        out_specs=(
            P("seq", None),
            P("seq", None),
            P(None, "tp"),
            P(None, "tp"),
            P(None, "tp"),
            P("tp", None),
            P(None, "tp"),
            P("tp", None),
            P("tp", None),
            P(),
            P(),
            P(),
            P(),
            P("tp", None, None),
        ),
        check_vma=False,
    )
```

```python
from functools import partial
import math

import jax
import jax.numpy as jnp
from jax import lax
from jax.experimental import pallas as pl
from jax.experimental.pallas import tpu as pltpu
from jax.sharding import PartitionSpec as P

TAU = 8
BITS = 8
CONV = 33
MOST = 4096
RIM = (CONV - 1) // 2

EPS_UNIT = 1e-06
EPS_LAYER = 1e-05
SHARP = 4.0
CLIP_EDGE = 0.999

CHUNK = 512
Q_TILE = 512
Q_TILE_BACK = 256
PAIR = 128
STRIP = 128
FAR_ID = 1 << 20

LIGHT = pl.CostEstimate(flops=1 << 20, bytes_accessed=1 << 16, transcendentals=0)

F32 = jnp.float32
BF16 = jnp.bfloat16

ARC = (
    0.49999961256980896,
    -0.06828052550554276,
    0.027964841574430466,
    -0.014291195198893547,
    0.006136968266218901,
    -0.001371906721033156,
)


def params(**kwargs):
    return pltpu.CompilerParams(vmem_limit_bytes=56 << 20, **kwargs)


def nn(left, right):
    return lax.dot_general(left, right, (((1,), (0,)), ((), ())), preferred_element_type=F32)


def nt(left, right):
    return lax.dot_general(left, right, (((1,), (1,)), ((), ())), preferred_element_type=F32)


def tn(left, right):
    return lax.dot_general(left, right, (((0,), (0,)), ((), ())), preferred_element_type=F32)


def head_masks(head_dim):
    lanes = lax.broadcasted_iota(jnp.int32, (1, PAIR), 1)
    first = (lanes < head_dim).astype(F32)
    return first.astype(BF16), (1.0 - first).astype(BF16)


def head_sum(rows, head_dim):
    here = lax.broadcasted_iota(jnp.int32, (PAIR, PAIR), 0) // head_dim
    there = lax.broadcasted_iota(jnp.int32, (PAIR, PAIR), 1) // head_dim
    ones = (here == there).astype(F32).astype(BF16)
    sums = []
    for start in range(0, rows.shape[1], PAIR):
        part = rows[:, start : start + PAIR]
        high = part.astype(BF16)
        low = (part - high.astype(F32)).astype(BF16)
        sums.append(nn(high, ones) + nn(low, ones))
    return jnp.concatenate(sums, axis=1)


def pick_half(mine_refs, other_ref, kept):
    step = pl.program_id(0)
    for index, ref in enumerate(mine_refs):

        @pl.when(step == index)
        def _():
            kept[...] = ref[...]

    @pl.when(step >= len(mine_refs))
    def _():
        kept[...] = other_ref[...]


def other_spec(count, shape):
    return pl.BlockSpec(shape, lambda i, t: (jnp.maximum(i - count, 0), 0))


def half_specs(count, shape):
    return [pl.BlockSpec(shape, lambda i, t: (0, 0))] * count + [other_spec(count, shape)]


def project_kernel(units, count, head_dim, table, *refs):
    if count:
        mine_refs, other_ref, w_ref = refs[:count], refs[count], refs[count + 1]
        out_refs, kept = refs[count + 2 : -1], refs[-1]
        pick_half(mine_refs, other_ref, kept)
    else:
        kept, w_ref = refs[:2]
        out_refs = refs[2:]
    width = out_refs[-1].shape[1]
    needed = table[pl.num_programs(0) + pl.program_id(0)] > 0

    @pl.when(needed)
    def _():
        whole = nn(kept[...], w_ref[...])
        for index in range(units):
            part = whole[:, index * width : (index + 1) * width]
            scale = lax.rsqrt(head_sum(part * part, head_dim) * (1.0 / head_dim) + EPS_UNIT)
            scale = scale * (1.0 / math.sqrt(head_dim))
            out_refs[2 * index][...] = (part * scale).astype(BF16)
            out_refs[2 * index + 1][...] = scale
        out_refs[-1][...] = whole[:, units * width :].astype(BF16)


def project(table, halves, weight, units, head_dim, chunks=None):
    depth = halves[0].shape[1]
    rows = sum(h.shape[0] for h in halves)
    count = len(halves) - 1
    width = weight.shape[1] // (units + 1)
    row_spec = pl.BlockSpec((CHUNK, width), lambda i, t: (t[i], 0))
    held = (chunks + 1) * CHUNK if count else rows
    if count:
        x_specs = half_specs(count, (CHUNK, depth))
    else:
        x_specs = [pl.BlockSpec((CHUNK, depth), lambda i, t: (i, 0))]
    unit_shapes = [
        jax.ShapeDtypeStruct((held, width), BF16),
        jax.ShapeDtypeStruct((held, width), F32),
    ]
    return pl.pallas_call(
        partial(project_kernel, units, count, head_dim),
        grid_spec=pltpu.PrefetchScalarGridSpec(
            num_scalar_prefetch=1,
            grid=(rows // CHUNK,),
            in_specs=x_specs + [pl.BlockSpec(weight.shape, lambda i, t: (0, 0))],
            out_specs=[row_spec] * (2 * units + 1),
            scratch_shapes=[pltpu.VMEM((CHUNK, depth), BF16)] if count else [],
        ),
        out_shape=unit_shapes * units + [jax.ShapeDtypeStruct((held, width), BF16)],
        compiler_params=params(),
        cost_estimate=pl.CostEstimate(
            flops=4 * rows * depth * weight.shape[1], bytes_accessed=rows * depth, transcendentals=0
        ),
        name="project",
    )(table, *halves, weight)


def collide(scores):
    size = jnp.minimum(jnp.abs(scores), CLIP_EDGE)
    rest = 1.0 - size
    poly = ARC[5]
    for factor in ARC[4::-1]:
        poly = poly * size + factor
    angle = (rest * lax.rsqrt(rest)) * poly
    return jnp.where(scores < 0.0, angle, 1.0 - angle)


def tile_facts(table, tiles_q, tiles_k, qi, kt):
    q_low, q_high = table[qi], table[tiles_q + qi]
    k_low, k_high = table[2 * tiles_q + kt], table[2 * tiles_q + tiles_k + kt]
    needed = (k_high >= q_low) & (k_low <= q_high)
    whole = (q_low == q_high) & (k_low == k_high)
    return needed, whole


def id_column(row, lanes):
    column = jnp.broadcast_to(row, (PAIR, row.shape[1])).T
    return jnp.concatenate([column] * (lanes // PAIR), axis=1)


def attend_kernel(
    head_dim, tiles_k, seeded, table, q_ref, qrow_ref, krow_ref, k_ref, v_ref, *rest
):
    out_ref, w_ref = rest[-2:]
    tiles_q = q_ref.shape[0] // Q_TILE
    step, steps = pl.program_id(1), pl.num_programs(1)
    order = 2 * (tiles_q + tiles_k)
    masks = head_masks(head_dim)

    @pl.when(step == 0)
    def _():
        if seeded:
            out_ref[...] = rest[0][...]
        else:
            out_ref[...] = jnp.zeros_like(out_ref)

    @pl.when(step < table[order + steps])
    def _():
        kt = table[order + step]

        def q_loop(qi, carry):
            rows = pl.ds(pl.multiple_of(qi * Q_TILE, Q_TILE), Q_TILE)
            needed, whole = tile_facts(table, tiles_q, tiles_k, qi, kt)

            def part(same):
                q, k = q_ref[rows, :], k_ref[...]
                v_turned = v_ref[...].T
                for index, mask in enumerate(masks):
                    chance = collide(nt(k, q * mask))
                    chance = chance * chance
                    chance = chance * chance
                    chance = chance * chance
                    if same is not None:
                        chance = jnp.where(same, chance, 0.0)
                    weights = chance.astype(BF16)
                    w_ref[index, :, rows] = weights
                    half = slice(index * head_dim, (index + 1) * head_dim)
                    out_ref[half, rows] += nn(v_turned[half, :], weights)

            @pl.when(needed & whole)
            def _():
                part(None)

            @pl.when(needed & jnp.logical_not(whole))
            def _():
                part(id_column(krow_ref[pl.ds(kt, 1), :], Q_TILE) == qrow_ref[pl.ds(qi, 1), :])

            @pl.when(jnp.logical_not(needed))
            def _():
                w_ref[:, :, rows] = jnp.zeros((2, CHUNK, Q_TILE), BF16)

            return carry

        lax.fori_loop(0, tiles_q, q_loop, 0)


def attend(table, q, k, v, qrow, krow, head_dim, seed=None):
    tokens, width = q.shape
    tiles_k = krow.shape[0]
    order = 2 * (tokens // Q_TILE + tiles_k)
    k_spec = pl.BlockSpec((CHUNK, PAIR), lambda p, j, t: (t[order + j], p))
    turned_spec = pl.BlockSpec((PAIR, tokens), lambda p, j, t: (p, 0))
    operands = [q, qrow, krow, k, v]
    specs = [
        pl.BlockSpec((tokens, PAIR), lambda p, j, t: (0, p)),
        pl.BlockSpec(qrow.shape, lambda p, j, t: (0, 0)),
        pl.BlockSpec(krow.shape, lambda p, j, t: (0, 0)),
        k_spec,
        k_spec,
    ]
    if seed is not None:
        operands.append(seed)
        specs.append(turned_spec)
    return pl.pallas_call(
        partial(attend_kernel, head_dim, tiles_k, seed is not None),
        grid_spec=pltpu.PrefetchScalarGridSpec(
            num_scalar_prefetch=1,
            grid=(width // PAIR, tiles_k),
            in_specs=specs,
            out_specs=[
                turned_spec,
                pl.BlockSpec((2, CHUNK, tokens), lambda p, j, t: (p, t[order + j], 0)),
            ],
        ),
        out_shape=[
            jax.ShapeDtypeStruct((width, tokens), F32),
            jax.ShapeDtypeStruct((width // head_dim, tiles_k * CHUNK, tokens), BF16),
        ],
        compiler_params=params(),
        cost_estimate=pl.CostEstimate(
            flops=32 * tokens * tiles_k * CHUNK * width,
            bytes_accessed=tokens * width * 4,
            transcendentals=0,
        ),
        name="attend",
    )(table, *operands)


def back_attend_kernel(
    head_dim, tiles_k, seeded, table, q_ref, g_ref, k_ref, v_ref, w_ref, *rest
):
    dk_ref, dv_ref, dq_ref, acc_k, acc_v = rest[-5:]
    tiles_q = q_ref.shape[0] // Q_TILE_BACK
    step, steps = pl.program_id(1), pl.num_programs(1)
    order = 2 * (tiles_q + tiles_k)
    masks = head_masks(head_dim)

    @pl.when(step == 0)
    def _():
        if seeded:
            dq_ref[...] = rest[0][...]
        else:
            dq_ref[...] = jnp.zeros_like(dq_ref)

    @pl.when(step < table[order + steps])
    def _():
        kt = table[order + step]
        acc_k[...] = jnp.zeros_like(acc_k)
        acc_v[...] = jnp.zeros_like(acc_v)

        def q_loop(qi, carry):
            needed, _ = tile_facts(table, tiles_q, tiles_k, qi, kt)

            @pl.when(needed)
            def _():
                rows = pl.ds(pl.multiple_of(qi * Q_TILE_BACK, Q_TILE_BACK), Q_TILE_BACK)
                q, g, k, v = q_ref[rows, :], g_ref[rows, :], k_ref[...], v_ref[...]
                k_turned = k.T
                sum_k, sum_v = None, None
                for index, mask in enumerate(masks):
                    q_half, g_half = q * mask, g * mask
                    scores = nt(k, q_half)
                    weights = w_ref[index, :, rows]
                    power = jnp.exp(((TAU - 1) / TAU) * jnp.log(weights.astype(F32)))
                    square = scores * scores
                    slope = nt(v, g_half) * (power * lax.rsqrt(1.0 - square))
                    slope = jnp.where(square <= CLIP_EDGE * CLIP_EDGE, slope, 0.0).astype(BF16)
                    term_v = nn(weights, g_half)
                    term_k = nn(slope, q_half)
                    sum_v = term_v if sum_v is None else sum_v + term_v
                    sum_k = term_k if sum_k is None else sum_k + term_k
                    half = slice(index * head_dim, (index + 1) * head_dim)
                    dq_ref[half, rows] += nn(k_turned[half, :], slope)
                acc_v[...] += sum_v
                acc_k[...] += sum_k

            return carry

        lax.fori_loop(0, tiles_q, q_loop, 0)
        dk_ref[...] = acc_k[...].astype(BF16)
        dv_ref[...] = acc_v[...].astype(BF16)


def back_attend(table, tiles_k, q, g, k, v, weights, head_dim, seed=None, cost=LIGHT):
    tokens, width = q.shape
    order = 2 * (tokens // Q_TILE_BACK + tiles_k)
    q_spec = pl.BlockSpec((tokens, PAIR), lambda p, j, t: (0, p))
    k_spec = pl.BlockSpec((CHUNK, PAIR), lambda p, j, t: (t[order + j], p))
    dq_spec = pl.BlockSpec((PAIR, tokens), lambda p, j, t: (p, 0))
    specs = [
        q_spec,
        q_spec,
        k_spec,
        k_spec,
        pl.BlockSpec((2, CHUNK, tokens), lambda p, j, t: (p, t[order + j], 0)),
    ]
    operands = [q, g, k, v, weights]
    if seed is not None:
        operands.append(seed)
        specs.append(dq_spec)
    return pl.pallas_call(
        partial(back_attend_kernel, head_dim, tiles_k, seed is not None),
        grid_spec=pltpu.PrefetchScalarGridSpec(
            num_scalar_prefetch=1,
            grid=(width // PAIR, tiles_k),
            in_specs=specs,
            out_specs=[k_spec, k_spec, dq_spec],
            scratch_shapes=[pltpu.VMEM((CHUNK, PAIR), F32), pltpu.VMEM((CHUNK, PAIR), F32)],
        ),
        out_shape=[
            jax.ShapeDtypeStruct((tiles_k * CHUNK, width), BF16),
            jax.ShapeDtypeStruct((tiles_k * CHUNK, width), BF16),
            jax.ShapeDtypeStruct((width, tokens), F32),
        ],
        compiler_params=params(),
        cost_estimate=cost,
        name="back_attend",
    )(table, *operands)


def back_project_kernel(units, turned, terms, rims, count, head_dim, table, *refs):
    mine_refs, other_ref, w_ref = refs[:count], refs[count], refs[count + 1]
    dx_mine, dx_other, dw_ref, kept, sum_ref = refs[-5:]
    refs = refs[count + 2 : -5]
    step = pl.program_id(0)
    place, needed = table[step], table[pl.num_programs(0) + step] > 0

    @pl.when(step == 0)
    def _():
        dw_ref[...] = jnp.zeros_like(dw_ref)

    def store(value):
        @pl.when(step < count)
        def _():
            dx_mine[...] = value

        @pl.when(step >= count)
        def _():
            dx_other[...] = value

    @pl.when(needed)
    def _():
        pick_half(mine_refs, other_ref, kept)
        grads = []
        for index in range(units):
            unit_ref, scale_ref, grad_ref = refs[3 * index : 3 * index + 3]
            grad = grad_ref[...].astype(F32)
            if index < turned:
                grad = grad.T
            unit = unit_ref[...].astype(F32)
            inner = head_sum(grad * unit, head_dim)
            grads.append(
                ((TAU / math.pi) * scale_ref[...] * (grad - unit * inner)).astype(BF16)
            )
        value_refs = refs[3 * units : 3 * units + terms]
        value = value_refs[0][...].astype(F32)
        for extra in value_refs[1:]:
            value = value + extra[...].astype(F32)
        if rims is not None:
            rim_ref = refs[-1]
            sum_ref[...] = value

            @pl.when(place == rims)
            def _():
                sum_ref[CHUNK - STRIP :, :] += rim_ref[:STRIP, :]

            @pl.when(place == rims + 1)
            def _():
                sum_ref[:STRIP, :] += rim_ref[STRIP:, :]

            value = sum_ref[...]
        grads.append(value.astype(BF16))
        joined = jnp.concatenate(grads, axis=1)
        store(nt(joined, w_ref[...]).astype(BF16))
        dw_ref[...] += tn(kept[...], joined)

    @pl.when(jnp.logical_not(needed))
    def _():
        store(jnp.zeros(dx_mine.shape, BF16))


def back_project(table, halves, weight, parts, turned, values, head_dim, rims=None, rim=None):
    depth = halves[0].shape[1]
    count = len(halves) - 1
    width = values[0].shape[1]
    row_spec = pl.BlockSpec((CHUNK, width), lambda i, t: (t[4 * count + i], 0))
    weight_spec = pl.BlockSpec(weight.shape, lambda i, t: (0, 0))
    wide_specs = [
        pl.BlockSpec((CHUNK, depth), lambda i, t: (jnp.minimum(i, count - 1), 0)),
        other_spec(count, (CHUNK, depth)),
    ]
    specs = half_specs(count, (CHUNK, depth)) + [weight_spec]
    operands = [*halves, weight]
    for index, (unit, scale, grad) in enumerate(parts):
        operands += [unit, scale, grad]
        specs += [row_spec, row_spec]
        specs.append(
            pl.BlockSpec((width, CHUNK), lambda i, t: (0, t[4 * count + i]))
            if index < turned
            else row_spec
        )
    operands += values
    specs += [row_spec] * len(values)
    if rim is not None:
        operands.append(rim)
        specs.append(pl.BlockSpec(rim.shape, lambda i, t: (0, 0)))
    return pl.pallas_call(
        partial(back_project_kernel, len(parts), turned, len(values), rims, count, head_dim),
        grid_spec=pltpu.PrefetchScalarGridSpec(
            num_scalar_prefetch=1,
            grid=(2 * count,),
            in_specs=specs,
            out_specs=wide_specs + [weight_spec],
            scratch_shapes=[pltpu.VMEM((CHUNK, depth), BF16), pltpu.VMEM((CHUNK, width), F32)],
        ),
        out_shape=[
            jax.ShapeDtypeStruct((count * CHUNK, depth), BF16),
            jax.ShapeDtypeStruct((count * CHUNK, depth), BF16),
            jax.ShapeDtypeStruct(weight.shape, F32),
        ],
        compiler_params=params(),
        cost_estimate=LIGHT,
        name="back_project",
    )(table, *operands)


def lane_taps(conv_taps, mirrored):
    front = STRIP // 2 - RIM
    heads = conv_taps.shape[0]
    taps = conv_taps[:, ::-1] if mirrored else conv_taps
    return jnp.pad(taps, ((0, -heads % 8), (front, 2 * STRIP - front - CONV)))


def fill_bands(taps_ref, bands, heads):
    for head in range(heads):
        row = jnp.broadcast_to(taps_ref[head : head + 1, :], (STRIP, 2 * STRIP))
        bands[head] = pltpu.roll(row, 0, 1, stride=1, stride_axis=0)


def band_product(band, same, window):
    band = jnp.where(same, band, 0.0)
    high = band.astype(BF16)
    low = (band - high.astype(F32)).astype(BF16)
    return nn(high, window) + nn(low, window)


def fill_extended(kept, edge, centre_ref, rim_ref):
    rows = centre_ref.shape[0]
    kept[...] = jnp.zeros_like(kept)
    kept[edge : edge + rows, :] = centre_ref[...]
    if rim_ref is not None:
        kept[edge - RIM : edge, :] = rim_ref[:RIM, :]
        kept[edge + rows : edge + rows + RIM, :] = rim_ref[RIM:, :]


def mix_kernel(head_dim, g_ref, col_ref, v_ref, rim_ref, row_ref, taps_ref, out_ref, bands, kept):
    heads = g_ref.shape[0] // head_dim
    step = pl.program_id(0)

    @pl.when(step == 0)
    def _():
        fill_bands(taps_ref, bands, heads)
        fill_extended(kept, STRIP, v_ref, rim_ref)

    masks = head_masks(head_dim)
    window = kept[pl.ds(pl.multiple_of(step * STRIP + STRIP // 2, STRIP // 2), 2 * STRIP), :]
    ids = col_ref[...]
    same = jnp.concatenate([ids, ids], axis=1) == row_ref[pl.ds(step, 1), :]
    pieces = []
    for pair in range(heads // 2):
        values = window[:, pair * PAIR : (pair + 1) * PAIR]
        total = None
        for index, mask in enumerate(masks):
            term = band_product(bands[2 * pair + index], same, values * mask)
            total = term if total is None else total + term
        pieces.append(total)
    gathered = g_ref[...].T
    scale = lax.rsqrt(head_sum(gathered * gathered, head_dim) * (1.0 / head_dim) + EPS_UNIT)
    out_ref[...] = (gathered * scale + jnp.concatenate(pieces, axis=1)).astype(BF16)


def mix(gathered, values, rim, row, col, conv_taps, head_dim):
    width, tokens = gathered.shape
    heads = width // head_dim
    strips = tokens // STRIP
    taps = lane_taps(conv_taps, False)
    row_spec = pl.BlockSpec((STRIP, width), lambda i: (i, 0))
    whole = [values, rim, row, taps]
    return pl.pallas_call(
        partial(mix_kernel, head_dim),
        grid=(strips,),
        in_specs=[
            pl.BlockSpec((width, STRIP), lambda i: (0, i)),
            pl.BlockSpec((STRIP, PAIR), lambda i: (i + 2, 0)),
        ]
        + [pl.BlockSpec(a.shape, lambda i: (0, 0)) for a in whole],
        out_specs=row_spec,
        out_shape=jax.ShapeDtypeStruct((tokens, width), BF16),
        scratch_shapes=[
            pltpu.VMEM((heads, STRIP, 2 * STRIP), F32),
            pltpu.VMEM((tokens + 2 * STRIP, width), BF16),
        ],
        compiler_params=params(),
        cost_estimate=LIGHT,
        name="mix",
    )(gathered, col, *whole)


def back_norm_kernel(head_dim, g_ref, m_ref, out_ref):
    gathered, grad = g_ref[...].T, m_ref[...].astype(F32)
    scale = lax.rsqrt(head_sum(gathered * gathered, head_dim) * (1.0 / head_dim) + EPS_UNIT)
    mean = head_sum(grad * gathered, head_dim) * (1.0 / head_dim)
    out_ref[...] = (scale * (grad - (scale * scale) * gathered * mean)).astype(BF16)


def back_norm(gathered, grad_mixed, head_dim):
    width, tokens = gathered.shape
    row_spec = pl.BlockSpec((CHUNK, width), lambda i: (i, 0))
    return pl.pallas_call(
        partial(back_norm_kernel, head_dim),
        grid=(tokens // CHUNK,),
        in_specs=[pl.BlockSpec((width, CHUNK), lambda i: (0, i)), row_spec],
        out_specs=row_spec,
        out_shape=jax.ShapeDtypeStruct((tokens, width), BF16),
        compiler_params=params(),
        cost_estimate=LIGHT,
        name="back_norm",
    )(gathered, grad_mixed)


def back_conv_kernel(
    head_dim, col_ref, v_ref, rim_ref, m_ref, row_ref, taps_ref, dv_ref, tap_ref, bands, sums, kept_v, kept_m
):
    heads = dv_ref.shape[1] // head_dim
    step, steps = pl.program_id(0), pl.num_programs(0)

    @pl.when(step == 0)
    def _():
        fill_bands(taps_ref, bands, heads)
        fill_extended(kept_v, 2 * STRIP, v_ref, rim_ref)
        fill_extended(kept_m, 2 * STRIP, m_ref, None)
        sums[...] = jnp.zeros_like(sums)

    masks = head_masks(head_dim)
    around = pl.ds(pl.multiple_of(step * STRIP + STRIP // 2, STRIP // 2), 2 * STRIP)
    centre = pl.ds(pl.multiple_of(step * STRIP + STRIP, STRIP), STRIP)
    ids = col_ref[...]
    same = jnp.concatenate([ids, ids], axis=1) == row_ref[pl.ds(step, 1), :]
    pieces = []
    for pair in range(heads // 2):
        cols = slice(pair * PAIR, (pair + 1) * PAIR)
        grads, values, here = kept_m[around, cols], kept_v[around, cols], kept_m[centre, cols]
        total = None
        for index, mask in enumerate(masks):
            head = 2 * pair + index
            term = band_product(bands[head], same, grads * mask)
            total = term if total is None else total + term
            sums[head] += jnp.where(same, nt(here * mask, values), 0.0)
        pieces.append(total)
    dv_ref[...] = jnp.concatenate(pieces, axis=1)

    @pl.when(step == steps - 1)
    def _():
        tap_ref[...] = jnp.zeros_like(tap_ref)
        places = [lax.broadcasted_iota(jnp.int32, (STRIP, STRIP), d) for d in (0, 1)]
        flip = (places[0] + places[1] == STRIP - 1).astype(F32).astype(BF16)
        for head in range(heads):
            total = sums[head]
            high = total.astype(BF16)
            low = (total - high.astype(F32)).astype(BF16)
            turned = pltpu.roll(
                nn(flip, high) + nn(flip, low), STRIP + 1, 1, stride=1, stride_axis=0
            )
            tap_ref[head : head + 1, :] = jnp.sum(turned, axis=0, keepdims=True)


def back_conv(values, rim, grad_mixed, row, col, conv_taps, head_dim):
    tokens, width = values.shape
    heads = width // head_dim
    strips = tokens // STRIP + 2
    taps = lane_taps(conv_taps, True)
    front = STRIP // 2 - RIM
    whole = [values, rim, grad_mixed, row, taps]
    grad_values, tap_sums = pl.pallas_call(
        partial(back_conv_kernel, head_dim),
        grid=(strips,),
        in_specs=[pl.BlockSpec((STRIP, PAIR), lambda i: (i + 1, 0))]
        + [pl.BlockSpec(a.shape, lambda i: (0, 0)) for a in whole],
        out_specs=[
            pl.BlockSpec((STRIP, width), lambda i: (i, 0)),
            pl.BlockSpec(taps.shape, lambda i: (0, 0)),
        ],
        out_shape=[
            jax.ShapeDtypeStruct((strips * STRIP, width), F32),
            jax.ShapeDtypeStruct(taps.shape, F32),
        ],
        scratch_shapes=[
            pltpu.VMEM((heads, STRIP, 2 * STRIP), F32),
            pltpu.VMEM((heads, STRIP, 2 * STRIP), F32),
            pltpu.VMEM((tokens + 4 * STRIP, width), BF16),
            pltpu.VMEM((tokens + 4 * STRIP, width), BF16),
        ],
        compiler_params=params(),
        cost_estimate=LIGHT,
        name="back_conv",
    )(col, *whole)
    return grad_values, tap_sums[:heads, front : front + CONV]


def occupancy_kernel(hashes, k_ref, w_ref, out_ref, counts):
    combos = 4
    lanes = hashes * combos
    side = combos * combos
    wide = hashes * side

    @pl.when(pl.program_id(1) == 0)
    def _():
        counts[...] = jnp.zeros_like(counts)

    source = lax.broadcasted_iota(jnp.int32, (lanes, wide), 0)
    target = lax.broadcasted_iota(jnp.int32, (lanes, wide), 1)
    same_hash = (source // combos) == (target // side)
    picks = []
    for divisor in (1, combos):
        chosen = same_hash & ((source % combos) == ((target // divisor) % combos))
        picks.append(chosen.astype(F32).astype(BF16))
    keys = k_ref[...]
    for index in range(2):
        signed = nn(keys, w_ref[index])
        halves = []
        for half in range(2):
            product = None
            for pick in range(2):
                start = (half * 2 + pick) * 2 * lanes
                one = 1.0 + jnp.exp(-signed[:, start : start + lanes])
                two = 1.0 + jnp.exp(-signed[:, start + lanes : start + 2 * lanes])
                spread = nn((1.0 / (one * two)).astype(BF16), picks[pick])
                product = spread if product is None else product * spread
            halves.append(product.astype(BF16))
        low, high = halves
        for start in range(0, wide, PAIR):
            block = slice(start, start + PAIR)
            counts[index, block, :] += tn(high[:, block], low[:, block])

    @pl.when(pl.program_id(1) == pl.num_programs(1) - 1)
    def _():
        row = lax.broadcasted_iota(jnp.int32, (wide, PAIR), 0)
        lane = lax.broadcasted_iota(jnp.int32, (wide, PAIR), 1)
        diagonal = ((row % PAIR) // side) == (lane // side)
        fold = [lax.broadcasted_iota(jnp.int32, (PAIR, side * side), d) for d in (0, 1)]
        fold = ((fold[0] % side) == (fold[1] % side)).astype(F32).astype(BF16)
        spot = [lax.broadcasted_iota(jnp.int32, (wide, side * side), d) for d in (0, 1)]
        kept = (spot[0] % side) == (spot[1] // side)
        home = [lax.broadcasted_iota(jnp.int32, (hashes, wide), d) for d in (0, 1)]
        home = (home[0] == home[1] // side).astype(F32).astype(BF16)
        for index in range(2):
            left = jnp.where(diagonal, counts[index], 0.0)
            total = None
            for _ in range(3):
                piece = left.astype(BF16)
                left = left - piece.astype(F32)
                spread = jnp.where(kept, nn(piece, fold), 0.0).astype(BF16)
                term = nn(home, spread)
                total = term if total is None else total + term
            out_ref[index] = total


def occupancy(key_unit, hyperplanes, scale):
    tokens, width = key_unit.shape
    hashes, bits, head_dim = hyperplanes.shape
    pairs = width // PAIR
    wide = hashes * 16
    planes = SHARP * hyperplanes.astype(F32)
    columns = []
    for group in range(bits // 2):
        for bit in range(2):
            signs = 2.0 * ((jnp.arange(4) // (2**bit)) % 2).astype(F32) - 1.0
            plane = planes[:, 2 * group + bit, :]
            columns.append((plane.T[:, :, None] * signs).reshape(head_dim, hashes * 4))
    weight = jnp.concatenate(columns, axis=1).astype(BF16)
    blank = jnp.zeros_like(weight)
    weights = jnp.stack(
        [jnp.concatenate([weight, blank], axis=0), jnp.concatenate([blank, weight], axis=0)]
    )
    counts = pl.pallas_call(
        partial(occupancy_kernel, hashes),
        grid=(pairs, tokens // CHUNK),
        in_specs=[
            pl.BlockSpec((CHUNK, PAIR), lambda p, t: (t, p)),
            pl.BlockSpec(weights.shape, lambda p, t: (0, 0, 0)),
        ],
        out_specs=pl.BlockSpec((2, hashes, 256), lambda p, t: (p, 0, 0)),
        out_shape=jax.ShapeDtypeStruct((2 * pairs, hashes, 256), F32),
        scratch_shapes=[pltpu.VMEM((2, wide, PAIR), F32)],
        compiler_params=params(),
        cost_estimate=pl.CostEstimate(
            flops=tokens * width * 32000, bytes_accessed=tokens * width * 4, transcendentals=0
        ),
        name="occupancy",
    )(key_unit, weights)
    return counts * scale


BELL_STEP = 0.3275911
BELL = (0.254829592, -0.284496736, 1.421413741, -1.453152027, 1.061405429)


def feed_kernel(x_ref, up_ref, down_ref, out_ref, active_ref, slope_ref):
    hidden = nn(x_ref[...], up_ref[...])
    size = jnp.abs(hidden)
    step = 1.0 / (1.0 + (BELL_STEP / math.sqrt(2.0)) * size)
    poly = BELL[4]
    for factor in BELL[3::-1]:
        poly = poly * step + factor
    bell = jnp.exp(-0.5 * (hidden * hidden))
    tail = (0.5 * step) * (poly * bell)
    phi = jnp.where(hidden < 0.0, tail, 1.0 - tail)
    active = (hidden * phi).astype(BF16)
    active_ref[...] = active
    slope_ref[...] = (phi + hidden * (bell * (1.0 / math.sqrt(2.0 * math.pi)))).astype(BF16)
    out_ref[...] = nn(active, down_ref[...]).astype(BF16)


def feed(x, up_weight, down_weight):
    tokens, depth = x.shape
    hidden = up_weight.shape[1]
    rows = 256
    wide = pl.BlockSpec((rows, hidden), lambda i: (i, 0))
    narrow = pl.BlockSpec((rows, depth), lambda i: (i, 0))
    return pl.pallas_call(
        feed_kernel,
        grid=(tokens // rows,),
        in_specs=[
            narrow,
            pl.BlockSpec(up_weight.shape, lambda i: (0, 0)),
            pl.BlockSpec(down_weight.shape, lambda i: (0, 0)),
        ],
        out_specs=[narrow, wide, wide],
        out_shape=[
            jax.ShapeDtypeStruct((tokens, depth), BF16),
            jax.ShapeDtypeStruct((tokens, hidden), BF16),
            jax.ShapeDtypeStruct((tokens, hidden), BF16),
        ],
        compiler_params=params(),
        cost_estimate=LIGHT,
        name="feed",
    )(x, up_weight, down_weight)


PLANE = 4


def sum_plan(n, rows):
    unit = 16 * n
    units = -(-rows // unit)
    first = -(-2 * units // 3)
    streams = [(0, first * unit, True)]
    if units > first:
        streams.append((first * unit, (units - first) * unit, False))
    return units * unit, streams


def sum_kernel(n, streams, split, *refs):
    count = len(streams)
    table_ref, misc_ref = refs[:2]
    outs, misc_out = refs[2 : 2 + split], refs[2 + split]
    scratch = refs[3 + split :]
    send, recv = scratch[-2:]
    me = lax.axis_index("seq")
    groups = n // PLANE
    near_me, far_me = lax.rem(me, PLANE), me // PLANE

    def device(plane_first, one, two):
        return {"seq": two * PLANE + one if plane_first else one * PLANE + two}

    barrier = pltpu.get_barrier_semaphore()
    for step in range(1, PLANE):
        pl.semaphore_signal(
            barrier, 1, device_id=device(True, lax.rem(near_me + step, PLANE), far_me)
        )
    for step in range(1, groups):
        pl.semaphore_signal(
            barrier, 1, device_id=device(True, near_me, lax.rem(far_me + step, groups))
        )
    pl.semaphore_wait(barrier, PLANE - 1 + groups - 1)

    facts = []
    for index, (base, rows, plane_first) in enumerate(streams):
        sizes = (PLANE, groups) if plane_first else (groups, PLANE)
        mine = (near_me, far_me) if plane_first else (far_me, near_me)
        buffers = scratch[5 * index : 5 * index + 5]
        source = misc_ref if index == count - 1 else table_ref
        block, chunk = rows // sizes[0], rows // n
        facts.append((index, source, base, plane_first, sizes, mine, block, chunk, buffers))

    def at(start, number):
        return pl.ds(pl.multiple_of(start, 8), number)

    def start_all(phase):
        started = []
        for index, source, base, plane_first, sizes, mine, block, chunk, buffers in facts:
            got_one, part, got_two, merged, full = buffers
            side = 0 if phase in (0, 3) else 1
            for step in range(1, sizes[side]):
                to = lax.rem(mine[side] + step, sizes[side])
                if phase == 0:
                    src, dst = source.at[at(base + to * block, block), :], got_one.at[step - 1]
                elif phase == 1:
                    src, dst = part.at[at(to * chunk, chunk), :], got_two.at[step - 1]
                elif phase == 2:
                    src = dst = merged.at[at(mine[1] * chunk, chunk), :]
                else:
                    src, dst = merged, full.at[at(mine[0] * block, block), :]
                pair = (to, mine[1]) if side == 0 else (mine[0], to)
                copy = pltpu.make_async_remote_copy(
                    src_ref=src,
                    dst_ref=dst,
                    send_sem=send.at[index, phase, step - 1],
                    recv_sem=recv.at[index, phase, step - 1],
                    device_id=device(plane_first, *pair),
                    device_id_type=pl.DeviceIdType.MESH,
                )
                copy.start()
                started.append(copy)
        return started

    def wait_all(started):
        for copy in started:
            copy.wait()

    wait_all(start_all(0))
    for index, source, base, plane_first, sizes, mine, block, chunk, buffers in facts:
        got_one, part, got_two, merged, full = buffers

        def add(piece, carry):
            rows = at(piece * chunk, chunk)
            total = source[at(base + mine[0] * block + piece * chunk, chunk), :].astype(F32)
            for step in range(sizes[0] - 1):
                total = total + got_one[step, rows, :].astype(F32)
            part[rows, :] = total.astype(part.dtype)
            return carry

        lax.fori_loop(0, sizes[1], add, 0)
    wait_all(start_all(1))
    for index, source, base, plane_first, sizes, mine, block, chunk, buffers in facts:
        got_one, part, got_two, merged, full = buffers
        rows = at(mine[1] * chunk, chunk)
        total = part[rows, :].astype(F32)
        for step in range(sizes[1] - 1):
            total = total + got_two[step].astype(F32)
        merged[rows, :] = total.astype(merged.dtype)
    wait_all(start_all(2))
    started = start_all(3)
    for index, source, base, plane_first, sizes, mine, block, chunk, buffers in facts:
        merged, full = buffers[3:]
        full[at(mine[0] * block, block), :] = merged[...]
    wait_all(started)
    for index, source, base, plane_first, sizes, mine, block, chunk, buffers in facts:
        full = buffers[4]

        def put(piece, carry):
            rows = at(piece * chunk, chunk)
            if index == count - 1:
                misc_out[rows, :] = full[rows, :]
            else:
                there = at(base + piece * chunk, chunk)
                for part_index, out in enumerate(outs):
                    width = out.shape[1]
                    lanes = slice(part_index * width, (part_index + 1) * width)
                    out[there, :] = full[rows, lanes].astype(F32)
            return carry

        lax.fori_loop(0, n, put, 0)


def sum_over_seq(table, misc, split):
    n = lax.axis_size("seq")
    rows, width = table.shape
    padded, streams = sum_plan(n, rows)
    if padded > rows:
        table = jnp.pad(table, ((0, padded - rows), (0, 0)))
    lanes = -(-misc.size // (8 * n * PAIR)) * PAIR
    misc_table = jnp.pad(misc, (0, 8 * n * lanes - misc.size)).reshape(8 * n, lanes)
    streams = streams + [(0, 8 * n, True)]
    scratch = []
    for index, (_, stream_rows, plane_first) in enumerate(streams):
        last = index == len(streams) - 1
        kind, lane_count = (F32, lanes) if last else (BF16, width)
        one, two = (PLANE, n // PLANE) if plane_first else (n // PLANE, PLANE)
        block, chunk = stream_rows // one, stream_rows // n
        scratch += [
            pltpu.VMEM((one - 1, block, lane_count), kind),
            pltpu.VMEM((block, lane_count), kind),
            pltpu.VMEM((two - 1, chunk, lane_count), kind),
            pltpu.VMEM((block, lane_count), kind),
            pltpu.VMEM((stream_rows, lane_count), kind),
        ]
    partners = max(PLANE, n // PLANE) - 1
    sems = pltpu.SemaphoreType.DMA((len(streams), 4, partners))
    in_vmem = pl.BlockSpec(memory_space=pltpu.VMEM)
    shapes = [jax.ShapeDtypeStruct((padded, width // split), F32)] * split
    *sums, misc_sum = pl.pallas_call(
        partial(sum_kernel, n, streams, split),
        in_specs=[in_vmem, in_vmem],
        out_specs=[in_vmem] * (split + 1),
        out_shape=shapes + [jax.ShapeDtypeStruct(misc_table.shape, F32)],
        scratch_shapes=scratch + [sems, sems],
        compiler_params=params(collective_id=0, has_side_effects=True),
        cost_estimate=pl.CostEstimate(flops=1 << 36, bytes_accessed=1 << 24, transcendentals=0),
        name="sum_over_seq",
    )(table, misc_table)
    return [total[:rows] for total in sums], misc_sum.reshape(-1)[: misc.size]


def plan_kernel(tokens, groups, length_ref, *refs):
    outs, end_ref = refs[:-1], refs[-1]
    docs = length_ref.shape[0]
    my_index, my_side = lax.axis_index("seq"), lax.axis_index("tp")
    all_tokens = tokens * lax.axis_size("seq")
    first = my_index * tokens
    half = tokens // CHUNK

    def add(doc, total):
        total = total + length_ref[doc]
        end_ref[doc] = total
        return total

    lax.fori_loop(0, docs, add, jnp.int32(0))

    q_count = tokens // Q_TILE_BACK
    spots = [first + i * Q_TILE_BACK for i in range(q_count)]
    spots += [spot + Q_TILE_BACK - 1 for spot in spots]
    starts = []
    for distances in groups:
        starts.append([first - d * tokens + h * CHUNK for d in distances for h in range(half)])
        spots += starts[-1] + [start + CHUNK - 1 for start in starts[-1]]

    def count_ends(doc, found):
        end = end_ref[doc]
        return [f + (end <= spot).astype(jnp.int32) for f, spot in zip(found, spots)]

    found = lax.fori_loop(0, docs, count_ends, [jnp.int32(0)] * len(spots))
    found = [
        jnp.where(spot < 0, -1, jnp.where(spot >= all_tokens, FAR_ID, f))
        for f, spot in zip(found, spots)
    ]
    q_low, q_high = found[:q_count], found[q_count : 2 * q_count]
    ratio = Q_TILE // Q_TILE_BACK
    at, rest = 2 * q_count, list(outs)
    for group in starts:
        number = len(group)
        low, high = found[at : at + number], found[at + number : at + 2 * number]
        at += 2 * number
        need = [
            ((h >= q_low[0]) & (l <= q_high[-1])).astype(jnp.int32) for l, h in zip(low, high)
        ]
        ends = [
            [*q_low[::ratio], *q_high[ratio - 1 :: ratio], *low, *high],
            [*q_low, *q_high, *low, *high],
        ]
        for values in ends:
            table = rest.pop(0)
            for i, value in enumerate(values):
                table[i] = value
            base, last, taken = len(values), jnp.int32(0), jnp.int32(0)
            for i in range(number):
                table[base + i] = jnp.int32(0)
            for i in range(number):
                spot = jnp.where(need[i] > 0, taken, number - 1)
                kept = table[base + spot]
                table[base + spot] = jnp.where(need[i] > 0, i, kept)
                last = jnp.where(need[i] > 0, i, last)
                taken = taken + need[i]
            for i in range(number):
                table[base + i] = jnp.where(i < taken, table[base + i], last)
            table[base + number] = taken
        chunk_table, fill_table = rest.pop(0), rest.pop(0)
        for i in range(number):
            block, side = i % (number // 2), i // (number // 2)
            place = 2 * block + jnp.where(my_side == 0, side, 1 - side)
            one, two = need[2 * block + side], need[2 * block + 1 - side]
            wanted = jnp.where(my_side == 0, one, two)
            chunk_table[i] = place
            chunk_table[number + i] = wanted
            chunk_table[2 * number + i] = place * wanted
            fill_table[i] = jnp.where(wanted > 0, place, number)
            fill_table[number + i] = wanted
        need_ref = rest.pop(0)
        for i in range(number):
            need_ref[i] = need[i]

    def ids_of(positions):
        def step(doc, total):
            return total + (end_ref[doc] <= positions).astype(jnp.int32)

        total = lax.fori_loop(0, docs, step, jnp.zeros_like(positions))
        total = jnp.where(positions < 0, -1, total)
        return jnp.where(positions >= all_tokens, FAR_ID, total)

    def rows_of(bases, lanes):
        row = lax.broadcasted_iota(jnp.int32, (len(bases), lanes), 0)
        positions = lax.broadcasted_iota(jnp.int32, (len(bases), lanes), 1)
        for i, base in enumerate(bases):
            positions = positions + jnp.where(row == i, base, 0)
        return ids_of(positions)

    for group in starts:
        rest.pop(0)[...] = rows_of(group, CHUNK)
    rest.pop(0)[...] = rows_of([first + i * Q_TILE for i in range(tokens // Q_TILE)], Q_TILE)
    strips = tokens // STRIP
    for extra in (0, 1):
        bases = [first + i * STRIP - STRIP // 2 for i in range(-extra, strips + extra)]
        rest.pop(0)[...] = rows_of(bases, 2 * STRIP)
    col_ref = rest.pop(0)

    def fill(strip, carry):
        row = lax.broadcasted_iota(jnp.int32, (STRIP, PAIR), 0)
        rows = pl.ds(pl.multiple_of(strip * STRIP, STRIP), STRIP)
        col_ref[rows, :] = ids_of(row + (first + (strip - 2) * STRIP))
        return carry

    lax.fori_loop(0, strips + 4, fill, 0)


def plan(lengths, tokens, groups):
    half = tokens // CHUNK
    q_tiles, q_back = tokens // Q_TILE, tokens // Q_TILE_BACK
    strips = tokens // STRIP
    sizes, rows = [], []
    for distances in groups:
        number = half * len(distances)
        sizes += [
            2 * q_tiles + 3 * number + 1,
            2 * q_back + 3 * number + 1,
            3 * number,
            2 * number,
            number,
        ]
        rows.append((number, CHUNK))
    rows += [(q_tiles, Q_TILE), (strips, 2 * STRIP), (strips + 2, 2 * STRIP)]
    rows.append(((strips + 4) * STRIP, PAIR))
    smem = pl.BlockSpec(memory_space=pltpu.SMEM)
    vmem = pl.BlockSpec(memory_space=pltpu.VMEM)
    shapes = [(size,) for size in sizes] + rows
    outs = pl.pallas_call(
        partial(plan_kernel, tokens, groups),
        in_specs=[smem],
        out_specs=[smem] * len(sizes) + [vmem] * len(rows),
        out_shape=[jax.ShapeDtypeStruct(shape, jnp.int32) for shape in shapes],
        scratch_shapes=[pltpu.SMEM(lengths.shape, jnp.int32)],
        compiler_params=params(),
        cost_estimate=LIGHT,
        name="plan",
    )(lengths)
    tables = [outs[5 * i : 5 * i + 5] for i in range(len(groups))]
    return [list(column) for column in zip(*tables)], outs[len(sizes) :]


def shifted(block, axis, distance):
    count = lax.axis_size(axis)
    route = [(i, i + distance) for i in range(count) if 0 <= i + distance < count]
    return lax.ppermute(block, axis, route)


def swapped(block, axis):
    return lax.ppermute(block, axis, [(0, 1), (1, 0)])


def tp_sum(partial_low):
    return partial_low.astype(F32) + swapped(partial_low, "tp").astype(F32)


def after(value, *others):
    return lax.optimization_barrier((value, *others))[0]


def layer_norm(vectors, gain_row, shift_row):
    center = vectors - jnp.mean(vectors, axis=-1, keepdims=True)
    spread = jnp.mean(center * center, axis=-1, keepdims=True)
    return center * lax.rsqrt(spread + EPS_LAYER) * gain_row + shift_row


def body(
    inputs,
    cotangent,
    query_weight,
    key_weight,
    value_weight,
    out_weight,
    up_weight,
    down_weight,
    conv_taps,
    attn_gain,
    attn_shift,
    ffn_gain,
    ffn_shift,
    hyperplanes,
    lengths,
):
    tokens, depth = inputs.shape
    head_dim = hyperplanes.shape[2]
    width = query_weight.shape[1]
    half = tokens // 2
    my_side = lax.axis_index("tp")
    all_tokens = tokens * lax.axis_size("seq")
    far_reach = (MOST + tokens - 2) // tokens
    close = far_reach // 2
    near = list(range(close, 0, -1)) + list(range(-1, -close - 1, -1))
    far = list(range(far_reach, close, -1)) + list(range(-close - 1, -far_reach - 1, -1))

    mine_rows = lax.dynamic_slice_in_dim(inputs, my_side * half, half, 0)
    near_mine = [shifted(mine_rows, "seq", d) for d in near]

    near_at, far_at, own_at = range(3)
    k_counts = [tokens // CHUNK * len(distances) for distances in (near, far, [0])]
    (tables, back_tables, chunk_tables, fill_tables, needs), id_rows = plan(
        lengths, tokens, (near, far, [0])
    )
    near_rows, far_rows, own_key_rows, own_rows, mix_row, back_row, ids_col = id_rows

    weight_qkv = jnp.concatenate([query_weight, key_weight, value_weight], axis=1)
    weight_kv = weight_qkv[:, width:]
    plain_table = jnp.array(list(range(tokens // CHUNK)) + [1] * (tokens // CHUNK), jnp.int32)
    query_unit, query_scale, key_unit, key_scale, values = project(
        plain_table, [inputs], weight_qkv, 2, head_dim
    )
    gathered, own_weights = attend(
        tables[own_at], query_unit, key_unit, values, own_rows, own_key_rows, head_dim
    )

    def other_half(mine):
        return jnp.concatenate([swapped(term, "tp") for term in mine], axis=0)

    *near_mine, late_rows = after((*near_mine, mine_rows), gathered)
    far_mine = [shifted(late_rows if i else mine_rows, "seq", d) for i, d in enumerate(far)]
    group_x, group_kv, group_weights = [], [], []
    for index, mine in ((near_at, near_mine), (far_at, far_mine)):
        if index == far_at:
            mine = after(tuple(mine), gathered)
        group_x.append([*mine, other_half(mine)])
        key_far, scale_far, value_far = project(
            fill_tables[index], group_x[index], weight_kv, 1, head_dim, k_counts[index]
        )
        group_kv.append((key_far, scale_far, value_far))
        gathered, weights = attend(
            tables[index],
            query_unit,
            key_far,
            value_far,
            own_rows,
            (near_rows, far_rows)[index],
            head_dim,
            seed=gathered,
        )
        group_weights.append(weights)
    edge = close * tokens
    sides = needs[near_at][edge // CHUNK - 1 : edge // CHUNK + 1]
    values_rim = jnp.where(
        jnp.repeat(sides, RIM)[:, None] > 0, group_kv[near_at][2][edge - RIM : edge + RIM], 0
    )
    mixed = mix(gathered, values, values_rim, mix_row, ids_col, conv_taps, head_dim)

    attn_out = tp_sum(nn(mixed, out_weight).astype(BF16))
    first_norm, first_back = jax.vjp(
        layer_norm, inputs.astype(F32) + attn_out, attn_gain, attn_shift
    )
    first_low = first_norm.astype(BF16)
    partial_out, active, slope = feed(first_low, up_weight, down_weight)
    ffn_out = tp_sum(partial_out)
    result, second_back = jax.vjp(layer_norm, first_norm + ffn_out, ffn_gain, ffn_shift)
    output = result.astype(BF16)
    grad_second, grad_ffn_gain, grad_ffn_shift = second_back(cotangent.astype(F32))
    grad_ffn = grad_second.astype(BF16)
    grad_hidden = (nt(grad_ffn, down_weight) * slope.astype(F32)).astype(BF16)
    grad_first = grad_second + tp_sum(nt(grad_hidden, up_weight).astype(BF16))
    grad_residual, grad_attn_gain, grad_attn_shift = first_back(grad_first)
    grad_attn = grad_residual.astype(BF16)
    grad_mixed = nt(grad_attn, out_weight).astype(BF16)

    grad_down = tn(active, grad_ffn).astype(BF16)
    grad_up = tn(first_low, grad_hidden).astype(BF16)
    grad_out = tn(mixed, grad_attn).astype(BF16)
    down_out = jnp.concatenate([grad_down, grad_out], axis=0)
    grad_up_low, down_out_low = grad_up, down_out
    grad_up, down_out = lax.psum((grad_up_low, down_out_low), "seq")

    grad_rows = back_norm(gathered, after(grad_mixed, grad_up_low, down_out_low), head_dim)

    def back_scores(index, grad_rows, seed):
        key_far, _, value_far = group_kv[index]
        return back_attend(
            back_tables[index],
            k_counts[index],
            query_unit,
            grad_rows,
            key_far,
            value_far,
            group_weights[index],
            head_dim,
            seed=seed,
        )

    def back_inputs(index, dk, dv, **rims):
        key_far, scale_far, _ = group_kv[index]
        parts = [(key_far, scale_far, dk)]
        return back_project(
            chunk_tables[index], group_x[index], weight_kv, parts, 0, [dv], head_dim, **rims
        )

    def both_sides(mine, came, first, number):
        rows = slice(first * half, (first + number) * half)
        return (mine[rows].astype(F32) + came[rows].astype(F32)).astype(BF16)

    dk, dv, turned = back_scores(far_at, grad_rows, None)
    far_dx, dx_other, far_dw = back_inputs(far_at, dk, dv)
    far_came = swapped(dx_other, "tp")
    grad_conv_values, grad_taps = back_conv(
        values, values_rim, after(grad_mixed, far_dx), back_row, ids_col, conv_taps, head_dim
    )
    rim = jnp.concatenate([grad_conv_values[:STRIP], grad_conv_values[-STRIP:]], axis=0)
    dk, dv, turned = back_scores(near_at, after(grad_rows, grad_conv_values), turned)
    near_dx, dx_other, near_dw = back_inputs(
        near_at, dk, dv, rims=close * (tokens // CHUNK) - 1, rim=rim
    )
    near_came = swapped(dx_other, "tp")
    occ_local = occupancy(after(key_unit, near_dx), hyperplanes, 2.0**BITS / all_tokens)
    far_came, near_came, grad_up, down_out = after(
        (far_came, near_came, grad_up, down_out), occ_local
    )
    count = lax.axis_size("seq")
    low_pair = both_sides(far_dx, far_came, 0, 2)
    high_pair = both_sides(far_dx, far_came, 2, 2)
    two_low, one_low, one_high, two_high = [
        both_sides(near_dx, near_came, i, 1) for i in range(len(near))
    ]
    low_far = shifted(low_pair, "seq", -far_reach)
    high_far = shifted(high_pair, "seq", far_reach)
    last = count - far_reach
    rest_home = lax.ppermute(
        jnp.where(lax.axis_index("seq") == last, high_pair[:half], low_pair[half:]),
        "seq",
        [(far_reach - 1, 0), (last, count - 1)],
    )
    two_homes = [shifted(two_low, "seq", -close), shifted(two_high, "seq", close)]
    dk, dv, turned = back_attend(
        back_tables[own_at],
        k_counts[own_at],
        query_unit,
        after(grad_rows, low_pair, high_pair, two_low, one_low, one_high, two_high),
        key_unit,
        values,
        own_weights,
        head_dim,
        seed=turned,
        cost=pl.CostEstimate(flops=1 << 35, bytes_accessed=1 << 20, transcendentals=0),
    )
    dk, low_far, high_far, rest_home, *two_homes = after(
        (dk, low_far, high_far, rest_home, *two_homes), dv
    )
    one_low = (one_low.astype(F32) + high_far[:half].astype(F32)).astype(BF16)
    one_high = (one_high.astype(F32) + low_far[half:].astype(F32)).astype(BF16)
    one_homes = [shifted(one_low, "seq", -1), shifted(one_high, "seq", 1)]
    dk = after(dk, one_low, one_high)
    own_mine = mine_rows
    own_other = lax.dynamic_slice_in_dim(inputs, (1 - my_side) * half, half, 0)
    dx_mine, dx_other, dw = back_project(
        chunk_tables[own_at],
        [own_mine, own_other],
        weight_qkv,
        [(query_unit, query_scale, turned), (key_unit, key_scale, dk)],
        1,
        [dv, grad_conv_values[STRIP:-STRIP]],
        head_dim,
    )

    homes = [low_far[:half], high_far[half:], rest_home, *two_homes]
    homes += after(tuple(one_homes), dw)
    qkv = jnp.concatenate([dw[:, :width], dw[:, width:] + near_dw + far_dw], axis=1).astype(BF16)
    misc = [
        occ_local,
        grad_taps,
        grad_attn_gain,
        grad_attn_shift,
        grad_ffn_gain,
        grad_ffn_shift,
    ]
    packed = jnp.concatenate([term.reshape(-1) for term in misc])
    qkv, packed = sum_over_seq(qkv, packed, 3)

    came = swapped(dx_other, "tp")
    total = (
        lax.dynamic_slice_in_dim(grad_residual, my_side * half, half, 0)
        + dx_mine.astype(F32)
        + came.astype(F32)
    )
    for home in homes:
        total = total + home.astype(F32)
    other_total = swapped(total, "tp")
    lower = jnp.where(my_side == 0, total, other_total)
    upper = jnp.where(my_side == 0, other_total, total)
    grad_inputs = jnp.concatenate([lower, upper], axis=0)

    unpacked, at = [], 0
    for term in misc:
        unpacked.append(packed[at : at + term.size].reshape(term.shape))
        at += term.size
    down_out = down_out.astype(F32)
    ff = down_weight.shape[0]
    return (
        output,
        grad_inputs,
        *qkv,
        down_out[ff:],
        grad_up.astype(F32),
        down_out[:ff],
        *unpacked[1:],
        unpacked[0],
    )


def solution(mesh):
    return jax.shard_map(
        body,
        mesh=mesh,
        in_specs=(
            P("seq", None),
            P("seq", None),
            P(None, "tp"),
            P(None, "tp"),
            P(None, "tp"),
            P("tp", None),
            P(None, "tp"),
            P("tp", None),
            P("tp", None),
            P(),
            P(),
            P(),
            P(),
            P(),
            P(),
        ),
        out_specs=(
            P("seq", None),
            P("seq", None),
            P(None, "tp"),
            P(None, "tp"),
            P(None, "tp"),
            P("tp", None),
            P(None, "tp"),
            P("tp", None),
            P("tp", None),
            P(),
            P(),
            P(),
            P(),
            P("tp", None, None),
        ),
        check_vma=False,
    )
```

```python
from functools import partial
import math

import jax
import jax.numpy as jnp
from jax import lax
from jax.experimental import pallas as pl
from jax.experimental.pallas import tpu as pltpu
from jax.sharding import PartitionSpec as P

TAU = 8
BITS = 8
CONV = 33
MOST = 4096
RIM = (CONV - 1) // 2

EPS_UNIT = 1e-06
EPS_LAYER = 1e-05
SHARP = 4.0
CLIP_EDGE = 0.999

CHUNK = 512
Q_TILE = 512
Q_TILE_BACK = 256
PAIR = 128
STRIP = 128
FAR_ID = 1 << 20

LIGHT = pl.CostEstimate(flops=1 << 20, bytes_accessed=1 << 16, transcendentals=0)

F32 = jnp.float32
BF16 = jnp.bfloat16

ARC = (
    0.49999961256980896,
    -0.06828052550554276,
    0.027964841574430466,
    -0.014291195198893547,
    0.006136968266218901,
    -0.001371906721033156,
)


def params(**kwargs):
    return pltpu.CompilerParams(vmem_limit_bytes=56 << 20, **kwargs)


def nn(left, right):
    return lax.dot_general(left, right, (((1,), (0,)), ((), ())), preferred_element_type=F32)


def nt(left, right):
    return lax.dot_general(left, right, (((1,), (1,)), ((), ())), preferred_element_type=F32)


def tn(left, right):
    return lax.dot_general(left, right, (((0,), (0,)), ((), ())), preferred_element_type=F32)


def head_masks(head_dim):
    lanes = lax.broadcasted_iota(jnp.int32, (1, PAIR), 1)
    first = (lanes < head_dim).astype(F32)
    return first.astype(BF16), (1.0 - first).astype(BF16)


def head_sum(rows, head_dim):
    here = lax.broadcasted_iota(jnp.int32, (PAIR, PAIR), 0) // head_dim
    there = lax.broadcasted_iota(jnp.int32, (PAIR, PAIR), 1) // head_dim
    ones = (here == there).astype(F32).astype(BF16)
    sums = []
    for start in range(0, rows.shape[1], PAIR):
        part = rows[:, start : start + PAIR]
        high = part.astype(BF16)
        low = (part - high.astype(F32)).astype(BF16)
        sums.append(nn(high, ones) + nn(low, ones))
    return jnp.concatenate(sums, axis=1)


def pick_half(mine_refs, other_ref, kept):
    step = pl.program_id(0)
    for index, ref in enumerate(mine_refs):

        @pl.when(step == index)
        def _():
            kept[...] = ref[...]

    @pl.when(step >= len(mine_refs))
    def _():
        kept[...] = other_ref[...]


def other_spec(count, shape):
    return pl.BlockSpec(shape, lambda i, t: (jnp.maximum(i - count, 0), 0))


def half_specs(count, shape):
    return [pl.BlockSpec(shape, lambda i, t: (0, 0))] * count + [other_spec(count, shape)]


def project_kernel(units, count, head_dim, table, *refs):
    if count:
        mine_refs, other_ref, w_ref = refs[:count], refs[count], refs[count + 1]
        out_refs, kept = refs[count + 2 : -1], refs[-1]
        pick_half(mine_refs, other_ref, kept)
    else:
        kept, w_ref = refs[:2]
        out_refs = refs[2:]
    width = out_refs[-1].shape[1]
    needed = table[pl.num_programs(0) + pl.program_id(0)] > 0

    @pl.when(needed)
    def _():
        whole = nn(kept[...], w_ref[...])
        for index in range(units):
            part = whole[:, index * width : (index + 1) * width]
            scale = lax.rsqrt(head_sum(part * part, head_dim) * (1.0 / head_dim) + EPS_UNIT)
            scale = scale * (1.0 / math.sqrt(head_dim))
            out_refs[2 * index][...] = (part * scale).astype(BF16)
            out_refs[2 * index + 1][...] = scale
        out_refs[-1][...] = whole[:, units * width :].astype(BF16)


def project(table, halves, weight, units, head_dim, chunks=None):
    depth = halves[0].shape[1]
    rows = sum(h.shape[0] for h in halves)
    count = len(halves) - 1
    width = weight.shape[1] // (units + 1)
    row_spec = pl.BlockSpec((CHUNK, width), lambda i, t: (t[i], 0))
    held = (chunks + 1) * CHUNK if count else rows
    if count:
        x_specs = half_specs(count, (CHUNK, depth))
    else:
        x_specs = [pl.BlockSpec((CHUNK, depth), lambda i, t: (i, 0))]
    unit_shapes = [
        jax.ShapeDtypeStruct((held, width), BF16),
        jax.ShapeDtypeStruct((held, width), F32),
    ]
    return pl.pallas_call(
        partial(project_kernel, units, count, head_dim),
        grid_spec=pltpu.PrefetchScalarGridSpec(
            num_scalar_prefetch=1,
            grid=(rows // CHUNK,),
            in_specs=x_specs + [pl.BlockSpec(weight.shape, lambda i, t: (0, 0))],
            out_specs=[row_spec] * (2 * units + 1),
            scratch_shapes=[pltpu.VMEM((CHUNK, depth), BF16)] if count else [],
        ),
        out_shape=unit_shapes * units + [jax.ShapeDtypeStruct((held, width), BF16)],
        compiler_params=params(),
        cost_estimate=pl.CostEstimate(
            flops=4 * rows * depth * weight.shape[1], bytes_accessed=rows * depth, transcendentals=0
        ),
        name="project",
    )(table, *halves, weight)


def collide(scores):
    size = jnp.minimum(jnp.abs(scores), CLIP_EDGE)
    rest = 1.0 - size
    poly = ARC[5]
    for factor in ARC[4::-1]:
        poly = poly * size + factor
    angle = (rest * lax.rsqrt(rest)) * poly
    return jnp.where(scores < 0.0, angle, 1.0 - angle)


def tile_facts(table, tiles_q, tiles_k, qi, kt):
    q_low, q_high = table[qi], table[tiles_q + qi]
    k_low, k_high = table[2 * tiles_q + kt], table[2 * tiles_q + tiles_k + kt]
    needed = (k_high >= q_low) & (k_low <= q_high)
    whole = (q_low == q_high) & (k_low == k_high)
    return needed, whole


def id_column(row, lanes):
    column = jnp.broadcast_to(row, (PAIR, row.shape[1])).T
    return jnp.concatenate([column] * (lanes // PAIR), axis=1)


def attend_kernel(
    head_dim, tiles_k, seeded, table, q_ref, qrow_ref, krow_ref, k_ref, v_ref, *rest
):
    out_ref, w_ref = rest[-2:]
    tiles_q = q_ref.shape[0] // Q_TILE
    step, steps = pl.program_id(1), pl.num_programs(1)
    order = 2 * (tiles_q + tiles_k)
    masks = head_masks(head_dim)

    @pl.when(step == 0)
    def _():
        if seeded:
            out_ref[...] = rest[0][...]
        else:
            out_ref[...] = jnp.zeros_like(out_ref)

    @pl.when(step < table[order + steps])
    def _():
        kt = table[order + step]

        def q_loop(qi, carry):
            rows = pl.ds(pl.multiple_of(qi * Q_TILE, Q_TILE), Q_TILE)
            needed, whole = tile_facts(table, tiles_q, tiles_k, qi, kt)

            def part(same):
                q, k = q_ref[rows, :], k_ref[...]
                v_turned = v_ref[...].T
                for index, mask in enumerate(masks):
                    chance = collide(nt(k, q * mask))
                    chance = chance * chance
                    chance = chance * chance
                    chance = chance * chance
                    if same is not None:
                        chance = jnp.where(same, chance, 0.0)
                    weights = chance.astype(BF16)
                    w_ref[index, :, rows] = weights
                    half = slice(index * head_dim, (index + 1) * head_dim)
                    out_ref[half, rows] += nn(v_turned[half, :], weights)

            @pl.when(needed & whole)
            def _():
                part(None)

            @pl.when(needed & jnp.logical_not(whole))
            def _():
                part(id_column(krow_ref[pl.ds(kt, 1), :], Q_TILE) == qrow_ref[pl.ds(qi, 1), :])

            @pl.when(jnp.logical_not(needed))
            def _():
                w_ref[:, :, rows] = jnp.zeros((2, CHUNK, Q_TILE), BF16)

            return carry

        lax.fori_loop(0, tiles_q, q_loop, 0)


def attend(table, q, k, v, qrow, krow, head_dim, seed=None):
    tokens, width = q.shape
    tiles_k = krow.shape[0]
    order = 2 * (tokens // Q_TILE + tiles_k)
    k_spec = pl.BlockSpec((CHUNK, PAIR), lambda p, j, t: (t[order + j], p))
    turned_spec = pl.BlockSpec((PAIR, tokens), lambda p, j, t: (p, 0))
    operands = [q, qrow, krow, k, v]
    specs = [
        pl.BlockSpec((tokens, PAIR), lambda p, j, t: (0, p)),
        pl.BlockSpec(qrow.shape, lambda p, j, t: (0, 0)),
        pl.BlockSpec(krow.shape, lambda p, j, t: (0, 0)),
        k_spec,
        k_spec,
    ]
    if seed is not None:
        operands.append(seed)
        specs.append(turned_spec)
    return pl.pallas_call(
        partial(attend_kernel, head_dim, tiles_k, seed is not None),
        grid_spec=pltpu.PrefetchScalarGridSpec(
            num_scalar_prefetch=1,
            grid=(width // PAIR, tiles_k),
            in_specs=specs,
            out_specs=[
                turned_spec,
                pl.BlockSpec((2, CHUNK, tokens), lambda p, j, t: (p, t[order + j], 0)),
            ],
        ),
        out_shape=[
            jax.ShapeDtypeStruct((width, tokens), F32),
            jax.ShapeDtypeStruct((width // head_dim, tiles_k * CHUNK, tokens), BF16),
        ],
        compiler_params=params(),
        cost_estimate=pl.CostEstimate(
            flops=32 * tokens * tiles_k * CHUNK * width,
            bytes_accessed=tokens * width * 4,
            transcendentals=0,
        ),
        name="attend",
    )(table, *operands)


def back_attend_kernel(
    head_dim, tiles_k, seeded, table, q_ref, g_ref, k_ref, v_ref, w_ref, *rest
):
    dk_ref, dv_ref, dq_ref, acc_k, acc_v = rest[-5:]
    tiles_q = q_ref.shape[0] // Q_TILE_BACK
    step, steps = pl.program_id(1), pl.num_programs(1)
    order = 2 * (tiles_q + tiles_k)
    masks = head_masks(head_dim)

    @pl.when(step == 0)
    def _():
        if seeded:
            dq_ref[...] = rest[0][...]
        else:
            dq_ref[...] = jnp.zeros_like(dq_ref)

    @pl.when(step < table[order + steps])
    def _():
        kt = table[order + step]
        acc_k[...] = jnp.zeros_like(acc_k)
        acc_v[...] = jnp.zeros_like(acc_v)

        def q_loop(qi, carry):
            needed, _ = tile_facts(table, tiles_q, tiles_k, qi, kt)

            @pl.when(needed)
            def _():
                rows = pl.ds(pl.multiple_of(qi * Q_TILE_BACK, Q_TILE_BACK), Q_TILE_BACK)
                q, g, k, v = q_ref[rows, :], g_ref[rows, :], k_ref[...], v_ref[...]
                k_turned = k.T
                sum_k, sum_v = None, None
                for index, mask in enumerate(masks):
                    q_half, g_half = q * mask, g * mask
                    scores = nt(k, q_half)
                    weights = w_ref[index, :, rows]
                    power = jnp.exp(((TAU - 1) / TAU) * jnp.log(weights.astype(F32)))
                    square = scores * scores
                    slope = nt(v, g_half) * (power * lax.rsqrt(1.0 - square))
                    slope = jnp.where(square <= CLIP_EDGE * CLIP_EDGE, slope, 0.0).astype(BF16)
                    term_v = nn(weights, g_half)
                    term_k = nn(slope, q_half)
                    sum_v = term_v if sum_v is None else sum_v + term_v
                    sum_k = term_k if sum_k is None else sum_k + term_k
                    half = slice(index * head_dim, (index + 1) * head_dim)
                    dq_ref[half, rows] += nn(k_turned[half, :], slope)
                acc_v[...] += sum_v
                acc_k[...] += sum_k

            return carry

        lax.fori_loop(0, tiles_q, q_loop, 0)
        dk_ref[...] = acc_k[...].astype(BF16)
        dv_ref[...] = acc_v[...].astype(BF16)


def back_attend(table, tiles_k, q, g, k, v, weights, head_dim, seed=None, cost=LIGHT):
    tokens, width = q.shape
    order = 2 * (tokens // Q_TILE_BACK + tiles_k)
    q_spec = pl.BlockSpec((tokens, PAIR), lambda p, j, t: (0, p))
    k_spec = pl.BlockSpec((CHUNK, PAIR), lambda p, j, t: (t[order + j], p))
    dq_spec = pl.BlockSpec((PAIR, tokens), lambda p, j, t: (p, 0))
    specs = [
        q_spec,
        q_spec,
        k_spec,
        k_spec,
        pl.BlockSpec((2, CHUNK, tokens), lambda p, j, t: (p, t[order + j], 0)),
    ]
    operands = [q, g, k, v, weights]
    if seed is not None:
        operands.append(seed)
        specs.append(dq_spec)
    return pl.pallas_call(
        partial(back_attend_kernel, head_dim, tiles_k, seed is not None),
        grid_spec=pltpu.PrefetchScalarGridSpec(
            num_scalar_prefetch=1,
            grid=(width // PAIR, tiles_k),
            in_specs=specs,
            out_specs=[k_spec, k_spec, dq_spec],
            scratch_shapes=[pltpu.VMEM((CHUNK, PAIR), F32), pltpu.VMEM((CHUNK, PAIR), F32)],
        ),
        out_shape=[
            jax.ShapeDtypeStruct((tiles_k * CHUNK, width), BF16),
            jax.ShapeDtypeStruct((tiles_k * CHUNK, width), BF16),
            jax.ShapeDtypeStruct((width, tokens), F32),
        ],
        compiler_params=params(),
        cost_estimate=cost,
        name="back_attend",
    )(table, *operands)


def back_project_kernel(units, turned, terms, rims, count, head_dim, table, *refs):
    mine_refs, other_ref, w_ref = refs[:count], refs[count], refs[count + 1]
    dx_mine, dx_other, dw_ref, kept, sum_ref = refs[-5:]
    refs = refs[count + 2 : -5]
    step = pl.program_id(0)
    place, needed = table[step], table[pl.num_programs(0) + step] > 0

    @pl.when(step == 0)
    def _():
        dw_ref[...] = jnp.zeros_like(dw_ref)

    def store(value):
        @pl.when(step < count)
        def _():
            dx_mine[...] = value

        @pl.when(step >= count)
        def _():
            dx_other[...] = value

    @pl.when(needed)
    def _():
        pick_half(mine_refs, other_ref, kept)
        grads = []
        for index in range(units):
            unit_ref, scale_ref, grad_ref = refs[3 * index : 3 * index + 3]
            grad = grad_ref[...].astype(F32)
            if index < turned:
                grad = grad.T
            unit = unit_ref[...].astype(F32)
            inner = head_sum(grad * unit, head_dim)
            grads.append(
                ((TAU / math.pi) * scale_ref[...] * (grad - unit * inner)).astype(BF16)
            )
        value_refs = refs[3 * units : 3 * units + terms]
        value = value_refs[0][...].astype(F32)
        for extra in value_refs[1:]:
            value = value + extra[...].astype(F32)
        if rims is not None:
            rim_ref = refs[-1]
            sum_ref[...] = value

            @pl.when(place == rims)
            def _():
                sum_ref[CHUNK - STRIP :, :] += rim_ref[:STRIP, :]

            @pl.when(place == rims + 1)
            def _():
                sum_ref[:STRIP, :] += rim_ref[STRIP:, :]

            value = sum_ref[...]
        grads.append(value.astype(BF16))
        joined = jnp.concatenate(grads, axis=1)
        store(nt(joined, w_ref[...]).astype(BF16))
        dw_ref[...] += tn(kept[...], joined)

    @pl.when(jnp.logical_not(needed))
    def _():
        store(jnp.zeros(dx_mine.shape, BF16))


def back_project(table, halves, weight, parts, turned, values, head_dim, rims=None, rim=None):
    depth = halves[0].shape[1]
    count = len(halves) - 1
    width = values[0].shape[1]
    row_spec = pl.BlockSpec((CHUNK, width), lambda i, t: (t[4 * count + i], 0))
    weight_spec = pl.BlockSpec(weight.shape, lambda i, t: (0, 0))
    wide_specs = [
        pl.BlockSpec((CHUNK, depth), lambda i, t: (jnp.minimum(i, count - 1), 0)),
        other_spec(count, (CHUNK, depth)),
    ]
    specs = half_specs(count, (CHUNK, depth)) + [weight_spec]
    operands = [*halves, weight]
    for index, (unit, scale, grad) in enumerate(parts):
        operands += [unit, scale, grad]
        specs += [row_spec, row_spec]
        specs.append(
            pl.BlockSpec((width, CHUNK), lambda i, t: (0, t[4 * count + i]))
            if index < turned
            else row_spec
        )
    operands += values
    specs += [row_spec] * len(values)
    if rim is not None:
        operands.append(rim)
        specs.append(pl.BlockSpec(rim.shape, lambda i, t: (0, 0)))
    return pl.pallas_call(
        partial(back_project_kernel, len(parts), turned, len(values), rims, count, head_dim),
        grid_spec=pltpu.PrefetchScalarGridSpec(
            num_scalar_prefetch=1,
            grid=(2 * count,),
            in_specs=specs,
            out_specs=wide_specs + [weight_spec],
            scratch_shapes=[pltpu.VMEM((CHUNK, depth), BF16), pltpu.VMEM((CHUNK, width), F32)],
        ),
        out_shape=[
            jax.ShapeDtypeStruct((count * CHUNK, depth), BF16),
            jax.ShapeDtypeStruct((count * CHUNK, depth), BF16),
            jax.ShapeDtypeStruct(weight.shape, F32),
        ],
        compiler_params=params(),
        cost_estimate=LIGHT,
        name="back_project",
    )(table, *operands)


def lane_taps(conv_taps, mirrored):
    front = STRIP // 2 - RIM
    heads = conv_taps.shape[0]
    taps = conv_taps[:, ::-1] if mirrored else conv_taps
    return jnp.pad(taps, ((0, -heads % 8), (front, 2 * STRIP - front - CONV)))


def fill_bands(taps_ref, bands, heads):
    for head in range(heads):
        row = jnp.broadcast_to(taps_ref[head : head + 1, :], (STRIP, 2 * STRIP))
        bands[head] = pltpu.roll(row, 0, 1, stride=1, stride_axis=0)


def band_product(band, same, window):
    band = jnp.where(same, band, 0.0)
    high = band.astype(BF16)
    low = (band - high.astype(F32)).astype(BF16)
    return nn(high, window) + nn(low, window)


def fill_extended(kept, edge, centre_ref, rim_ref):
    rows = centre_ref.shape[0]
    kept[...] = jnp.zeros_like(kept)
    kept[edge : edge + rows, :] = centre_ref[...]
    if rim_ref is not None:
        kept[edge - RIM : edge, :] = rim_ref[:RIM, :]
        kept[edge + rows : edge + rows + RIM, :] = rim_ref[RIM:, :]


def mix_kernel(head_dim, g_ref, col_ref, v_ref, rim_ref, row_ref, taps_ref, out_ref, bands, kept):
    heads = g_ref.shape[0] // head_dim
    step = pl.program_id(0)

    @pl.when(step == 0)
    def _():
        fill_bands(taps_ref, bands, heads)
        fill_extended(kept, STRIP, v_ref, rim_ref)

    masks = head_masks(head_dim)
    window = kept[pl.ds(pl.multiple_of(step * STRIP + STRIP // 2, STRIP // 2), 2 * STRIP), :]
    ids = col_ref[...]
    same = jnp.concatenate([ids, ids], axis=1) == row_ref[pl.ds(step, 1), :]
    pieces = []
    for pair in range(heads // 2):
        values = window[:, pair * PAIR : (pair + 1) * PAIR]
        total = None
        for index, mask in enumerate(masks):
            term = band_product(bands[2 * pair + index], same, values * mask)
            total = term if total is None else total + term
        pieces.append(total)
    gathered = g_ref[...].T
    scale = lax.rsqrt(head_sum(gathered * gathered, head_dim) * (1.0 / head_dim) + EPS_UNIT)
    out_ref[...] = (gathered * scale + jnp.concatenate(pieces, axis=1)).astype(BF16)


def mix(gathered, values, rim, row, col, conv_taps, head_dim):
    width, tokens = gathered.shape
    heads = width // head_dim
    strips = tokens // STRIP
    taps = lane_taps(conv_taps, False)
    row_spec = pl.BlockSpec((STRIP, width), lambda i: (i, 0))
    whole = [values, rim, row, taps]
    return pl.pallas_call(
        partial(mix_kernel, head_dim),
        grid=(strips,),
        in_specs=[
            pl.BlockSpec((width, STRIP), lambda i: (0, i)),
            pl.BlockSpec((STRIP, PAIR), lambda i: (i + 2, 0)),
        ]
        + [pl.BlockSpec(a.shape, lambda i: (0, 0)) for a in whole],
        out_specs=row_spec,
        out_shape=jax.ShapeDtypeStruct((tokens, width), BF16),
        scratch_shapes=[
            pltpu.VMEM((heads, STRIP, 2 * STRIP), F32),
            pltpu.VMEM((tokens + 2 * STRIP, width), BF16),
        ],
        compiler_params=params(),
        cost_estimate=LIGHT,
        name="mix",
    )(gathered, col, *whole)


def back_norm_kernel(head_dim, g_ref, m_ref, out_ref):
    gathered, grad = g_ref[...].T, m_ref[...].astype(F32)
    scale = lax.rsqrt(head_sum(gathered * gathered, head_dim) * (1.0 / head_dim) + EPS_UNIT)
    mean = head_sum(grad * gathered, head_dim) * (1.0 / head_dim)
    out_ref[...] = (scale * (grad - (scale * scale) * gathered * mean)).astype(BF16)


def back_norm(gathered, grad_mixed, head_dim):
    width, tokens = gathered.shape
    row_spec = pl.BlockSpec((CHUNK, width), lambda i: (i, 0))
    return pl.pallas_call(
        partial(back_norm_kernel, head_dim),
        grid=(tokens // CHUNK,),
        in_specs=[pl.BlockSpec((width, CHUNK), lambda i: (0, i)), row_spec],
        out_specs=row_spec,
        out_shape=jax.ShapeDtypeStruct((tokens, width), BF16),
        compiler_params=params(),
        cost_estimate=LIGHT,
        name="back_norm",
    )(gathered, grad_mixed)


def back_conv_kernel(
    head_dim, col_ref, v_ref, rim_ref, m_ref, row_ref, taps_ref, dv_ref, tap_ref, bands, sums, kept_v, kept_m
):
    heads = dv_ref.shape[1] // head_dim
    step, steps = pl.program_id(0), pl.num_programs(0)

    @pl.when(step == 0)
    def _():
        fill_bands(taps_ref, bands, heads)
        fill_extended(kept_v, 2 * STRIP, v_ref, rim_ref)
        fill_extended(kept_m, 2 * STRIP, m_ref, None)
        sums[...] = jnp.zeros_like(sums)

    masks = head_masks(head_dim)
    around = pl.ds(pl.multiple_of(step * STRIP + STRIP // 2, STRIP // 2), 2 * STRIP)
    centre = pl.ds(pl.multiple_of(step * STRIP + STRIP, STRIP), STRIP)
    ids = col_ref[...]
    same = jnp.concatenate([ids, ids], axis=1) == row_ref[pl.ds(step, 1), :]
    pieces = []
    for pair in range(heads // 2):
        cols = slice(pair * PAIR, (pair + 1) * PAIR)
        grads, values, here = kept_m[around, cols], kept_v[around, cols], kept_m[centre, cols]
        total = None
        for index, mask in enumerate(masks):
            head = 2 * pair + index
            term = band_product(bands[head], same, grads * mask)
            total = term if total is None else total + term
            sums[head] += jnp.where(same, nt(here * mask, values), 0.0)
        pieces.append(total)
    dv_ref[...] = jnp.concatenate(pieces, axis=1)

    @pl.when(step == steps - 1)
    def _():
        tap_ref[...] = jnp.zeros_like(tap_ref)
        places = [lax.broadcasted_iota(jnp.int32, (STRIP, STRIP), d) for d in (0, 1)]
        flip = (places[0] + places[1] == STRIP - 1).astype(F32).astype(BF16)
        for head in range(heads):
            total = sums[head]
            high = total.astype(BF16)
            low = (total - high.astype(F32)).astype(BF16)
            turned = pltpu.roll(
                nn(flip, high) + nn(flip, low), STRIP + 1, 1, stride=1, stride_axis=0
            )
            tap_ref[head : head + 1, :] = jnp.sum(turned, axis=0, keepdims=True)


def back_conv(values, rim, grad_mixed, row, col, conv_taps, head_dim):
    tokens, width = values.shape
    heads = width // head_dim
    strips = tokens // STRIP + 2
    taps = lane_taps(conv_taps, True)
    front = STRIP // 2 - RIM
    whole = [values, rim, grad_mixed, row, taps]
    grad_values, tap_sums = pl.pallas_call(
        partial(back_conv_kernel, head_dim),
        grid=(strips,),
        in_specs=[pl.BlockSpec((STRIP, PAIR), lambda i: (i + 1, 0))]
        + [pl.BlockSpec(a.shape, lambda i: (0, 0)) for a in whole],
        out_specs=[
            pl.BlockSpec((STRIP, width), lambda i: (i, 0)),
            pl.BlockSpec(taps.shape, lambda i: (0, 0)),
        ],
        out_shape=[
            jax.ShapeDtypeStruct((strips * STRIP, width), F32),
            jax.ShapeDtypeStruct(taps.shape, F32),
        ],
        scratch_shapes=[
            pltpu.VMEM((heads, STRIP, 2 * STRIP), F32),
            pltpu.VMEM((heads, STRIP, 2 * STRIP), F32),
            pltpu.VMEM((tokens + 4 * STRIP, width), BF16),
            pltpu.VMEM((tokens + 4 * STRIP, width), BF16),
        ],
        compiler_params=params(),
        cost_estimate=LIGHT,
        name="back_conv",
    )(col, *whole)
    return grad_values, tap_sums[:heads, front : front + CONV]


def occupancy_kernel(hashes, k_ref, w_ref, out_ref, counts):
    combos = 4
    lanes = hashes * combos
    side = combos * combos
    wide = hashes * side

    @pl.when(pl.program_id(1) == 0)
    def _():
        counts[...] = jnp.zeros_like(counts)

    source = lax.broadcasted_iota(jnp.int32, (lanes, wide), 0)
    target = lax.broadcasted_iota(jnp.int32, (lanes, wide), 1)
    same_hash = (source // combos) == (target // side)
    picks = []
    for divisor in (1, combos):
        chosen = same_hash & ((source % combos) == ((target // divisor) % combos))
        picks.append(chosen.astype(F32).astype(BF16))
    keys = k_ref[...]
    for index in range(2):
        signed = nn(keys, w_ref[index])
        halves = []
        for half in range(2):
            product = None
            for pick in range(2):
                start = (half * 2 + pick) * 2 * lanes
                one = 1.0 + jnp.exp(-signed[:, start : start + lanes])
                two = 1.0 + jnp.exp(-signed[:, start + lanes : start + 2 * lanes])
                spread = nn((1.0 / (one * two)).astype(BF16), picks[pick])
                product = spread if product is None else product * spread
            halves.append(product.astype(BF16))
        low, high = halves
        for start in range(0, wide, PAIR):
            block = slice(start, start + PAIR)
            counts[index, block, :] += tn(high[:, block], low[:, block])

    @pl.when(pl.program_id(1) == pl.num_programs(1) - 1)
    def _():
        row = lax.broadcasted_iota(jnp.int32, (wide, PAIR), 0)
        lane = lax.broadcasted_iota(jnp.int32, (wide, PAIR), 1)
        diagonal = ((row % PAIR) // side) == (lane // side)
        fold = [lax.broadcasted_iota(jnp.int32, (PAIR, side * side), d) for d in (0, 1)]
        fold = ((fold[0] % side) == (fold[1] % side)).astype(F32).astype(BF16)
        spot = [lax.broadcasted_iota(jnp.int32, (wide, side * side), d) for d in (0, 1)]
        kept = (spot[0] % side) == (spot[1] // side)
        home = [lax.broadcasted_iota(jnp.int32, (hashes, wide), d) for d in (0, 1)]
        home = (home[0] == home[1] // side).astype(F32).astype(BF16)
        for index in range(2):
            left = jnp.where(diagonal, counts[index], 0.0)
            total = None
            for _ in range(3):
                piece = left.astype(BF16)
                left = left - piece.astype(F32)
                spread = jnp.where(kept, nn(piece, fold), 0.0).astype(BF16)
                term = nn(home, spread)
                total = term if total is None else total + term
            out_ref[index] = total


def occupancy(key_unit, hyperplanes, scale):
    tokens, width = key_unit.shape
    hashes, bits, head_dim = hyperplanes.shape
    pairs = width // PAIR
    wide = hashes * 16
    planes = SHARP * hyperplanes.astype(F32)
    columns = []
    for group in range(bits // 2):
        for bit in range(2):
            signs = 2.0 * ((jnp.arange(4) // (2**bit)) % 2).astype(F32) - 1.0
            plane = planes[:, 2 * group + bit, :]
            columns.append((plane.T[:, :, None] * signs).reshape(head_dim, hashes * 4))
    weight = jnp.concatenate(columns, axis=1).astype(BF16)
    blank = jnp.zeros_like(weight)
    weights = jnp.stack(
        [jnp.concatenate([weight, blank], axis=0), jnp.concatenate([blank, weight], axis=0)]
    )
    counts = pl.pallas_call(
        partial(occupancy_kernel, hashes),
        grid=(pairs, tokens // CHUNK),
        in_specs=[
            pl.BlockSpec((CHUNK, PAIR), lambda p, t: (t, p)),
            pl.BlockSpec(weights.shape, lambda p, t: (0, 0, 0)),
        ],
        out_specs=pl.BlockSpec((2, hashes, 256), lambda p, t: (p, 0, 0)),
        out_shape=jax.ShapeDtypeStruct((2 * pairs, hashes, 256), F32),
        scratch_shapes=[pltpu.VMEM((2, wide, PAIR), F32)],
        compiler_params=params(),
        cost_estimate=pl.CostEstimate(
            flops=tokens * width * 32000, bytes_accessed=tokens * width * 4, transcendentals=0
        ),
        name="occupancy",
    )(key_unit, weights)
    return counts * scale


BELL_STEP = 0.3275911
BELL = (0.254829592, -0.284496736, 1.421413741, -1.453152027, 1.061405429)


def feed_kernel(x_ref, up_ref, down_ref, out_ref, active_ref, slope_ref):
    hidden = nn(x_ref[...], up_ref[...])
    size = jnp.abs(hidden)
    step = 1.0 / (1.0 + (BELL_STEP / math.sqrt(2.0)) * size)
    poly = BELL[4]
    for factor in BELL[3::-1]:
        poly = poly * step + factor
    bell = jnp.exp(-0.5 * (hidden * hidden))
    tail = (0.5 * step) * (poly * bell)
    phi = jnp.where(hidden < 0.0, tail, 1.0 - tail)
    active = (hidden * phi).astype(BF16)
    active_ref[...] = active
    slope_ref[...] = (phi + hidden * (bell * (1.0 / math.sqrt(2.0 * math.pi)))).astype(BF16)
    out_ref[...] = nn(active, down_ref[...]).astype(BF16)


def feed(x, up_weight, down_weight):
    tokens, depth = x.shape
    hidden = up_weight.shape[1]
    rows = 256
    wide = pl.BlockSpec((rows, hidden), lambda i: (i, 0))
    narrow = pl.BlockSpec((rows, depth), lambda i: (i, 0))
    return pl.pallas_call(
        feed_kernel,
        grid=(tokens // rows,),
        in_specs=[
            narrow,
            pl.BlockSpec(up_weight.shape, lambda i: (0, 0)),
            pl.BlockSpec(down_weight.shape, lambda i: (0, 0)),
        ],
        out_specs=[narrow, wide, wide],
        out_shape=[
            jax.ShapeDtypeStruct((tokens, depth), BF16),
            jax.ShapeDtypeStruct((tokens, hidden), BF16),
            jax.ShapeDtypeStruct((tokens, hidden), BF16),
        ],
        compiler_params=params(),
        cost_estimate=LIGHT,
        name="feed",
    )(x, up_weight, down_weight)


PLANE = 4


def sum_plan(n, rows):
    unit = 16 * n
    units = -(-rows // unit)
    first = -(-2 * units // 3)
    streams = [(0, first * unit, True)]
    if units > first:
        streams.append((first * unit, (units - first) * unit, False))
    return units * unit, streams


def sum_kernel(n, streams, split, *refs):
    count = len(streams)
    table_ref, misc_ref = refs[:2]
    outs, misc_out = refs[2 : 2 + split], refs[2 + split]
    scratch = refs[3 + split :]
    send, recv = scratch[-2:]
    me = lax.axis_index("seq")
    groups = n // PLANE
    near_me, far_me = lax.rem(me, PLANE), me // PLANE

    def device(plane_first, one, two):
        return {"seq": two * PLANE + one if plane_first else one * PLANE + two}

    barrier = pltpu.get_barrier_semaphore()
    for step in range(1, PLANE):
        pl.semaphore_signal(
            barrier, 1, device_id=device(True, lax.rem(near_me + step, PLANE), far_me)
        )
    for step in range(1, groups):
        pl.semaphore_signal(
            barrier, 1, device_id=device(True, near_me, lax.rem(far_me + step, groups))
        )
    pl.semaphore_wait(barrier, PLANE - 1 + groups - 1)

    facts = []
    for index, (base, rows, plane_first) in enumerate(streams):
        sizes = (PLANE, groups) if plane_first else (groups, PLANE)
        mine = (near_me, far_me) if plane_first else (far_me, near_me)
        buffers = scratch[5 * index : 5 * index + 5]
        source = misc_ref if index == count - 1 else table_ref
        block, chunk = rows // sizes[0], rows // n
        facts.append((index, source, base, plane_first, sizes, mine, block, chunk, buffers))

    def at(start, number):
        return pl.ds(pl.multiple_of(start, 8), number)

    def start_all(phase):
        started = []
        for index, source, base, plane_first, sizes, mine, block, chunk, buffers in facts:
            got_one, part, got_two, merged, full = buffers
            side = 0 if phase in (0, 3) else 1
            for step in range(1, sizes[side]):
                to = lax.rem(mine[side] + step, sizes[side])
                if phase == 0:
                    src, dst = source.at[at(base + to * block, block), :], got_one.at[step - 1]
                elif phase == 1:
                    src, dst = part.at[at(to * chunk, chunk), :], got_two.at[step - 1]
                elif phase == 2:
                    src = dst = merged.at[at(mine[1] * chunk, chunk), :]
                else:
                    src, dst = merged, full.at[at(mine[0] * block, block), :]
                pair = (to, mine[1]) if side == 0 else (mine[0], to)
                copy = pltpu.make_async_remote_copy(
                    src_ref=src,
                    dst_ref=dst,
                    send_sem=send.at[index, phase, step - 1],
                    recv_sem=recv.at[index, phase, step - 1],
                    device_id=device(plane_first, *pair),
                    device_id_type=pl.DeviceIdType.MESH,
                )
                copy.start()
                started.append(copy)
        return started

    def wait_all(started):
        for copy in started:
            copy.wait()

    wait_all(start_all(0))
    for index, source, base, plane_first, sizes, mine, block, chunk, buffers in facts:
        got_one, part, got_two, merged, full = buffers

        def add(piece, carry):
            rows = at(piece * chunk, chunk)
            total = source[at(base + mine[0] * block + piece * chunk, chunk), :].astype(F32)
            for step in range(sizes[0] - 1):
                total = total + got_one[step, rows, :].astype(F32)
            part[rows, :] = total.astype(part.dtype)
            return carry

        lax.fori_loop(0, sizes[1], add, 0)
    wait_all(start_all(1))
    for index, source, base, plane_first, sizes, mine, block, chunk, buffers in facts:
        got_one, part, got_two, merged, full = buffers
        rows = at(mine[1] * chunk, chunk)
        total = part[rows, :].astype(F32)
        for step in range(sizes[1] - 1):
            total = total + got_two[step].astype(F32)
        merged[rows, :] = total.astype(merged.dtype)
    wait_all(start_all(2))
    started = start_all(3)
    for index, source, base, plane_first, sizes, mine, block, chunk, buffers in facts:
        merged, full = buffers[3:]
        full[at(mine[0] * block, block), :] = merged[...]
    wait_all(started)
    for index, source, base, plane_first, sizes, mine, block, chunk, buffers in facts:
        full = buffers[4]

        def put(piece, carry):
            rows = at(piece * chunk, chunk)
            if index == count - 1:
                misc_out[rows, :] = full[rows, :]
            else:
                there = at(base + piece * chunk, chunk)
                for part_index, out in enumerate(outs):
                    width = out.shape[1]
                    lanes = slice(part_index * width, (part_index + 1) * width)
                    out[there, :] = full[rows, lanes].astype(F32)
            return carry

        lax.fori_loop(0, n, put, 0)


def sum_over_seq(table, misc, split):
    n = lax.axis_size("seq")
    rows, width = table.shape
    padded, streams = sum_plan(n, rows)
    if padded > rows:
        table = jnp.pad(table, ((0, padded - rows), (0, 0)))
    lanes = -(-misc.size // (8 * n * PAIR)) * PAIR
    misc_table = jnp.pad(misc, (0, 8 * n * lanes - misc.size)).reshape(8 * n, lanes)
    streams = streams + [(0, 8 * n, True)]
    scratch = []
    for index, (_, stream_rows, plane_first) in enumerate(streams):
        last = index == len(streams) - 1
        kind, lane_count = (F32, lanes) if last else (BF16, width)
        one, two = (PLANE, n // PLANE) if plane_first else (n // PLANE, PLANE)
        block, chunk = stream_rows // one, stream_rows // n
        scratch += [
            pltpu.VMEM((one - 1, block, lane_count), kind),
            pltpu.VMEM((block, lane_count), kind),
            pltpu.VMEM((two - 1, chunk, lane_count), kind),
            pltpu.VMEM((block, lane_count), kind),
            pltpu.VMEM((stream_rows, lane_count), kind),
        ]
    partners = max(PLANE, n // PLANE) - 1
    sems = pltpu.SemaphoreType.DMA((len(streams), 4, partners))
    in_vmem = pl.BlockSpec(memory_space=pltpu.VMEM)
    shapes = [jax.ShapeDtypeStruct((padded, width // split), F32)] * split
    *sums, misc_sum = pl.pallas_call(
        partial(sum_kernel, n, streams, split),
        in_specs=[in_vmem, in_vmem],
        out_specs=[in_vmem] * (split + 1),
        out_shape=shapes + [jax.ShapeDtypeStruct(misc_table.shape, F32)],
        scratch_shapes=scratch + [sems, sems],
        compiler_params=params(collective_id=0, has_side_effects=True),
        cost_estimate=pl.CostEstimate(flops=1 << 36, bytes_accessed=1 << 24, transcendentals=0),
        name="sum_over_seq",
    )(table, misc_table)
    return [total[:rows] for total in sums], misc_sum.reshape(-1)[: misc.size]


def plan_kernel(tokens, groups, length_ref, *refs):
    outs, end_ref = refs[:-1], refs[-1]
    docs = length_ref.shape[0]
    my_index, my_side = lax.axis_index("seq"), lax.axis_index("tp")
    all_tokens = tokens * lax.axis_size("seq")
    first = my_index * tokens
    half = tokens // CHUNK

    def add(doc, total):
        total = total + length_ref[doc]
        end_ref[doc] = total
        return total

    lax.fori_loop(0, docs, add, jnp.int32(0))

    q_count = tokens // Q_TILE_BACK
    spots = [first + i * Q_TILE_BACK for i in range(q_count)]
    spots += [spot + Q_TILE_BACK - 1 for spot in spots]
    starts = []
    for distances in groups:
        starts.append([first - d * tokens + h * CHUNK for d in distances for h in range(half)])
        spots += starts[-1] + [start + CHUNK - 1 for start in starts[-1]]

    def count_ends(doc, found):
        end = end_ref[doc]
        return [f + (end <= spot).astype(jnp.int32) for f, spot in zip(found, spots)]

    found = lax.fori_loop(0, docs, count_ends, [jnp.int32(0)] * len(spots))
    found = [
        jnp.where(spot < 0, -1, jnp.where(spot >= all_tokens, FAR_ID, f))
        for f, spot in zip(found, spots)
    ]
    q_low, q_high = found[:q_count], found[q_count : 2 * q_count]
    ratio = Q_TILE // Q_TILE_BACK
    at, rest = 2 * q_count, list(outs)
    for group in starts:
        number = len(group)
        low, high = found[at : at + number], found[at + number : at + 2 * number]
        at += 2 * number
        need = [
            ((h >= q_low[0]) & (l <= q_high[-1])).astype(jnp.int32) for l, h in zip(low, high)
        ]
        ends = [
            [*q_low[::ratio], *q_high[ratio - 1 :: ratio], *low, *high],
            [*q_low, *q_high, *low, *high],
        ]
        for values in ends:
            table = rest.pop(0)
            for i, value in enumerate(values):
                table[i] = value
            base, last, taken = len(values), jnp.int32(0), jnp.int32(0)
            for i in range(number):
                table[base + i] = jnp.int32(0)
            for i in range(number):
                spot = jnp.where(need[i] > 0, taken, number - 1)
                kept = table[base + spot]
                table[base + spot] = jnp.where(need[i] > 0, i, kept)
                last = jnp.where(need[i] > 0, i, last)
                taken = taken + need[i]
            for i in range(number):
                table[base + i] = jnp.where(i < taken, table[base + i], last)
            table[base + number] = taken
        chunk_table, fill_table = rest.pop(0), rest.pop(0)
        for i in range(number):
            block, side = i % (number // 2), i // (number // 2)
            place = 2 * block + jnp.where(my_side == 0, side, 1 - side)
            one, two = need[2 * block + side], need[2 * block + 1 - side]
            wanted = jnp.where(my_side == 0, one, two)
            chunk_table[i] = place
            chunk_table[number + i] = wanted
            chunk_table[2 * number + i] = place * wanted
            fill_table[i] = jnp.where(wanted > 0, place, number)
            fill_table[number + i] = wanted
        need_ref = rest.pop(0)
        for i in range(number):
            need_ref[i] = need[i]

    def ids_of(arrays):
        def step(doc, totals):
            end = end_ref[doc]
            return [
                total + (end <= positions).astype(jnp.int32)
                for total, positions in zip(totals, arrays)
            ]

        totals = lax.fori_loop(0, docs, step, [jnp.zeros_like(a) for a in arrays])
        return [
            jnp.where(
                positions < 0, -1, jnp.where(positions >= all_tokens, FAR_ID, total)
            )
            for total, positions in zip(totals, arrays)
        ]

    def rows_of(bases, lanes):
        row = lax.broadcasted_iota(jnp.int32, (len(bases), lanes), 0)
        positions = lax.broadcasted_iota(jnp.int32, (len(bases), lanes), 1)
        for i, base in enumerate(bases):
            positions = positions + jnp.where(row == i, base, 0)
        return positions

    arrays = [rows_of(group, CHUNK) for group in starts]
    arrays.append(rows_of([first + i * Q_TILE for i in range(tokens // Q_TILE)], Q_TILE))
    strips = tokens // STRIP
    for extra in (0, 1):
        bases = [first + i * STRIP - STRIP // 2 for i in range(-extra, strips + extra)]
        arrays.append(rows_of(bases, 2 * STRIP))
    for ids in ids_of(arrays):
        rest.pop(0)[...] = ids
    col_ref = rest.pop(0)

    def fill(strip, carry):
        row = lax.broadcasted_iota(jnp.int32, (2 * STRIP, PAIR), 0)
        rows = pl.ds(pl.multiple_of(strip * 2 * STRIP, STRIP), 2 * STRIP)
        col_ref[rows, :] = ids_of([row + (first + (strip - 1) * 2 * STRIP)])[0]
        return carry

    lax.fori_loop(0, strips // 2 + 2, fill, 0)


def plan(lengths, tokens, groups):
    half = tokens // CHUNK
    q_tiles, q_back = tokens // Q_TILE, tokens // Q_TILE_BACK
    strips = tokens // STRIP
    sizes, rows = [], []
    for distances in groups:
        number = half * len(distances)
        sizes += [
            2 * q_tiles + 3 * number + 1,
            2 * q_back + 3 * number + 1,
            3 * number,
            2 * number,
            number,
        ]
        rows.append((number, CHUNK))
    rows += [(q_tiles, Q_TILE), (strips, 2 * STRIP), (strips + 2, 2 * STRIP)]
    rows.append(((strips + 4) * STRIP, PAIR))
    smem = pl.BlockSpec(memory_space=pltpu.SMEM)
    vmem = pl.BlockSpec(memory_space=pltpu.VMEM)
    shapes = [(size,) for size in sizes] + rows
    outs = pl.pallas_call(
        partial(plan_kernel, tokens, groups),
        in_specs=[smem],
        out_specs=[smem] * len(sizes) + [vmem] * len(rows),
        out_shape=[jax.ShapeDtypeStruct(shape, jnp.int32) for shape in shapes],
        scratch_shapes=[pltpu.SMEM(lengths.shape, jnp.int32)],
        compiler_params=params(),
        cost_estimate=LIGHT,
        name="plan",
    )(lengths)
    tables = [outs[5 * i : 5 * i + 5] for i in range(len(groups))]
    return [list(column) for column in zip(*tables)], outs[len(sizes) :]


def shifted(block, axis, distance):
    count = lax.axis_size(axis)
    route = [(i, i + distance) for i in range(count) if 0 <= i + distance < count]
    return lax.ppermute(block, axis, route)


def swapped(block, axis):
    return lax.ppermute(block, axis, [(0, 1), (1, 0)])


def tp_sum(partial_low):
    return partial_low.astype(F32) + swapped(partial_low, "tp").astype(F32)


def after(value, *others):
    return lax.optimization_barrier((value, *others))[0]


def layer_norm(vectors, gain_row, shift_row):
    center = vectors - jnp.mean(vectors, axis=-1, keepdims=True)
    spread = jnp.mean(center * center, axis=-1, keepdims=True)
    return center * lax.rsqrt(spread + EPS_LAYER) * gain_row + shift_row


def body(
    inputs,
    cotangent,
    query_weight,
    key_weight,
    value_weight,
    out_weight,
    up_weight,
    down_weight,
    conv_taps,
    attn_gain,
    attn_shift,
    ffn_gain,
    ffn_shift,
    hyperplanes,
    lengths,
):
    tokens, depth = inputs.shape
    head_dim = hyperplanes.shape[2]
    width = query_weight.shape[1]
    half = tokens // 2
    my_side = lax.axis_index("tp")
    all_tokens = tokens * lax.axis_size("seq")
    far_reach = (MOST + tokens - 2) // tokens
    close = far_reach // 2
    near = list(range(close, 0, -1)) + list(range(-1, -close - 1, -1))
    far = list(range(far_reach, close, -1)) + list(range(-close - 1, -far_reach - 1, -1))

    mine_rows = lax.dynamic_slice_in_dim(inputs, my_side * half, half, 0)
    near_mine = [shifted(mine_rows, "seq", d) for d in near]

    near_at, far_at, own_at = range(3)
    k_counts = [tokens // CHUNK * len(distances) for distances in (near, far, [0])]
    (tables, back_tables, chunk_tables, fill_tables, needs), id_rows = plan(
        lengths, tokens, (near, far, [0])
    )
    near_rows, far_rows, own_key_rows, own_rows, mix_row, back_row, ids_col = id_rows

    weight_qkv = jnp.concatenate([query_weight, key_weight, value_weight], axis=1)
    weight_kv = weight_qkv[:, width:]
    plain_table = jnp.array(list(range(tokens // CHUNK)) + [1] * (tokens // CHUNK), jnp.int32)
    query_unit, query_scale, key_unit, key_scale, values = project(
        plain_table, [inputs], weight_qkv, 2, head_dim
    )
    gathered, own_weights = attend(
        tables[own_at], query_unit, key_unit, values, own_rows, own_key_rows, head_dim
    )

    def other_half(mine):
        return jnp.concatenate([swapped(term, "tp") for term in mine], axis=0)

    *near_mine, late_rows = after((*near_mine, mine_rows), gathered)
    far_mine = [shifted(late_rows if i else mine_rows, "seq", d) for i, d in enumerate(far)]
    group_x, group_kv, group_weights = [], [], []
    for index, mine in ((near_at, near_mine), (far_at, far_mine)):
        if index == far_at:
            mine = after(tuple(mine), gathered)
        group_x.append([*mine, other_half(mine)])
        key_far, scale_far, value_far = project(
            fill_tables[index], group_x[index], weight_kv, 1, head_dim, k_counts[index]
        )
        group_kv.append((key_far, scale_far, value_far))
        gathered, weights = attend(
            tables[index],
            query_unit,
            key_far,
            value_far,
            own_rows,
            (near_rows, far_rows)[index],
            head_dim,
            seed=gathered,
        )
        group_weights.append(weights)
    edge = close * tokens
    sides = needs[near_at][edge // CHUNK - 1 : edge // CHUNK + 1]
    values_rim = jnp.where(
        jnp.repeat(sides, RIM)[:, None] > 0, group_kv[near_at][2][edge - RIM : edge + RIM], 0
    )
    mixed = mix(gathered, values, values_rim, mix_row, ids_col, conv_taps, head_dim)

    attn_out = tp_sum(nn(mixed, out_weight).astype(BF16))
    first_norm, first_back = jax.vjp(
        layer_norm, inputs.astype(F32) + attn_out, attn_gain, attn_shift
    )
    first_low = first_norm.astype(BF16)
    partial_out, active, slope = feed(first_low, up_weight, down_weight)
    ffn_out = tp_sum(partial_out)
    result, second_back = jax.vjp(layer_norm, first_norm + ffn_out, ffn_gain, ffn_shift)
    output = result.astype(BF16)
    grad_second, grad_ffn_gain, grad_ffn_shift = second_back(cotangent.astype(F32))
    grad_ffn = grad_second.astype(BF16)
    grad_hidden = (nt(grad_ffn, down_weight) * slope.astype(F32)).astype(BF16)
    grad_first = grad_second + tp_sum(nt(grad_hidden, up_weight).astype(BF16))
    grad_residual, grad_attn_gain, grad_attn_shift = first_back(grad_first)
    grad_attn = grad_residual.astype(BF16)
    grad_mixed = nt(grad_attn, out_weight).astype(BF16)

    grad_down = tn(active, grad_ffn).astype(BF16)
    grad_up = tn(first_low, grad_hidden).astype(BF16)
    grad_out = tn(mixed, grad_attn).astype(BF16)
    down_out = jnp.concatenate([grad_down, grad_out], axis=0)
    grad_up_low, down_out_low = grad_up, down_out
    grad_up, down_out = lax.psum((grad_up_low, down_out_low), "seq")

    grad_rows = back_norm(gathered, after(grad_mixed, grad_up_low, down_out_low), head_dim)

    def back_scores(index, grad_rows, seed):
        key_far, _, value_far = group_kv[index]
        return back_attend(
            back_tables[index],
            k_counts[index],
            query_unit,
            grad_rows,
            key_far,
            value_far,
            group_weights[index],
            head_dim,
            seed=seed,
        )

    def back_inputs(index, dk, dv, **rims):
        key_far, scale_far, _ = group_kv[index]
        parts = [(key_far, scale_far, dk)]
        return back_project(
            chunk_tables[index], group_x[index], weight_kv, parts, 0, [dv], head_dim, **rims
        )

    def both_sides(mine, came, first, number):
        rows = slice(first * half, (first + number) * half)
        return (mine[rows].astype(F32) + came[rows].astype(F32)).astype(BF16)

    dk, dv, turned = back_scores(far_at, grad_rows, None)
    far_dx, dx_other, far_dw = back_inputs(far_at, dk, dv)
    far_came = swapped(dx_other, "tp")
    grad_conv_values, grad_taps = back_conv(
        values, values_rim, after(grad_mixed, far_dx), back_row, ids_col, conv_taps, head_dim
    )
    rim = jnp.concatenate([grad_conv_values[:STRIP], grad_conv_values[-STRIP:]], axis=0)
    dk, dv, turned = back_scores(near_at, after(grad_rows, grad_conv_values), turned)
    near_dx, dx_other, near_dw = back_inputs(
        near_at, dk, dv, rims=close * (tokens // CHUNK) - 1, rim=rim
    )
    near_came = swapped(dx_other, "tp")
    occ_local = occupancy(after(key_unit, near_dx), hyperplanes, 2.0**BITS / all_tokens)
    far_came, near_came = after((far_came, near_came), occ_local)
    count = lax.axis_size("seq")
    low_pair = both_sides(far_dx, far_came, 0, 2)
    high_pair = both_sides(far_dx, far_came, 2, 2)
    near_terms = [both_sides(near_dx, near_came, i, 1) for i in range(len(near))]
    low_pair, high_pair, near_terms, grad_up, down_out = after(
        (low_pair, high_pair, near_terms, grad_up, down_out), occ_local
    )
    two_low, one_low, one_high, two_high = near_terms
    low_far = shifted(low_pair, "seq", -far_reach)
    high_far = shifted(high_pair, "seq", far_reach)
    last = count - far_reach
    rest_home = lax.ppermute(
        jnp.where(lax.axis_index("seq") == last, high_pair[:half], low_pair[half:]),
        "seq",
        [(far_reach - 1, 0), (last, count - 1)],
    )
    two_homes = [shifted(two_low, "seq", -close), shifted(two_high, "seq", close)]
    dk, dv, turned = back_attend(
        back_tables[own_at],
        k_counts[own_at],
        query_unit,
        after(grad_rows, low_pair, high_pair, two_low, one_low, one_high, two_high),
        key_unit,
        values,
        own_weights,
        head_dim,
        seed=turned,
        cost=pl.CostEstimate(flops=1 << 35, bytes_accessed=1 << 20, transcendentals=0),
    )
    dk, low_far, high_far, rest_home, *two_homes = after(
        (dk, low_far, high_far, rest_home, *two_homes), dv
    )
    one_low = (one_low.astype(F32) + high_far[:half].astype(F32)).astype(BF16)
    one_high = (one_high.astype(F32) + low_far[half:].astype(F32)).astype(BF16)
    one_homes = [shifted(one_low, "seq", -1), shifted(one_high, "seq", 1)]
    dk = after(dk, one_low, one_high)
    own_mine = mine_rows
    own_other = lax.dynamic_slice_in_dim(inputs, (1 - my_side) * half, half, 0)
    dx_mine, dx_other, dw = back_project(
        chunk_tables[own_at],
        [own_mine, own_other],
        weight_qkv,
        [(query_unit, query_scale, turned), (key_unit, key_scale, dk)],
        1,
        [dv, grad_conv_values[STRIP:-STRIP]],
        head_dim,
    )

    homes = [low_far[:half], high_far[half:], rest_home, *two_homes]
    homes += after(tuple(one_homes), dw)
    qkv = jnp.concatenate([dw[:, :width], dw[:, width:] + near_dw + far_dw], axis=1).astype(BF16)
    misc = [
        occ_local,
        grad_taps,
        grad_attn_gain,
        grad_attn_shift,
        grad_ffn_gain,
        grad_ffn_shift,
    ]
    packed = jnp.concatenate([term.reshape(-1) for term in misc])
    qkv, packed = sum_over_seq(qkv, packed, 3)

    came = swapped(dx_other, "tp")
    total = (
        lax.dynamic_slice_in_dim(grad_residual, my_side * half, half, 0)
        + dx_mine.astype(F32)
        + came.astype(F32)
    )
    for home in homes:
        total = total + home.astype(F32)
    other_total = swapped(total, "tp")
    lower = jnp.where(my_side == 0, total, other_total)
    upper = jnp.where(my_side == 0, other_total, total)
    grad_inputs = jnp.concatenate([lower, upper], axis=0)

    unpacked, at = [], 0
    for term in misc:
        unpacked.append(packed[at : at + term.size].reshape(term.shape))
        at += term.size
    down_out = down_out.astype(F32)
    ff = down_weight.shape[0]
    return (
        output,
        grad_inputs,
        *qkv,
        down_out[ff:],
        grad_up.astype(F32),
        down_out[:ff],
        *unpacked[1:],
        unpacked[0],
    )


def solution(mesh):
    return jax.shard_map(
        body,
        mesh=mesh,
        in_specs=(
            P("seq", None),
            P("seq", None),
            P(None, "tp"),
            P(None, "tp"),
            P(None, "tp"),
            P("tp", None),
            P(None, "tp"),
            P("tp", None),
            P("tp", None),
            P(),
            P(),
            P(),
            P(),
            P(),
            P(),
        ),
        out_specs=(
            P("seq", None),
            P("seq", None),
            P(None, "tp"),
            P(None, "tp"),
            P(None, "tp"),
            P("tp", None),
            P(None, "tp"),
            P("tp", None),
            P("tp", None),
            P(),
            P(),
            P(),
            P(),
            P("tp", None, None),
        ),
        check_vma=False,
    )
```
